256 devices in a mesh: band: 32 (over x_hi, z, core), var: 8 (over y, x_lo).
Axes of the slice: x: 4 (x_hi: 2, x_lo: 2; x = x_hi * 2 + x_lo), y: 4, z: 8, core: 2. Of those that a mesh axis runs over, the one named last changes fastest.
Arguments:
- patches: bfloat16 [16, 32, 256, 64], P('var', 'band'), may hold values from -6 to 6
- w_embed: bfloat16 [16, 64, 2048], P('var'), may hold values from -0.75 to 0.75
- var_bias: float32 [16, 2048], P('var'), may hold values from -3 to 3
- agg_gain: float32 [2048], replicated, may hold values from 0.1 to 1.9
- wq: bfloat16 [2048, 2048], P(None, 'var'), may hold values from -4 to 4
- wk: bfloat16 [2048, 2048], P(None, 'var'), may hold values from -4 to 4
- wv: bfloat16 [2048, 2048], P(None, 'var'), may hold values from -0.125 to 0.125
- wo: bfloat16 [2048, 2048], P('var'), may hold values from -0.125 to 0.125
- w_up: bfloat16 [2048, 1024], replicated, may hold values from -0.125 to 0.125
- conv1: bfloat16 [9, 64, 64], replicated, may hold values from -0.25 to 0.25
- bias1: float32 [64], replicated, may hold values from -3 to 3
- conv2: bfloat16 [9, 64, 64], replicated, may hold values from -0.25 to 0.25
- cotangent: bfloat16 [128, 64, 1024], P('band', None, 'var'), may hold values from -6 to 6
Outputs:
- field_out: bfloat16 [128, 64, 1024], P('band', None, 'var')
- grad_fine: bfloat16 [128, 64, 1024], P('band', None, 'var')
- grad_conv1: float32 [9, 64, 64], replicated
- grad_conv2: float32 [9, 64, 64], replicated
- grad_bias: float32 [64], replicated
The draws below stay inside these ranges and needn't reach their ends.
All inputs are finite; a program needn't handle non-finite values.
Results may differ from the reference program's by a relative error of at most 0.03.
Values may be sent and summed in bfloat16 or wider, within the bound.
No kernel may reach another device: no remote copies, remote signals or barrier semaphores. Data moves between devices by JAX's collectives and lax.ppermute only.
A program may use at most 128 MiB of HBM per device.

```python
import math
import jax
import jax.numpy as jnp
from jax import lax

D = 2048
HEADS = 16
HD = 128
VARS = 16
P_SIZE = 64
C = 64
R = 4
LAT = 32
LON = 256
TOKENS = 8192
FY = 128
FX = 1024


def projection_pair(key):
    folded = jax.random.fold_in(key, 4242)
    first_key, second_key, third_key, fourth_key = jax.random.split(folded, 4)
    columns = HEADS * HD
    query_part = jax.random.normal(first_key, (D, columns), jnp.float32) / jnp.sqrt(jnp.float32(D))
    key_part = jax.random.normal(second_key, (D, columns), jnp.float32) / jnp.sqrt(jnp.float32(D))
    strength = jnp.exp(jax.random.uniform(fourth_key, (HEADS,), jnp.float32, math.log(1.5), math.log(4.0)))
    head_sign = (jax.random.randint(third_key, (HEADS,), 0, 2) * 2 - 1).astype(jnp.float32)
    key_part = jnp.repeat(head_sign * strength, HD)[None, :] * query_part + key_part
    return (jnp.clip(query_part, -4.0, 4.0), jnp.clip(key_part, -4.0, 4.0))


def draw_wq(key, part):
    return projection_pair(key)[0].astype(jnp.bfloat16)


def draw_wk(key, part):
    return projection_pair(key)[1].astype(jnp.bfloat16)


def draw_patches(key, part):
    folded = jax.random.fold_in(key, 777)
    order_key, shared_key, own_key = jax.random.split(folded, 3)
    order = jax.random.permutation(order_key, TOKENS)
    ranks = jnp.zeros((TOKENS,), jnp.int32).at[order].set(jnp.arange(TOKENS, dtype=jnp.int32))
    groups = ranks // 4
    token_sign = jnp.where(ranks % 4 < 2, 1.0, -1.0).astype(jnp.float32)
    shared = jax.random.normal(shared_key, (VARS, TOKENS // 4, P_SIZE), jnp.float32)
    own = jax.random.normal(own_key, (VARS, TOKENS, P_SIZE), jnp.float32)
    spread = jnp.take(shared, groups, axis=1)
    values = math.sqrt(0.9) * token_sign[None, :, None] * spread + math.sqrt(0.1) * own
    return jnp.clip(values, -6.0, 6.0).reshape(VARS, LAT, LON, P_SIZE).astype(jnp.bfloat16)


def with_spikes(array, stream_key, source, target, parts, factor):
    owner, partner = [(jnp.arange(array.shape[axis_at]) // (array.shape[axis_at] // parts)).reshape([-1 if axis == axis_at else 1 for axis in range(array.ndim)]) for axis_at in (source, target)]
    chosen = jax.random.permutation(stream_key, parts)[partner]
    strong = (owner == chosen) | (owner == (partner + parts // 2) % parts)
    return jnp.where(strong, factor * array, array)


def levels(key, extent, cuts, least, largest):
    def one(position, parts):
        draws = jax.random.uniform(jax.random.fold_in(jax.random.fold_in(key, 6), position), (parts,), jnp.float32, least / len(cuts), largest / len(cuts))
        return jnp.repeat(jnp.exp(draws), extent[position] // parts).reshape((-1,) + (1,) * (len(extent) - position - 1))

    loudness = one(*cuts[0])
    for cut in cuts[1:]:
        loudness = loudness * one(*cut)
    return loudness


def bell_draw(key, extent, deviation, most, cuts=(), kind=jnp.bfloat16):
    entries = jax.random.normal(key, extent, jnp.float32) * deviation
    if len(cuts) > 0:
        entries = levels(key, extent, cuts, -0.22, 0.18) * entries
    return jnp.clip(entries, min=-most, max=most).astype(kind)


def noise_with(key, extent, scale, limit, cuts, heavy, kind=jnp.bfloat16):
    drawn = scale * jax.random.normal(key, extent, jnp.float32)
    if cuts:
        drawn = drawn * levels(key, extent, cuts, -0.22, 0.18)
    return jnp.clip(with_spikes(drawn, jax.random.fold_in(key, 3), *heavy), -limit, limit).astype(kind)


def setup_inputs(seed: int = 0) -> dict:
    key_list = jax.random.split(jax.random.key(seed), 14)
    patches = draw_patches(jax.random.fold_in(key_list[13], 71), 0)
    w_embed = bell_draw(key_list[1], (VARS, P_SIZE, D), P_SIZE ** -0.5, 0.75, ((0, 8),))
    var_bias = bell_draw(key_list[2], (VARS, D), 0.5, 3.0, ((0, 8),), jnp.float32)
    agg_gain = jnp.clip(1.0 + 0.18 * jax.random.normal(key_list[3], (D,), jnp.float32), 0.1, 1.9)
    wq = draw_wq(jax.random.fold_in(key_list[13], 71), 0)
    wk = draw_wk(jax.random.fold_in(key_list[13], 71), 0)
    wv = bell_draw(key_list[6], (D, HEADS * HD), D ** -0.5, 0.125, ((1, 8),))
    wo = bell_draw(key_list[7], (HEADS * HD, D), (HEADS * HD) ** -0.5, 0.125, ((0, 8),))
    w_up = bell_draw(key_list[8], (D, R * R * C), D ** -0.5, 0.125)
    conv1 = bell_draw(key_list[9], (9, C, C), (9 * C) ** -0.5, 0.25)
    bias1 = bell_draw(key_list[10], (C,), 0.5, 3.0, (), jnp.float32)
    conv2 = bell_draw(key_list[11], (9, C, C), (9 * C) ** -0.5, 0.25)
    cotangent = noise_with(key_list[12], (FY, C, FX), 1.0, 6.0, ((0, 32), (2, 8)), (0, 1, 32, 2.75))
    return dict(patches=patches, w_embed=w_embed, var_bias=var_bias, agg_gain=agg_gain, wq=wq, wk=wk, wv=wv, wo=wo, w_up=w_up, conv1=conv1, bias1=bias1, conv2=conv2, cotangent=cotangent)


def tap_stack(padded, height, width):
    pieces = [padded[row_tap:row_tap + height, :, col_tap:col_tap + width] for row_tap in range(3) for col_tap in range(3)]
    return jnp.concatenate(pieces, axis=1)

def conv_apply(field, weight):
    padded = jnp.pad(field, ((1, 1), (0, 0), (1, 1)))
    stacked = tap_stack(padded, field.shape[0], field.shape[2]).astype(jnp.float32)
    return jnp.einsum('ykx,ko->yox', stacked, weight.reshape(-1, weight.shape[2]).astype(jnp.float32))

def flipped(weight):
    return jnp.transpose(weight[::-1], (0, 2, 1))

def weight_grad(field, grads):
    padded = jnp.pad(field, ((1, 1), (0, 0), (1, 1)))
    stacked = tap_stack(padded, field.shape[0], field.shape[2]).astype(jnp.float32)
    summed = jnp.einsum('ykx,yox->ko', stacked, grads.astype(jnp.float32))
    return summed.reshape(9, field.shape[1], grads.shape[1])

def head_attention(inputs):
    query_head, key_head, value_head = inputs
    block = math.gcd(TOKENS, 1024)
    blocks = query_head.reshape(TOKENS // block, block, HD)
    key_float = key_head.astype(jnp.float32)

    def one_block(query_block):
        scores = jnp.dot(query_block.astype(jnp.float32), key_float.T, preferred_element_type=jnp.float32) / math.sqrt(HD)
        weights = jnp.exp(scores - lax.optimization_barrier(jnp.max(scores, axis=1, keepdims=True)))
        numer = jnp.dot(weights.astype(jnp.bfloat16), value_head, preferred_element_type=jnp.float32)
        return (numer / lax.optimization_barrier(jnp.sum(weights, axis=1, keepdims=True))).astype(jnp.bfloat16)
    return lax.map(one_block, blocks).reshape(TOKENS, HD)

def split_heads(matrix):
    return jnp.transpose(matrix.reshape(TOKENS, HEADS, HD), (1, 0, 2))

def reference(patches, w_embed, var_bias, agg_gain, wq, wk, wv, wo, w_up, conv1, bias1, conv2, cotangent):
    flattened = jnp.transpose(patches, (1, 2, 0, 3)).reshape(LAT * LON, VARS * P_SIZE)
    mixed = jnp.dot(flattened, w_embed.reshape(VARS * P_SIZE, D), preferred_element_type=jnp.float32) + lax.optimization_barrier(jnp.sum(var_bias, axis=0))
    normed = (mixed * lax.rsqrt(lax.optimization_barrier(jnp.mean(mixed * mixed, axis=1, keepdims=True)) + 1e-05) * agg_gain).astype(jnp.bfloat16)
    queries = jnp.dot(normed, wq, preferred_element_type=jnp.float32).astype(jnp.bfloat16)
    keys_all = jnp.dot(normed, wk, preferred_element_type=jnp.float32).astype(jnp.bfloat16)
    values_all = jnp.dot(normed, wv, preferred_element_type=jnp.float32).astype(jnp.bfloat16)
    context = lax.map(head_attention, (split_heads(queries), split_heads(keys_all), split_heads(values_all)))
    context = jnp.transpose(context, (1, 0, 2)).reshape(TOKENS, HEADS * HD)
    hidden = (normed.astype(jnp.float32) + jnp.dot(context, wo, preferred_element_type=jnp.float32)).astype(jnp.bfloat16)
    upsampled = jnp.dot(hidden, w_up, preferred_element_type=jnp.float32).astype(jnp.bfloat16)
    upsampled = jnp.transpose(upsampled.reshape(LAT, LON, R, R, C), (0, 2, 4, 1, 3)).reshape(FY, C, FX)
    pre = conv_apply(upsampled, conv1) + bias1[None, :, None]
    active = jax.nn.gelu(pre).astype(jnp.bfloat16)
    field_out = (conv_apply(active, conv2) + upsampled.astype(jnp.float32)).astype(jnp.bfloat16)
    d_active = conv_apply(cotangent, flipped(conv2))
    d_pre = jax.vjp(jax.nn.gelu, pre)[1](d_active)[0].astype(jnp.bfloat16)
    grad_fine = (cotangent.astype(jnp.float32) + conv_apply(d_pre, flipped(conv1))).astype(jnp.bfloat16)
    factor = 1.0 / math.sqrt(FY * FX)
    grad_conv1 = weight_grad(upsampled, d_pre) * factor
    grad_conv2 = weight_grad(active, cotangent) * factor
    grad_bias = lax.optimization_barrier(jnp.sum(d_pre.astype(jnp.float32), axis=(0, 2))) * factor
    return (field_out, grad_fine, grad_conv1, grad_conv2, grad_bias)
```

```python
import math

import jax
import jax.numpy as jnp
import numpy as np
from jax import lax
from jax.experimental import pallas as pl
from jax.experimental.pallas import tpu as pltpu
from jax.sharding import Mesh, PartitionSpec as P

D = 2048
HD = 128
C = 64
R = 4
BAND = ("xh", "z", "core")
VAR = ("y", "xl")
PLANE = ("xh", "core", "y", "xl")
BF = jnp.bfloat16
F32 = jnp.float32
VMEM_SPEC = pl.BlockSpec(memory_space=pltpu.VMEM)
SMEM_SPEC = pl.BlockSpec(memory_space=pltpu.SMEM)
SCORE_SCALE = math.log2(math.e) / math.sqrt(HD)


def dot_nn(a, b):
    return lax.dot_general(a, b, (((1,), (0,)), ((), ())), preferred_element_type=F32)


def dot_nt(a, b):
    return lax.dot_general(a, b, (((1,), (1,)), ((), ())), preferred_element_type=F32)


def dot_tn(a, b):
    return lax.dot_general(a, b, (((0,), (0,)), ((), ())), preferred_element_type=F32)


def flash_kernel(blocks, chunks, first, last):
    def body(*refs):
        q_refs = refs[:blocks]
        kv_refs = refs[blocks : blocks + chunks]
        rest = refs[blocks + chunks :]
        if not first:
            stat_in, acc_in = rest[0], rest[1]
            rest = rest[2:]
        for block in range(blocks):
            cols = slice(block * 256, (block + 1) * 256)
            stat_rows = []
            lse_rows = []
            for h in range(2):
                head = slice(h * HD, (h + 1) * HD)
                vals = slice(256 + h * HD, 256 + (h + 1) * HD)
                q = q_refs[block][:, head]
                scores = [dot_nt(kv[:, head], q) * SCORE_SCALE for kv in kv_refs]
                top = jnp.max(scores[0], axis=0, keepdims=True)
                for s in scores[1:]:
                    top = jnp.maximum(top, jnp.max(s, axis=0, keepdims=True))
                if not first:
                    old_top = stat_in[h : h + 1, cols]
                    top = jnp.maximum(top, old_top)
                    shrink = jnp.exp2(old_top - top)
                total = None
                update = None
                for s, kv in zip(scores, kv_refs):
                    w = jnp.exp2(s - top)
                    part = jnp.sum(w, axis=0, keepdims=True)
                    prod = dot_tn(kv[:, vals], w.astype(BF))
                    total = part if total is None else total + part
                    update = prod if update is None else update + prod
                if not first:
                    total = total + stat_in[2 + h : 3 + h, cols] * shrink
                    update = update + acc_in[head, cols] * shrink
                if last:
                    rest[block][head, :] = (update / total).astype(BF)
                    lse = top + jnp.log2(total)
                    high = lse.astype(BF)
                    left = lse - high.astype(F32)
                    mid = left.astype(BF)
                    low = (left - mid.astype(F32)).astype(BF)
                    lse_rows += [high.astype(F32), mid.astype(F32), low.astype(F32)]
                else:
                    rest[1][head, cols] = update
                    stat_rows.append((top, total))
            if last:
                lse_rows.append(jnp.zeros((10, 256), F32))
                rest[block][256:272, :] = jnp.concatenate(lse_rows, axis=0).astype(BF)
            else:
                for h in range(2):
                    rest[0][h : h + 1, cols] = stat_rows[h][0]
                    rest[0][2 + h : 3 + h, cols] = stat_rows[h][1]

    return body


def flash_step(queries, chunks, carry, last):
    blocks = len(queries)
    first = carry is None
    ins = list(queries) + list(chunks) + ([] if first else list(carry))
    if last:
        outs = [jax.ShapeDtypeStruct((272, 256), BF)] * blocks
    else:
        outs = [
            jax.ShapeDtypeStruct((8, 256 * blocks), F32),
            jax.ShapeDtypeStruct((256, 256 * blocks), F32),
        ]
    return pl.pallas_call(
        flash_kernel(blocks, len(chunks), first, last),
        out_shape=outs,
        in_specs=[VMEM_SPEC] * len(ins),
        out_specs=[VMEM_SPEC] * len(outs),
        name="flash_last" if last else "flash_step",
    )(*ins)


def merge_body(b0, b1, b2, b3, mat, out):
    parts = (b0, b1, b2, b3)
    context = []
    for h in range(2):
        head = slice(h * HD, (h + 1) * HD)
        lses = []
        for b in parts:
            tail = b[256:272, :].astype(F32)
            lses.append(tail[3 * h : 3 * h + 1] + tail[3 * h + 1 : 3 * h + 2] + tail[3 * h + 2 : 3 * h + 3])
        top = jnp.maximum(jnp.maximum(lses[0], lses[1]), jnp.maximum(lses[2], lses[3]))
        ws = [jnp.exp2(v - top) for v in lses]
        total = ws[0] + ws[1] + ws[2] + ws[3]
        mixed = sum(b[head, :].astype(F32) * (w / total) for b, w in zip(parts, ws))
        context.append(mixed.astype(BF))
    up = dot_tn(jnp.concatenate(context, axis=0), mat[...])
    for j in range(8):
        for half in range(2):
            rows = []
            for k in range(4):
                lanes = slice((half * 4 + k) * 128, (half * 4 + k + 1) * 128)
                out[j, half, k * 32 : (k + 1) * 32, :] = up[32 * j : 32 * j + 32, lanes].astype(BF)
                token = 32 * j + 32 if k % 2 == 0 else 32 * j - 1
                inside = 0 <= token < 256
                rows.append(up[token : token + 1, lanes] if inside else jnp.zeros((1, 128), F32))
            rows.append(jnp.zeros((12, 128), F32))
            out[j, half, 128:144, :] = jnp.concatenate(rows, axis=0).astype(BF)


def merge(parts, mat):
    return pl.pallas_call(
        merge_body,
        out_shape=jax.ShapeDtypeStruct((8, 2, 144, 128), BF),
        in_specs=[VMEM_SPEC] * 5,
        out_specs=VMEM_SPEC,
        name="merge_heads",
    )(*parts, mat)


def spread_matrix():
    spread = np.zeros((144, 2, 2, 256), np.float32)
    for a in range(2):
        for bh in range(2):
            k = 2 * a + bh
            for bl in range(2):
                for token in range(32):
                    spread[k * 32 + token, a, bl, 4 * token + 2 * bh + bl] = 1
                spread[128 + k, a, bl, (128 + bl) if bh == 0 else (254 + bl)] = 1
    return spread.reshape(144, 1024)


def gelu_pair(x):
    root = math.sqrt(2.0 / math.pi)
    t = jnp.tanh(root * (x + 0.044715 * (x * x * x)))
    half = 0.5 * (1.0 + t)
    slope = half + 0.5 * x * (1.0 - t * t) * (root * (1.0 + 3 * 0.044715 * (x * x)))
    return x * half, slope


def shifted(row):
    return jnp.concatenate(
        [pltpu.roll(row, 1, 1), row, pltpu.roll(row, row.shape[1] - 1, 1)], axis=0
    )


def fine_body(factor):
    def body(flags, own, prev, nxt, spread, grad, rim, mats, bias, field, grad_fine, terms):
        spread_all = spread[...]
        ups = []
        for block in (prev[...], own[0], own[1], nxt[...]):
            wide = dot_tn(block, spread_all)
            for a in range(2):
                ups.append(
                    wide[0:64, 512 * a : 512 * a + 256] + wide[64:128, 512 * a + 256 : 512 * a + 512]
                )
        grads = [
            jnp.concatenate([grad[r].astype(F32), rim[r].astype(F32)], axis=1) for r in range(8)
        ]
        up_taps = [shifted(u).astype(BF) for u in ups]
        grad_taps = [shifted(g).astype(BF) for g in grads]
        pre_all = dot_nn(mats[0], jnp.concatenate(up_taps, axis=1))
        act_all = dot_nn(mats[1], jnp.concatenate(grad_taps, axis=1))

        def gather(products, i, width):
            return (
                products[0:64, i * width : (i + 1) * width]
                + products[64:128, (i + 1) * width : (i + 2) * width]
                + products[128:192, (i + 2) * width : (i + 3) * width]
            )

        lane = lax.broadcasted_iota(jnp.int32, (64, 256), 1)
        cols_ok = (lane < 128) | ((lane == 128) & (flags[3] > 0)) | ((lane == 255) & (flags[2] > 0))
        offset = bias[...]
        act_taps = []
        pre_taps = []
        d_rows = []
        for i in range(6):
            pre = gather(pre_all, i, 256) + offset
            value, slope = gelu_pair(pre)
            ok = cols_ok
            if i == 0:
                ok = ok & (flags[0] > 0)
            if i == 5:
                ok = ok & (flags[1] > 0)
            value = jnp.where(ok, value, 0.0)
            d_pre = jnp.where(ok, gather(act_all, i, 256) * slope, 0.0)
            act_taps.append(shifted(value)[:, 0:128].astype(BF))
            pre_taps.append(shifted(d_pre)[:, 0:128].astype(BF))
            if 1 <= i <= 4:
                d_rows.append(d_pre[:, 0:128].astype(BF))
        act_wide = jnp.concatenate(act_taps, axis=1)
        out_all = dot_nn(mats[2], act_wide)
        fine_all = dot_nn(mats[3], jnp.concatenate(pre_taps, axis=1))
        for j in range(4):
            field[j] = (
                gather(out_all, j, 128) + ups[j + 2][:, 0:128]
            ).astype(BF)
            grad_fine[j] = (gather(fine_all, j, 128) + grads[j + 2][:, 0:128]).astype(BF)
        d_own = jnp.concatenate(d_rows, axis=1)
        g_own = jnp.concatenate([grad[r] for r in range(2, 6)], axis=1)
        for p in range(3):
            up_cut = jnp.concatenate([up_taps[r][:, 0:128] for r in range(p + 1, p + 5)], axis=1)
            first = dot_nt(up_cut, d_own)
            second = dot_nt(act_wide[:, p * 128 : p * 128 + 512], g_own)
            terms[p * 192 : (p + 1) * 192, :] = (
                jnp.concatenate([first, second], axis=1) * factor
            ).astype(BF)
        ones = jnp.ones((16, 512), BF)
        third = dot_nt(ones, d_own) * factor
        terms[576:592, :] = jnp.concatenate([third, jnp.zeros((16, 64), F32)], axis=1).astype(BF)
        terms[592:768, :] = jnp.zeros((176, 128), BF)

    return body


def fine_stage(flags, own, prev, nxt, spread, grad, rim, mats, bias, factor):
    return pl.pallas_call(
        fine_body(factor),
        out_shape=[
            jax.ShapeDtypeStruct((4, 64, 128), BF),
            jax.ShapeDtypeStruct((4, 64, 128), BF),
            jax.ShapeDtypeStruct((768, 128), BF),
        ],
        in_specs=[SMEM_SPEC] + [VMEM_SPEC] * 8,
        out_specs=[VMEM_SPEC] * 3,
        name="fine_stage",
    )(flags, own, prev, nxt, spread, grad, rim, mats, bias)


def copies(piece, axis, count):
    return lax.all_to_all(jnp.broadcast_to(piece[None], (count,) + piece.shape), axis, 0, 0)


def flip(count, bit):
    return [(i, i ^ bit) for i in range(count)]


def turn(count, step):
    return [(i, (i + step) % count) for i in range(count)]


def tap_matrix(weight):
    return jnp.transpose(weight.reshape(3, 3, C, C), (0, 3, 1, 2)).reshape(3 * C, 3 * C)


def flipped(weight):
    return jnp.transpose(weight[::-1], (0, 2, 1))


def on_device(
    patches, w_embed, var_bias, agg_gain, wq, wk, wv, wo, w_up, conv1, bias1, conv2, cotangent
):
    flattened = jnp.transpose(patches, (1, 2, 0, 3)).reshape(256, 128)
    partial_mix = jnp.dot(flattened, w_embed.reshape(128, D), preferred_element_type=F32)
    partial_mix = (partial_mix + jnp.sum(var_bias, axis=0)).astype(BF).reshape(8, 32, D)
    mixed = jnp.sum(lax.all_to_all(partial_mix, VAR, 0, 0).astype(F32), axis=0)
    normed_slab = (
        mixed * lax.rsqrt(jnp.mean(mixed * mixed, axis=-1, keepdims=True) + 1e-05) * agg_gain
    ).astype(BF)
    normed = copies(normed_slab, VAR, 8).reshape(256, D)

    keys = jnp.dot(normed, wk, preferred_element_type=F32).astype(BF)
    values = jnp.dot(normed, wv, preferred_element_type=F32).astype(BF)
    queries = jnp.dot(normed, wq, preferred_element_type=F32).astype(BF)
    keyvals = jnp.concatenate([keys, values], axis=1)

    group = ("xh", "core")
    all_queries = [queries] + [lax.ppermute(queries, group, flip(4, k)) for k in (1, 2, 3)]
    ahead = [keyvals]
    behind = [keyvals]
    for _ in range(3):
        ahead.append(lax.ppermute(ahead[-1], "z", turn(8, 1)))
        behind.append(lax.ppermute(behind[-1], "z", turn(8, -1)))
    ahead.append(lax.ppermute(ahead[-1][:128], "z", turn(8, 1)))
    behind.append(lax.ppermute(behind[-1][128:], "z", turn(8, -1)))
    carry = flash_step(all_queries, [keyvals, ahead[1], behind[1]], None, False)
    carry = flash_step(all_queries, [ahead[2], behind[2]], carry, False)
    carry = flash_step(all_queries, [ahead[3], behind[3]], carry, False)

    var_at = lax.axis_index(VAR)
    band_at = lax.axis_index(BAND)
    up_mat = jnp.dot(wo, w_up, preferred_element_type=F32).astype(BF)
    padded = jnp.pad(normed, ((1, 1), (0, 0)))
    around = lax.dynamic_slice_in_dim(padded, var_at * 32, 34, 0)
    base = jnp.dot(around, w_up, preferred_element_type=F32)
    base_main = jnp.transpose(base[1:33].reshape(32, 2, 4, 128), (1, 2, 0, 3)).reshape(2, 128, 128)
    left = base[0].reshape(2, 4, 128)
    right = base[33].reshape(2, 4, 128)
    base_rim = jnp.where(jnp.arange(4)[None, :, None] % 2 == 0, right, left)
    base_all = jnp.concatenate([base_main, base_rim, jnp.zeros((2, 12, 128), F32)], axis=1)

    shift_down = [(i, i + 1) for i in range(31)]
    shift_up = [(i + 1, i) for i in range(31)]
    cells, up_mat = lax.optimization_barrier((cotangent, up_mat))
    grad_rows = jnp.concatenate(
        [
            lax.ppermute(cells[2:4], BAND, shift_down),
            cells,
            lax.ppermute(cells[0:2], BAND, shift_up),
        ],
        axis=0,
    )
    from_right = lax.ppermute(grad_rows[:, :, 0:2], VAR, [(i + 1, i) for i in range(7)])
    from_left = lax.ppermute(grad_rows[:, :, 126:128], VAR, [(i, i + 1) for i in range(7)])
    rim = jnp.concatenate([from_right, jnp.zeros((8, C, 124), BF), from_left], axis=2)
    mats = jnp.stack(
        [tap_matrix(conv1), tap_matrix(flipped(conv2)), tap_matrix(conv2), tap_matrix(flipped(conv1))]
    )

    blocks = flash_step(all_queries, [ahead[4], behind[4]], carry, True)
    parts = [blocks[0]] + [lax.ppermute(blocks[k], group, flip(4, k)) for k in (1, 2, 3)]
    pieces = lax.all_to_all(merge(parts, up_mat), VAR, 0, 0)
    up = (jnp.sum(pieces.astype(F32), axis=0) + base_all).astype(BF)
    prev = lax.ppermute(up[1], BAND, shift_down)
    nxt = lax.ppermute(up[0], BAND, shift_up)
    flags = jnp.stack([band_at > 0, band_at < 31, var_at > 0, var_at < 7]).astype(jnp.int32)
    factor = 1.0 / math.sqrt(128 * 1024)
    spread = jnp.asarray(spread_matrix(), BF)
    field_out, grad_fine, terms = fine_stage(
        flags, up, prev, nxt, spread, grad_rows, rim, mats, bias1.reshape(C, 1), factor
    )
    shares = lax.all_to_all(terms.reshape(32, 24, 128), PLANE, 0, 0)
    share = jnp.sum(shares.astype(F32), axis=0).astype(BF)
    share = jnp.sum(copies(share, "z", 8).astype(F32), axis=0).astype(BF)
    totals = copies(share, PLANE, 32).reshape(768, 128).astype(F32)
    grad_conv1 = totals[:576, :C].reshape(9, C, C)
    grad_conv2 = totals[:576, C:].reshape(9, C, C)
    return (field_out, grad_fine, grad_conv1, grad_conv2, totals[576, :C])


def solution(mesh):
    fine_mesh = Mesh(mesh.devices.reshape(2, 8, 2, 4, 2), BAND + VAR)
    in_specs = (
        P(VAR, BAND, None, None),
        P(VAR, None, None),
        P(VAR, None),
        P(),
        P(None, VAR),
        P(None, VAR),
        P(None, VAR),
        P(VAR, None),
        P(),
        P(),
        P(),
        P(),
        P(BAND, None, VAR),
    )
    out_specs = (P(BAND, None, VAR), P(BAND, None, VAR), P(), P(), P())
    return jax.shard_map(
        on_device, mesh=fine_mesh, in_specs=in_specs, out_specs=out_specs, check_vma=False
    )
```

```python
import math

import jax
import jax.numpy as jnp
import numpy as np
from jax import lax
from jax.experimental import pallas as pl
from jax.experimental.pallas import tpu as pltpu
from jax.sharding import Mesh, PartitionSpec as P

D = 2048
HD = 128
C = 64
R = 4
BAND = ("xh", "z", "core")
VAR = ("y", "xl")
PLANE = ("xh", "core", "y", "xl")
BF = jnp.bfloat16
F32 = jnp.float32
VMEM_SPEC = pl.BlockSpec(memory_space=pltpu.VMEM)
SMEM_SPEC = pl.BlockSpec(memory_space=pltpu.SMEM)
SCORE_SCALE = math.log2(math.e) / math.sqrt(HD)


def dot_nn(a, b):
    return lax.dot_general(a, b, (((1,), (0,)), ((), ())), preferred_element_type=F32)


def dot_nt(a, b):
    return lax.dot_general(a, b, (((1,), (1,)), ((), ())), preferred_element_type=F32)


def dot_tn(a, b):
    return lax.dot_general(a, b, (((0,), (0,)), ((), ())), preferred_element_type=F32)


def flash_kernel(blocks, chunks, first, last):
    def body(*refs):
        q_refs = refs[:blocks]
        kv_refs = refs[blocks : blocks + chunks]
        rest = refs[blocks + chunks :]
        if not first:
            stat_in, acc_in = rest[0], rest[1]
            rest = rest[2:]
        for block in range(blocks):
            cols = slice(block * 256, (block + 1) * 256)
            stat_rows = []
            lse_rows = []
            for h in range(2):
                head = slice(h * HD, (h + 1) * HD)
                vals = slice(256 + h * HD, 256 + (h + 1) * HD)
                q = q_refs[block][:, head]
                scores = [dot_nt(kv[:, head], q) * SCORE_SCALE for kv in kv_refs]
                top = jnp.max(scores[0], axis=0, keepdims=True)
                for s in scores[1:]:
                    top = jnp.maximum(top, jnp.max(s, axis=0, keepdims=True))
                if not first:
                    old_top = stat_in[h : h + 1, cols]
                    top = jnp.maximum(top, old_top)
                    shrink = jnp.exp2(old_top - top)
                total = None
                update = None
                for s, kv in zip(scores, kv_refs):
                    w = jnp.exp2(s - top)
                    part = jnp.sum(w, axis=0, keepdims=True)
                    prod = dot_tn(kv[:, vals], w.astype(BF))
                    total = part if total is None else total + part
                    update = prod if update is None else update + prod
                if not first:
                    total = total + stat_in[2 + h : 3 + h, cols] * shrink
                    update = update + acc_in[head, cols] * shrink
                if last:
                    rest[block][head, :] = (update / total).astype(BF)
                    lse = top + jnp.log2(total)
                    high = lse.astype(BF)
                    left = lse - high.astype(F32)
                    mid = left.astype(BF)
                    low = (left - mid.astype(F32)).astype(BF)
                    lse_rows += [high.astype(F32), mid.astype(F32), low.astype(F32)]
                else:
                    rest[1][head, cols] = update
                    stat_rows.append((top, total))
            if last:
                lse_rows.append(jnp.zeros((10, 256), F32))
                rest[block][256:272, :] = jnp.concatenate(lse_rows, axis=0).astype(BF)
            else:
                for h in range(2):
                    rest[0][h : h + 1, cols] = stat_rows[h][0]
                    rest[0][2 + h : 3 + h, cols] = stat_rows[h][1]

    return body


def flash_step(queries, chunks, carry, last):
    blocks = len(queries)
    first = carry is None
    ins = list(queries) + list(chunks) + ([] if first else list(carry))
    if last:
        outs = [jax.ShapeDtypeStruct((272, 256), BF)] * blocks
    else:
        outs = [
            jax.ShapeDtypeStruct((8, 256 * blocks), F32),
            jax.ShapeDtypeStruct((256, 256 * blocks), F32),
        ]
    return pl.pallas_call(
        flash_kernel(blocks, len(chunks), first, last),
        out_shape=outs,
        in_specs=[VMEM_SPEC] * len(ins),
        out_specs=[VMEM_SPEC] * len(outs),
        name="flash_last" if last else "flash_step",
    )(*ins)


def merge_body(b0, b1, b2, b3, mat, out):
    parts = (b0, b1, b2, b3)
    context = []
    for h in range(2):
        head = slice(h * HD, (h + 1) * HD)
        lses = []
        for b in parts:
            tail = b[256:272, :].astype(F32)
            lses.append(tail[3 * h : 3 * h + 1] + tail[3 * h + 1 : 3 * h + 2] + tail[3 * h + 2 : 3 * h + 3])
        top = jnp.maximum(jnp.maximum(lses[0], lses[1]), jnp.maximum(lses[2], lses[3]))
        ws = [jnp.exp2(v - top) for v in lses]
        total = ws[0] + ws[1] + ws[2] + ws[3]
        mixed = sum(b[head, :].astype(F32) * (w / total) for b, w in zip(parts, ws))
        context.append(mixed.astype(BF))
    up = dot_tn(jnp.concatenate(context, axis=0), mat[...])
    for j in range(8):
        for half in range(2):
            rows = []
            for k in range(4):
                lanes = slice((half * 4 + k) * 128, (half * 4 + k + 1) * 128)
                out[j, half, k * 32 : (k + 1) * 32, :] = up[32 * j : 32 * j + 32, lanes].astype(BF)
                token = 32 * j + 32 if k % 2 == 0 else 32 * j - 1
                inside = 0 <= token < 256
                rows.append(up[token : token + 1, lanes] if inside else jnp.zeros((1, 128), F32))
            rows.append(jnp.zeros((12, 128), F32))
            out[j, half, 128:144, :] = jnp.concatenate(rows, axis=0).astype(BF)


def merge(parts, mat):
    return pl.pallas_call(
        merge_body,
        out_shape=jax.ShapeDtypeStruct((8, 2, 144, 128), BF),
        in_specs=[VMEM_SPEC] * 5,
        out_specs=VMEM_SPEC,
        name="merge_heads",
    )(*parts, mat)


def spread_matrix():
    spread = np.zeros((144, 2, 2, 256), np.float32)
    for a in range(2):
        for bh in range(2):
            k = 2 * a + bh
            for bl in range(2):
                for token in range(32):
                    spread[k * 32 + token, a, bl, 4 * token + 2 * bh + bl] = 1
                spread[128 + k, a, bl, (128 + bl) if bh == 0 else (254 + bl)] = 1
    return spread.reshape(144, 1024)


def gelu_pair(x):
    root = math.sqrt(2.0 / math.pi)
    t = jnp.tanh(root * (x + 0.044715 * (x * x * x)))
    half = 0.5 * (1.0 + t)
    slope = half + 0.5 * x * (1.0 - t * t) * (root * (1.0 + 3 * 0.044715 * (x * x)))
    return x * half, slope


def shifted(row):
    return jnp.concatenate(
        [pltpu.roll(row, 1, 1), row, pltpu.roll(row, row.shape[1] - 1, 1)], axis=0
    )


def fine_body(factor):
    def body(flags, own, prev, nxt, spread, grad, rim, mats, bias, field, grad_fine, terms):
        spread_all = spread[...]
        ups = []
        for block in (prev[...], own[0], own[1], nxt[...]):
            wide = dot_tn(block, spread_all)
            for a in range(2):
                ups.append(
                    wide[0:64, 512 * a : 512 * a + 256] + wide[64:128, 512 * a + 256 : 512 * a + 512]
                )
        grads = [
            jnp.concatenate([grad[r].astype(F32), rim[r].astype(F32)], axis=1) for r in range(8)
        ]
        up_taps = [shifted(u).astype(BF) for u in ups]
        grad_taps = [shifted(g).astype(BF) for g in grads]
        pre_all = dot_nn(mats[0], jnp.concatenate(up_taps, axis=1))
        act_all = dot_nn(mats[1], jnp.concatenate(grad_taps, axis=1))

        def gather(products, i, width):
            return (
                products[0:64, i * width : (i + 1) * width]
                + products[64:128, (i + 1) * width : (i + 2) * width]
                + products[128:192, (i + 2) * width : (i + 3) * width]
            )

        lane = lax.broadcasted_iota(jnp.int32, (64, 256), 1)
        cols_ok = (lane < 128) | ((lane == 128) & (flags[3] > 0)) | ((lane == 255) & (flags[2] > 0))
        offset = bias[...]
        act_taps = []
        pre_taps = []
        d_rows = []
        for i in range(6):
            pre = gather(pre_all, i, 256) + offset
            value, slope = gelu_pair(pre)
            ok = cols_ok
            if i == 0:
                ok = ok & (flags[0] > 0)
            if i == 5:
                ok = ok & (flags[1] > 0)
            value = jnp.where(ok, value, 0.0)
            d_pre = jnp.where(ok, gather(act_all, i, 256) * slope, 0.0)
            act_taps.append(shifted(value)[:, 0:128].astype(BF))
            pre_taps.append(shifted(d_pre)[:, 0:128].astype(BF))
            if 1 <= i <= 4:
                d_rows.append(d_pre[:, 0:128].astype(BF))
        act_wide = jnp.concatenate(act_taps, axis=1)
        out_all = dot_nn(mats[2], act_wide)
        fine_all = dot_nn(mats[3], jnp.concatenate(pre_taps, axis=1))
        for j in range(4):
            field[j] = (
                gather(out_all, j, 128) + ups[j + 2][:, 0:128]
            ).astype(BF)
            grad_fine[j] = (gather(fine_all, j, 128) + grads[j + 2][:, 0:128]).astype(BF)
        d_own = jnp.concatenate(d_rows, axis=1)
        g_own = jnp.concatenate([grad[r] for r in range(2, 6)], axis=1)
        for p in range(3):
            up_cut = jnp.concatenate([up_taps[r][:, 0:128] for r in range(p + 1, p + 5)], axis=1)
            first = dot_nt(up_cut, d_own)
            second = dot_nt(act_wide[:, p * 128 : p * 128 + 512], g_own)
            terms[p * 192 : (p + 1) * 192, :] = (
                jnp.concatenate([first, second], axis=1) * factor
            ).astype(BF)
        ones = jnp.ones((16, 512), BF)
        third = dot_nt(ones, d_own) * factor
        terms[576:592, :] = jnp.concatenate([third, jnp.zeros((16, 64), F32)], axis=1).astype(BF)
        terms[592:768, :] = jnp.zeros((176, 128), BF)

    return body


def fine_stage(flags, own, prev, nxt, spread, grad, rim, mats, bias, factor):
    return pl.pallas_call(
        fine_body(factor),
        out_shape=[
            jax.ShapeDtypeStruct((4, 64, 128), BF),
            jax.ShapeDtypeStruct((4, 64, 128), BF),
            jax.ShapeDtypeStruct((768, 128), BF),
        ],
        in_specs=[SMEM_SPEC] + [VMEM_SPEC] * 8,
        out_specs=[VMEM_SPEC] * 3,
        name="fine_stage",
    )(flags, own, prev, nxt, spread, grad, rim, mats, bias)


def copies(piece, axis, count):
    return lax.all_to_all(jnp.broadcast_to(piece[None], (count,) + piece.shape), axis, 0, 0)


def flip(count, bit):
    return [(i, i ^ bit) for i in range(count)]


def turn(count, step):
    return [(i, (i + step) % count) for i in range(count)]


def tap_matrix(weight):
    return jnp.transpose(weight.reshape(3, 3, C, C), (0, 3, 1, 2)).reshape(3 * C, 3 * C)


def flipped(weight):
    return jnp.transpose(weight[::-1], (0, 2, 1))


def on_device(
    patches, w_embed, var_bias, agg_gain, wq, wk, wv, wo, w_up, conv1, bias1, conv2, cotangent
):
    flattened = jnp.transpose(patches, (1, 2, 0, 3)).reshape(256, 128)
    partial_mix = jnp.dot(flattened, w_embed.reshape(128, D), preferred_element_type=F32)
    partial_mix = (partial_mix + jnp.sum(var_bias, axis=0)).astype(BF).reshape(8, 32, D)
    mixed = jnp.sum(lax.all_to_all(partial_mix, VAR, 0, 0).astype(F32), axis=0)
    normed_slab = (
        mixed * lax.rsqrt(jnp.mean(mixed * mixed, axis=-1, keepdims=True) + 1e-05) * agg_gain
    ).astype(BF)
    cells, normed_slab = lax.optimization_barrier((cotangent, normed_slab))
    normed = copies(normed_slab, VAR, 8).reshape(256, D)
    var_at = lax.axis_index(VAR)
    band_at = lax.axis_index(BAND)
    shift_down = [(i, i + 1) for i in range(31)]
    shift_up = [(i + 1, i) for i in range(31)]
    grad_rows = jnp.concatenate(
        [
            lax.ppermute(cells[2:4], BAND, shift_down),
            cells,
            lax.ppermute(cells[0:2], BAND, shift_up),
        ],
        axis=0,
    )
    from_right = lax.ppermute(grad_rows[:, :, 0:2], VAR, [(i + 1, i) for i in range(7)])
    from_left = lax.ppermute(grad_rows[:, :, 126:128], VAR, [(i, i + 1) for i in range(7)])
    rim = jnp.concatenate([from_right, jnp.zeros((8, C, 124), BF), from_left], axis=2)
    normed, rim = lax.optimization_barrier((normed, rim))

    group = ("xh", "core")
    queries = jnp.dot(normed, wq, preferred_element_type=F32).astype(BF)
    all_queries = [queries] + [lax.ppermute(queries, group, flip(4, k)) for k in (2, 3, 1)]
    keys_in, queries = lax.optimization_barrier((normed, queries))
    keys = jnp.dot(keys_in, wk, preferred_element_type=F32).astype(BF)
    values = jnp.dot(keys_in, wv, preferred_element_type=F32).astype(BF)
    keyvals = jnp.concatenate([keys, values], axis=1)
    ahead, behind = keyvals, keyvals
    carry = None
    fresh = [keyvals]
    for step in range(4):
        if step == 3:
            ahead, behind = ahead[:128], behind[128:]
        ahead = lax.ppermute(ahead, "z", turn(8, 1))
        behind = lax.ppermute(behind, "z", turn(8, -1))
        carry = flash_step(all_queries, fresh, carry, False)
        ahead, behind, carry = lax.optimization_barrier((ahead, behind, carry))
        fresh = [ahead, behind]

    up_mat = jnp.dot(wo, w_up, preferred_element_type=F32).astype(BF)
    padded = jnp.pad(normed, ((1, 1), (0, 0)))
    around = lax.dynamic_slice_in_dim(padded, var_at * 32, 34, 0)
    base = jnp.dot(around, w_up, preferred_element_type=F32)
    base_main = jnp.transpose(base[1:33].reshape(32, 2, 4, 128), (1, 2, 0, 3)).reshape(2, 128, 128)
    left = base[0].reshape(2, 4, 128)
    right = base[33].reshape(2, 4, 128)
    base_rim = jnp.where(jnp.arange(4)[None, :, None] % 2 == 0, right, left)
    base_all = jnp.concatenate([base_main, base_rim, jnp.zeros((2, 12, 128), F32)], axis=1)
    mats = jnp.stack(
        [tap_matrix(conv1), tap_matrix(flipped(conv2)), tap_matrix(conv2), tap_matrix(flipped(conv1))]
    )

    blocks = flash_step(all_queries, fresh, carry, True)
    parts = [blocks[0]] + [lax.ppermute(b, group, flip(4, k)) for b, k in zip(blocks[1:], (2, 3, 1))]
    pieces = lax.all_to_all(merge(parts, up_mat), VAR, 0, 0)
    up = (jnp.sum(pieces.astype(F32), axis=0) + base_all).astype(BF)
    prev = lax.ppermute(up[1], BAND, shift_down)
    nxt = lax.ppermute(up[0], BAND, shift_up)
    flags = jnp.stack([band_at > 0, band_at < 31, var_at > 0, var_at < 7]).astype(jnp.int32)
    factor = 1.0 / math.sqrt(128 * 1024)
    spread = jnp.asarray(spread_matrix(), BF)
    field_out, grad_fine, terms = fine_stage(
        flags, up, prev, nxt, spread, grad_rows, rim, mats, bias1.reshape(C, 1), factor
    )
    shares = lax.all_to_all(terms.reshape(32, 24, 128), PLANE, 0, 0)
    share = jnp.sum(shares.astype(F32), axis=0).astype(BF)
    share = jnp.sum(copies(share, "z", 8).astype(F32), axis=0).astype(BF)
    totals = copies(share, PLANE, 32).reshape(768, 128).astype(F32)
    grad_conv1 = totals[:576, :C].reshape(9, C, C)
    grad_conv2 = totals[:576, C:].reshape(9, C, C)
    return (field_out, grad_fine, grad_conv1, grad_conv2, totals[576, :C])


def solution(mesh):
    fine_mesh = Mesh(mesh.devices.reshape(2, 8, 2, 4, 2), BAND + VAR)
    in_specs = (
        P(VAR, BAND, None, None),
        P(VAR, None, None),
        P(VAR, None),
        P(),
        P(None, VAR),
        P(None, VAR),
        P(None, VAR),
        P(VAR, None),
        P(),
        P(),
        P(),
        P(),
        P(BAND, None, VAR),
    )
    out_specs = (P(BAND, None, VAR), P(BAND, None, VAR), P(), P(), P())
    return jax.shard_map(
        on_device, mesh=fine_mesh, in_specs=in_specs, out_specs=out_specs, check_vma=False
    )
```

```python
import math

import jax
import jax.numpy as jnp
import numpy as np
from jax import lax
from jax.experimental import pallas as pl
from jax.experimental.pallas import tpu as pltpu
from jax.sharding import Mesh, PartitionSpec as P


D = 2048
HD = 128
C = 64
BAND = ("xh", "z", "core")
VAR = ("y", "xl")
PLANE = ("xh", "core", "y", "xl")
BF = jnp.bfloat16
F32 = jnp.float32
VMEM_SPEC = pl.BlockSpec(memory_space=pltpu.VMEM)
SMEM_SPEC = pl.BlockSpec(memory_space=pltpu.SMEM)
SCORE_SCALE = math.log2(math.e) / math.sqrt(HD)


def dot_nn(a, b):
    return lax.dot_general(a, b, (((1,), (0,)), ((), ())), preferred_element_type=F32)


def dot_nt(a, b):
    return lax.dot_general(a, b, (((1,), (1,)), ((), ())), preferred_element_type=F32)


def dot_tn(a, b):
    return lax.dot_general(a, b, (((0,), (0,)), ((), ())), preferred_element_type=F32)


def flash_kernel(blocks, chunks, first, last):
    def body(*refs):
        q_refs = refs[:blocks]
        kv_refs = refs[blocks : blocks + chunks]
        rest = refs[blocks + chunks :]
        if not first:
            stat_in, acc_in = rest[0], rest[1]
            rest = rest[2:]
        for block in range(blocks):
            for part in range(2):
                inner = slice(part * 128, (part + 1) * 128)
                cols = slice(block * 256 + part * 128, block * 256 + (part + 1) * 128)
                stats = []
                for h in range(2):
                    head = slice(h * HD, (h + 1) * HD)
                    vals = slice(256 + h * HD, 256 + (h + 1) * HD)
                    q = q_refs[block][inner, head]
                    state = None
                    if not first:
                        state = (
                            stat_in[h : h + 1, cols],
                            stat_in[2 + h : 3 + h, cols],
                            acc_in[head, cols],
                        )
                    for kv in kv_refs:
                        s = dot_nt(kv[:, head], q) * SCORE_SCALE
                        top = jnp.max(s, axis=0, keepdims=True)
                        if state is not None:
                            top = jnp.maximum(top, state[0])
                        w = jnp.exp2(s - top)
                        total = jnp.sum(w, axis=0, keepdims=True)
                        update = dot_tn(kv[:, vals], w.astype(BF))
                        if state is not None:
                            shrink = jnp.exp2(state[0] - top)
                            total = total + state[1] * shrink
                            update = update + state[2] * shrink
                        state = (top, total, update)
                    top, total, update = state
                    if last:
                        rest[block][head, inner] = (update / total).astype(BF)
                        lse = top + jnp.log2(total)
                        high = lse.astype(BF)
                        left = lse - high.astype(F32)
                        mid = left.astype(BF)
                        low = (left - mid.astype(F32)).astype(BF)
                        stats += [high.astype(F32), mid.astype(F32), low.astype(F32)]
                    else:
                        rest[1][head, cols] = update
                        stats += [top, total]
                if last:
                    stats.append(jnp.zeros((10, 128), F32))
                    rest[block][256:272, inner] = jnp.concatenate(stats, axis=0).astype(BF)
                else:
                    for h in range(2):
                        rest[0][h : h + 1, cols] = stats[2 * h]
                        rest[0][2 + h : 3 + h, cols] = stats[2 * h + 1]

    return body


def near(x):
    return pltpu.with_memory_space_constraint(x, pltpu.VMEM)


def flash_step(queries, chunks, carry, last):
    blocks = len(queries)
    first = carry is None
    ins = list(queries) + list(chunks) + ([] if first else list(carry))
    if last:
        outs = [pltpu.VMEM((272, 256), BF)] * blocks
    else:
        outs = [
            pltpu.VMEM((8, 256 * blocks), F32),
            pltpu.VMEM((256, 256 * blocks), F32),
        ]
    return pl.pallas_call(
        flash_kernel(blocks, len(chunks), first, last),
        out_shape=outs,
        in_specs=[VMEM_SPEC] * len(ins),
        out_specs=[VMEM_SPEC] * len(outs),
        compiler_params=pltpu.CompilerParams(vmem_limit_bytes=12 * 2**20),
        name="flash_last" if last else "flash_step",
    )(*[near(x) for x in ins])


def merge_body(b0, b1, b2, b3, mat, out):
    parts = (b0, b1, b2, b3)
    context = []
    for h in range(2):
        head = slice(h * HD, (h + 1) * HD)
        lses = []
        for b in parts:
            tail = b[256:272, :].astype(F32)
            lses.append(tail[3 * h : 3 * h + 1] + tail[3 * h + 1 : 3 * h + 2] + tail[3 * h + 2 : 3 * h + 3])
        top = jnp.maximum(jnp.maximum(lses[0], lses[1]), jnp.maximum(lses[2], lses[3]))
        ws = [jnp.exp2(v - top) for v in lses]
        total = ws[0] + ws[1] + ws[2] + ws[3]
        mixed = sum(b[head, :].astype(F32) * (w / total) for b, w in zip(parts, ws))
        context.append(mixed.astype(BF))
    up = dot_tn(jnp.concatenate(context, axis=0), mat[...])
    for j in range(8):
        for half in range(2):
            rows = []
            for k in range(4):
                lanes = slice((half * 4 + k) * 128, (half * 4 + k + 1) * 128)
                out[j, half, k * 32 : (k + 1) * 32, :] = up[32 * j : 32 * j + 32, lanes].astype(BF)
                token = 32 * j + 32 if k % 2 == 0 else 32 * j - 1
                inside = 0 <= token < 256
                rows.append(up[token : token + 1, lanes] if inside else jnp.zeros((1, 128), F32))
            rows.append(jnp.zeros((12, 128), F32))
            out[j, half, 128:144, :] = jnp.concatenate(rows, axis=0).astype(BF)


def merge(parts, mat):
    return pl.pallas_call(
        merge_body,
        out_shape=pltpu.VMEM((8, 2, 144, 128), BF),
        in_specs=[VMEM_SPEC] * 5,
        out_specs=VMEM_SPEC,
        compiler_params=pltpu.CompilerParams(vmem_limit_bytes=12 * 2**20),
        name="merge_heads",
    )(*[near(x) for x in parts], near(mat))


def spread_matrix():
    spread = np.zeros((144, 2, 2, 256), np.float32)
    for a in range(2):
        for bh in range(2):
            k = 2 * a + bh
            for bl in range(2):
                for token in range(32):
                    spread[k * 32 + token, a, bl, 4 * token + 2 * bh + bl] = 1
                spread[128 + k, a, bl, (128 + bl) if bh == 0 else (254 + bl)] = 1
    return spread.reshape(144, 1024)


def gelu_pair(x):
    root = math.sqrt(2.0 / math.pi)
    t = jnp.tanh(root * (x + 0.044715 * (x * x * x)))
    half = 0.5 * (1.0 + t)
    slope = half + 0.5 * x * (1.0 - t * t) * (root * (1.0 + 3 * 0.044715 * (x * x)))
    return x * half, slope


def shifted(row):
    return jnp.concatenate(
        [pltpu.roll(row, 1, 1), row, pltpu.roll(row, row.shape[1] - 1, 1)], axis=0
    )


def fine_body(factor):
    def body(flags, own, prev, nxt, spread, grad, rim, mats, bias, field, grad_fine, terms):
        spread_all = spread[...]
        ups = []
        for block in (prev[...], own[0], own[1], nxt[...]):
            wide = dot_tn(block, spread_all)
            for a in range(2):
                ups.append(
                    wide[0:64, 512 * a : 512 * a + 256] + wide[64:128, 512 * a + 256 : 512 * a + 512]
                )
        grads = [
            jnp.concatenate([grad[r].astype(F32), rim[r].astype(F32)], axis=1) for r in range(8)
        ]
        up_taps = [shifted(u).astype(BF) for u in ups]
        grad_taps = [shifted(g).astype(BF) for g in grads]
        pre_all = dot_nn(mats[0], jnp.concatenate(up_taps, axis=1))
        act_all = dot_nn(mats[1], jnp.concatenate(grad_taps, axis=1))

        def gather(products, i, width):
            return (
                products[0:64, i * width : (i + 1) * width]
                + products[64:128, (i + 1) * width : (i + 2) * width]
                + products[128:192, (i + 2) * width : (i + 3) * width]
            )

        lane = lax.broadcasted_iota(jnp.int32, (64, 256), 1)
        cols_ok = (lane < 128) | ((lane == 128) & (flags[3] > 0)) | ((lane == 255) & (flags[2] > 0))
        offset = bias[...]
        act_taps = []
        pre_taps = []
        d_rows = []
        for i in range(6):
            pre = gather(pre_all, i, 256) + offset
            value, slope = gelu_pair(pre)
            ok = cols_ok
            if i == 0:
                ok = ok & (flags[0] > 0)
            if i == 5:
                ok = ok & (flags[1] > 0)
            value = jnp.where(ok, value, 0.0)
            d_pre = jnp.where(ok, gather(act_all, i, 256) * slope, 0.0)
            act_taps.append(shifted(value)[:, 0:128].astype(BF))
            pre_taps.append(shifted(d_pre)[:, 0:128].astype(BF))
            if 1 <= i <= 4:
                d_rows.append(d_pre[:, 0:128].astype(BF))
        act_wide = jnp.concatenate(act_taps, axis=1)
        out_all = dot_nn(mats[2], act_wide)
        fine_all = dot_nn(mats[3], jnp.concatenate(pre_taps, axis=1))
        for j in range(4):
            field[j] = (
                gather(out_all, j, 128) + ups[j + 2][:, 0:128]
            ).astype(BF)
            grad_fine[j] = (gather(fine_all, j, 128) + grads[j + 2][:, 0:128]).astype(BF)
        d_own = jnp.concatenate(d_rows, axis=1)
        g_own = jnp.concatenate([grad[r] for r in range(2, 6)], axis=1)
        for p in range(3):
            up_cut = jnp.concatenate([up_taps[r][:, 0:128] for r in range(p + 1, p + 5)], axis=1)
            first = dot_nt(up_cut, d_own)
            second = dot_nt(act_wide[:, p * 128 : p * 128 + 512], g_own)
            terms[p * 192 : (p + 1) * 192, :] = (
                jnp.concatenate([first, second], axis=1) * factor
            ).astype(BF)
        ones = jnp.ones((16, 512), BF)
        third = dot_nt(ones, d_own) * factor
        terms[576:592, :] = jnp.concatenate([third, jnp.zeros((16, 64), F32)], axis=1).astype(BF)
        terms[592:768, :] = jnp.zeros((176, 128), BF)

    return body


def fine_stage(flags, own, prev, nxt, spread, grad, rim, mats, bias, factor):
    return pl.pallas_call(
        fine_body(factor),
        out_shape=[
            jax.ShapeDtypeStruct((4, 64, 128), BF),
            jax.ShapeDtypeStruct((4, 64, 128), BF),
            pltpu.VMEM((768, 128), BF),
        ],
        in_specs=[SMEM_SPEC] + [VMEM_SPEC] * 8,
        out_specs=[VMEM_SPEC] * 3,
        compiler_params=pltpu.CompilerParams(vmem_limit_bytes=20 * 2**20),
        name="fine_stage",
    )(flags, *[near(x) for x in (own, prev, nxt, spread, grad, rim, mats, bias)])


def copies(piece, axis, count):
    return lax.all_to_all(jnp.broadcast_to(piece[None], (count,) + piece.shape), axis, 0, 0)


def flip(count, bit):
    return [(i, i ^ bit) for i in range(count)]


def turn(count, step):
    return [(i, (i + step) % count) for i in range(count)]


def tap_matrix(weight):
    return jnp.transpose(weight.reshape(3, 3, C, C), (0, 3, 1, 2)).reshape(3 * C, 3 * C)


def flipped(weight):
    return jnp.transpose(weight[::-1], (0, 2, 1))


def device_step(
    patches, w_embed, var_bias, agg_gain, wq, wk, wv, wo, w_up, conv1, bias1, conv2, cotangent
):
    var_at = lax.axis_index(VAR)
    band_at = lax.axis_index(BAND)
    shift_down = [(i, i + 1) for i in range(31)]
    shift_up = [(i + 1, i) for i in range(31)]
    group = ("xh", "core")

    flattened = jnp.transpose(patches, (1, 2, 0, 3)).reshape(256, 128)
    partial_mix = jnp.dot(flattened, w_embed.reshape(128, D), preferred_element_type=F32)
    partial_mix = (partial_mix + jnp.sum(var_bias, axis=0)).astype(BF).reshape(8, 32, D)
    partial_mix, cells, wo, wk, wv = lax.optimization_barrier((partial_mix, cotangent, wo, wk, wv))
    pieces = lax.all_to_all(partial_mix, VAR, 0, 0)
    up_mat = jnp.dot(wo, w_up, preferred_element_type=F32).astype(BF)
    wkv = jnp.concatenate([wk, wv], axis=1)
    grad_rows = jnp.concatenate(
        [
            lax.ppermute(cells[2:4], BAND, shift_down),
            cells,
            lax.ppermute(cells[0:2], BAND, shift_up),
        ],
        axis=0,
    )
    pieces, up_mat, wkv, grad_rows = lax.optimization_barrier((pieces, up_mat, wkv, grad_rows))
    mixed = jnp.sum(pieces.astype(F32), axis=0)
    normed_slab = (
        mixed * lax.rsqrt(jnp.mean(mixed * mixed, axis=-1, keepdims=True) + 1e-05) * agg_gain
    ).astype(BF)
    normed_slab, grad_rows, conv1, conv2, bias1 = lax.optimization_barrier(
        (normed_slab, grad_rows, conv1, conv2, bias1)
    )
    normed = copies(normed_slab, VAR, 8).reshape(256, D)
    from_right = lax.ppermute(grad_rows[:, :, 0:2], VAR, [(i + 1, i) for i in range(7)])
    from_left = lax.ppermute(grad_rows[:, :, 126:128], VAR, [(i, i + 1) for i in range(7)])
    rim = jnp.concatenate([from_right, jnp.zeros((8, C, 124), BF), from_left], axis=2)
    mats = jnp.stack(
        [tap_matrix(conv1), tap_matrix(flipped(conv2)), tap_matrix(conv2), tap_matrix(flipped(conv1))]
    )
    bias = bias1.reshape(C, 1)
    flags = jnp.stack([band_at > 0, band_at < 31, var_at > 0, var_at < 7]).astype(jnp.int32)
    normed, rim, mats, bias, flags = lax.optimization_barrier((normed, rim, mats, bias, flags))

    queries = jnp.dot(normed, wq, preferred_element_type=F32).astype(BF)
    all_queries = [queries] + [lax.ppermute(queries, group, flip(4, k)) for k in (2, 3, 1)]
    keys_in, queries = lax.optimization_barrier((normed, queries))
    keyvals = jnp.dot(keys_in, wkv, preferred_element_type=F32).astype(BF)
    ahead, behind = keyvals, keyvals
    carry = None
    fresh = [keyvals]
    for step in range(4):
        if step == 3:
            ahead, behind = ahead[:128], behind[128:]
        ahead = lax.ppermute(ahead, "z", turn(8, 1))
        behind = lax.ppermute(behind, "z", turn(8, -1))
        carry = flash_step(all_queries, fresh, carry, False)
        ahead, behind, carry = lax.optimization_barrier((ahead, behind, carry))
        fresh = [ahead, behind]

    padded = jnp.pad(normed, ((1, 1), (0, 0)))
    around = lax.dynamic_slice_in_dim(padded, var_at * 32, 34, 0)
    base = jnp.dot(around, w_up, preferred_element_type=F32)
    base_main = jnp.transpose(base[1:33].reshape(32, 2, 4, 128), (1, 2, 0, 3)).reshape(2, 128, 128)
    left = base[0].reshape(2, 4, 128)
    right = base[33].reshape(2, 4, 128)
    base_rim = jnp.where(jnp.arange(4)[None, :, None] % 2 == 0, right, left)
    base_all = jnp.concatenate([base_main, base_rim, jnp.zeros((2, 12, 128), F32)], axis=1)

    blocks = flash_step(all_queries, fresh, carry, True)
    parts = [blocks[0]] + [lax.ppermute(b, group, flip(4, k)) for b, k in zip(blocks[1:], (2, 3, 1))]
    pieces = lax.all_to_all(merge(parts, up_mat), VAR, 0, 0)
    up = (jnp.sum(pieces.astype(F32), axis=0) + base_all).astype(BF)
    prev = lax.ppermute(up[1], BAND, shift_down)
    nxt = lax.ppermute(up[0], BAND, shift_up)
    factor = 1.0 / math.sqrt(128 * 1024)
    spread = jnp.asarray(spread_matrix(), BF)
    field_out, grad_fine, terms = fine_stage(
        flags, up, prev, nxt, spread, grad_rows, rim, mats, bias, factor
    )
    shares = lax.all_to_all(terms.reshape(32, 24, 128), PLANE, 0, 0)
    share = jnp.sum(shares.astype(F32), axis=0).astype(BF)
    share = jnp.sum(copies(share, "z", 8).astype(F32), axis=0).astype(BF)
    totals = copies(share, PLANE, 32).reshape(768, 128).astype(F32)
    grad_conv1 = totals[:576, :C].reshape(9, C, C)
    grad_conv2 = totals[:576, C:].reshape(9, C, C)
    return (field_out, grad_fine, grad_conv1, grad_conv2, totals[576, :C])


def solution(mesh):
    fine_mesh = Mesh(mesh.devices.reshape(2, 8, 2, 4, 2), BAND + VAR)
    in_specs = (
        P(VAR, BAND, None, None),
        P(VAR, None, None),
        P(VAR, None),
        P(),
        P(None, VAR),
        P(None, VAR),
        P(None, VAR),
        P(VAR, None),
        P(),
        P(),
        P(),
        P(),
        P(BAND, None, VAR),
    )
    out_specs = (P(BAND, None, VAR), P(BAND, None, VAR), P(), P(), P())
    return jax.shard_map(
        device_step, mesh=fine_mesh, in_specs=in_specs, out_specs=out_specs, check_vma=False
    )
```

```python
import math

import jax
import jax.numpy as jnp
import numpy as np
from jax import lax
from jax.experimental import pallas as pl
from jax.experimental.pallas import tpu as pltpu
from jax.sharding import Mesh, PartitionSpec as P


D = 2048
HD = 128
C = 64
BAND = ("xh", "z", "core")
VAR = ("y", "xl")
PLANE = ("xh", "core", "y", "xl")
BF = jnp.bfloat16
F32 = jnp.float32
VMEM_SPEC = pl.BlockSpec(memory_space=pltpu.VMEM)
SMEM_SPEC = pl.BlockSpec(memory_space=pltpu.SMEM)
SCORE_SCALE = math.log2(math.e) / math.sqrt(HD)


def dot_nn(a, b):
    return lax.dot_general(a, b, (((1,), (0,)), ((), ())), preferred_element_type=F32)


def dot_nt(a, b):
    return lax.dot_general(a, b, (((1,), (1,)), ((), ())), preferred_element_type=F32)


def dot_tn(a, b):
    return lax.dot_general(a, b, (((0,), (0,)), ((), ())), preferred_element_type=F32)


def near(x):
    return pltpu.with_memory_space_constraint(x, pltpu.VMEM)


def mix_body(patches, weights, offsets, out):
    lhs = patches[...]
    offset = offsets[0:1, :] + offsets[1:2, :]
    for k in range(8):
        cols = slice(k * 256, (k + 1) * 256)
        out[:, cols] = (dot_tn(lhs, weights[:, cols]) + offset[:, cols]).astype(BF)


def mix(patches, weights, offsets):
    return pl.pallas_call(
        mix_body,
        out_shape=pltpu.VMEM((256, D), BF),
        in_specs=[VMEM_SPEC] * 3,
        out_specs=VMEM_SPEC,
        compiler_params=pltpu.CompilerParams(vmem_limit_bytes=12 * 2**20),
        name="mix_variables",
    )(near(patches), near(weights), near(offsets))


def norm_body(pieces, gain, out):
    total = pieces[0].astype(F32)
    for k in range(1, 8):
        total = total + pieces[k].astype(F32)
    scale = lax.rsqrt(jnp.mean(total * total, axis=1, keepdims=True) + 1e-05)
    normed = (total * scale * gain[...]).astype(BF)
    for k in range(8):
        out[k] = normed


def norm_copies(pieces, gain):
    return pl.pallas_call(
        norm_body,
        out_shape=pltpu.VMEM((8, 32, D), BF),
        in_specs=[VMEM_SPEC] * 2,
        out_specs=VMEM_SPEC,
        compiler_params=pltpu.CompilerParams(vmem_limit_bytes=12 * 2**20),
        name="norm_slab",
    )(near(pieces), near(gain))


def flash_kernel(blocks, chunks, first, last):
    def body(*refs):
        q_refs = refs[:blocks]
        kv_refs = refs[blocks : blocks + chunks]
        rest = refs[blocks + chunks :]
        if not first:
            stat_in, acc_in = rest[0], rest[1]
            rest = rest[2:]
        for block in range(blocks):
            for part in range(2):
                inner = slice(part * 128, (part + 1) * 128)
                cols = slice(block * 256 + part * 128, block * 256 + (part + 1) * 128)
                stats = []
                for h in range(2):
                    head = slice(h * HD, (h + 1) * HD)
                    vals = slice(256 + h * HD, 256 + (h + 1) * HD)
                    q = q_refs[block][inner, head]
                    state = None
                    if not first:
                        state = (
                            stat_in[h : h + 1, cols],
                            stat_in[2 + h : 3 + h, cols],
                            acc_in[head, cols],
                        )
                    for kv in kv_refs:
                        s = dot_nt(kv[:, head], q) * SCORE_SCALE
                        top = jnp.max(s, axis=0, keepdims=True)
                        if state is not None:
                            top = jnp.maximum(top, state[0])
                        w = jnp.exp2(s - top)
                        total = jnp.sum(w, axis=0, keepdims=True)
                        update = dot_tn(kv[:, vals], w.astype(BF))
                        if state is not None:
                            shrink = jnp.exp2(state[0] - top)
                            total = total + state[1] * shrink
                            update = update + state[2] * shrink
                        state = (top, total, update)
                    top, total, update = state
                    if last:
                        rest[block][head, inner] = (update * (1.0 / total)).astype(BF)
                        lse = top + jnp.log2(total)
                        high = lse.astype(BF)
                        left = lse - high.astype(F32)
                        mid = left.astype(BF)
                        low = (left - mid.astype(F32)).astype(BF)
                        stats += [high.astype(F32), mid.astype(F32), low.astype(F32)]
                    else:
                        rest[1][head, cols] = update
                        stats += [top, total]
                if last:
                    stats.append(jnp.zeros((10, 128), F32))
                    rest[block][256:272, inner] = jnp.concatenate(stats, axis=0).astype(BF)
                else:
                    for h in range(2):
                        rest[0][h : h + 1, cols] = stats[2 * h]
                        rest[0][2 + h : 3 + h, cols] = stats[2 * h + 1]

    return body


def flash_step(queries, chunks, carry, last):
    blocks = len(queries)
    first = carry is None
    ins = list(queries) + list(chunks) + ([] if first else list(carry))
    if last:
        outs = [pltpu.VMEM((272, 256), BF)] * blocks
    else:
        outs = [
            pltpu.VMEM((8, 256 * blocks), F32),
            pltpu.VMEM((256, 256 * blocks), F32),
        ]
    return pl.pallas_call(
        flash_kernel(blocks, len(chunks), first, last),
        out_shape=outs,
        in_specs=[VMEM_SPEC] * len(ins),
        out_specs=[VMEM_SPEC] * len(outs),
        compiler_params=pltpu.CompilerParams(vmem_limit_bytes=12 * 2**20),
        name="flash_last" if last else "flash_step",
    )(*[near(x) for x in ins])


def merge_body(b0, b1, b2, b3, mat, out):
    parts = (b0, b1, b2, b3)
    context = []
    for h in range(2):
        head = slice(h * HD, (h + 1) * HD)
        lses = []
        for b in parts:
            tail = b[256:272, :].astype(F32)
            lses.append(tail[3 * h : 3 * h + 1] + tail[3 * h + 1 : 3 * h + 2] + tail[3 * h + 2 : 3 * h + 3])
        top = jnp.maximum(jnp.maximum(lses[0], lses[1]), jnp.maximum(lses[2], lses[3]))
        ws = [jnp.exp2(v - top) for v in lses]
        total = ws[0] + ws[1] + ws[2] + ws[3]
        mixed = sum(b[head, :].astype(F32) * (w / total) for b, w in zip(parts, ws))
        context.append(mixed.astype(BF))
    up = dot_tn(jnp.concatenate(context, axis=0), mat[...])
    for j in range(8):
        for half in range(2):
            rows = []
            for k in range(4):
                lanes = slice((half * 4 + k) * 128, (half * 4 + k + 1) * 128)
                out[j, half, k * 32 : (k + 1) * 32, :] = up[32 * j : 32 * j + 32, lanes].astype(BF)
                token = 32 * j + 32 if k % 2 == 0 else 32 * j - 1
                inside = 0 <= token < 256
                rows.append(up[token : token + 1, lanes] if inside else jnp.zeros((1, 128), F32))
            rows.append(jnp.zeros((12, 128), F32))
            out[j, half, 128:144, :] = jnp.concatenate(rows, axis=0).astype(BF)


def merge(parts, mat):
    return pl.pallas_call(
        merge_body,
        out_shape=pltpu.VMEM((8, 2, 144, 128), BF),
        in_specs=[VMEM_SPEC] * 5,
        out_specs=VMEM_SPEC,
        compiler_params=pltpu.CompilerParams(vmem_limit_bytes=12 * 2**20),
        name="merge_heads",
    )(*[near(x) for x in parts], near(mat))


def spread_matrix():
    spread = np.zeros((144, 2, 2, 256), np.float32)
    for a in range(2):
        for bh in range(2):
            k = 2 * a + bh
            for bl in range(2):
                for token in range(32):
                    spread[k * 32 + token, a, bl, 4 * token + 2 * bh + bl] = 1
                spread[128 + k, a, bl, (128 + bl) if bh == 0 else (254 + bl)] = 1
    return spread.reshape(144, 1024)


def edge_matrix():
    edges = np.zeros((2, 2, 8, 8, 128), np.float32)
    for q in range(2):
        for r in range(8):
            edges[0, q, r, r, q] = 1
            edges[1, q, r, r, 126 + q] = 1
    return edges.reshape(32, 1024)


def gelu_pair(x):
    root = math.sqrt(2.0 / math.pi)
    t = jnp.tanh(root * (x + 0.044715 * (x * x * x)))
    half = 0.5 * (1.0 + t)
    slope = half + 0.5 * x * (1.0 - t * t) * (root * (1.0 + 3 * 0.044715 * (x * x)))
    return x * half, slope


def shifted(row):
    return jnp.concatenate(
        [pltpu.roll(row, 1, 1), row, pltpu.roll(row, row.shape[1] - 1, 1)], axis=0
    )


def fine_body(factor):
    def body(flags, own, near_up, far_up, spread, edges, grad, rim, mats, bias, field, grad_fine, terms):
        spread_all = spread[...]
        ups = []
        second_core = flags[4] > 0
        close, distant = near_up[...].astype(F32), far_up[...].astype(F32)
        prev = jnp.where(second_core, close, distant).astype(BF)
        nxt = jnp.where(second_core, distant, close).astype(BF)
        for block in (prev, own[0], own[1], nxt):
            wide = dot_tn(block, spread_all)
            for a in range(2):
                ups.append(
                    wide[0:64, 512 * a : 512 * a + 256] + wide[64:128, 512 * a + 256 : 512 * a + 512]
                )
        rims = dot_tn(rim[...], edges[...])
        grads = [
            jnp.concatenate([grad[r].astype(F32), rims[:, r * 128 : (r + 1) * 128]], axis=1)
            for r in range(8)
        ]
        up_taps = [shifted(u).astype(BF) for u in ups]
        grad_taps = [shifted(g).astype(BF) for g in grads]
        pre_all = dot_nn(mats[0], jnp.concatenate(up_taps, axis=1))
        act_all = dot_nn(mats[1], jnp.concatenate(grad_taps, axis=1))

        def gather(products, i, width):
            return (
                products[0:64, i * width : (i + 1) * width]
                + products[64:128, (i + 1) * width : (i + 2) * width]
                + products[128:192, (i + 2) * width : (i + 3) * width]
            )

        lane = lax.broadcasted_iota(jnp.int32, (64, 256), 1)
        cols_ok = (lane < 128) | ((lane == 128) & (flags[3] > 0)) | ((lane == 255) & (flags[2] > 0))
        offset = bias[...]
        act_taps = []
        pre_taps = []
        d_rows = []
        for i in range(6):
            pre = gather(pre_all, i, 256) + offset
            value, slope = gelu_pair(pre)
            ok = cols_ok
            if i == 0:
                ok = ok & (flags[0] > 0)
            if i == 5:
                ok = ok & (flags[1] > 0)
            value = jnp.where(ok, value, 0.0)
            d_pre = jnp.where(ok, gather(act_all, i, 256) * slope, 0.0)
            act_taps.append(shifted(value)[:, 0:128].astype(BF))
            pre_taps.append(shifted(d_pre)[:, 0:128].astype(BF))
            if 1 <= i <= 4:
                d_rows.append(d_pre[:, 0:128].astype(BF))
        act_wide = jnp.concatenate(act_taps, axis=1)
        out_all = dot_nn(mats[2], act_wide)
        fine_all = dot_nn(mats[3], jnp.concatenate(pre_taps, axis=1))
        for j in range(4):
            field[j] = (
                gather(out_all, j, 128) + ups[j + 2][:, 0:128]
            ).astype(BF)
            grad_fine[j] = (gather(fine_all, j, 128) + grads[j + 2][:, 0:128]).astype(BF)
        d_own = jnp.concatenate(d_rows, axis=1)
        g_own = jnp.concatenate([grad[r] for r in range(2, 6)], axis=1)
        for p in range(3):
            up_cut = jnp.concatenate([up_taps[r][:, 0:128] for r in range(p + 1, p + 5)], axis=1)
            first = dot_nt(up_cut, d_own)
            second = dot_nt(act_wide[:, p * 128 : p * 128 + 512], g_own)
            terms[p * 192 : (p + 1) * 192, :] = (
                jnp.concatenate([first, second], axis=1) * factor
            ).astype(BF)
        ones = jnp.ones((16, 512), BF)
        third = dot_nt(ones, d_own) * factor
        terms[576:592, :] = jnp.concatenate([third, jnp.zeros((16, 64), F32)], axis=1).astype(BF)
        terms[592:768, :] = jnp.zeros((176, 128), BF)

    return body


def fine_stage(flags, own, near_up, far_up, spread, edges, grad, rim, mats, bias, factor):
    return pl.pallas_call(
        fine_body(factor),
        out_shape=[
            jax.ShapeDtypeStruct((4, 64, 128), BF),
            jax.ShapeDtypeStruct((4, 64, 128), BF),
            pltpu.VMEM((768, 128), BF),
        ],
        in_specs=[SMEM_SPEC] + [VMEM_SPEC] * 9,
        out_specs=[VMEM_SPEC] * 3,
        compiler_params=pltpu.CompilerParams(vmem_limit_bytes=20 * 2**20),
        name="fine_stage",
    )(flags, *[near(x) for x in (own, near_up, far_up, spread, edges, grad, rim, mats, bias)])


def copies(piece, axis, count):
    return lax.all_to_all(jnp.broadcast_to(piece[None], (count,) + piece.shape), axis, 0, 0)


def flip(count, bit):
    return [(i, i ^ bit) for i in range(count)]


def turn(count, step):
    return [(i, (i + step) % count) for i in range(count)]


def tap_matrix(weight):
    return jnp.transpose(weight.reshape(3, 3, C, C), (0, 3, 1, 2)).reshape(3 * C, 3 * C)


def flipped(weight):
    return jnp.transpose(weight[::-1], (0, 2, 1))


def device_step(
    patches, w_embed, var_bias, agg_gain, wq, wk, wv, wo, w_up, conv1, bias1, conv2, cotangent
):
    var_at = lax.axis_index(VAR)
    band_at = lax.axis_index(BAND)
    shift_down = [(i, i + 1) for i in range(31)]
    shift_up = [(i + 1, i) for i in range(31)]
    group = ("xh", "core")

    core_at = lax.axis_index("core")
    turned = jnp.transpose(patches, (0, 1, 3, 2)).reshape(128, 256)
    partial_mix = mix(turned, w_embed.reshape(128, D), var_bias).reshape(8, 32, D)
    partial_mix, cells, wo, wk, wv = lax.optimization_barrier((partial_mix, cotangent, wo, wk, wv))
    pieces = lax.all_to_all(partial_mix, VAR, 0, 0)
    up_mat = jnp.dot(wo, w_up, preferred_element_type=F32).astype(BF)
    wkv = jnp.concatenate([wk, wv], axis=1)
    grad_rows = jnp.concatenate(
        [
            lax.ppermute(cells[2:4], BAND, shift_down),
            cells,
            lax.ppermute(cells[0:2], BAND, shift_up),
        ],
        axis=0,
    )
    pieces, up_mat, wkv, grad_rows = lax.optimization_barrier((pieces, up_mat, wkv, grad_rows))
    spread_out = norm_copies(pieces, agg_gain.reshape(1, D))
    spread_out, grad_rows, conv1, conv2, bias1 = lax.optimization_barrier(
        (spread_out, grad_rows, conv1, conv2, bias1)
    )
    normed = lax.all_to_all(spread_out, VAR, 0, 0).reshape(256, D)
    edge_right = jnp.transpose(grad_rows[:, :, 0:2], (2, 0, 1)).reshape(16, C)
    edge_left = jnp.transpose(grad_rows[:, :, 126:128], (2, 0, 1)).reshape(16, C)
    mats = jnp.stack(
        [tap_matrix(conv1), tap_matrix(flipped(conv2)), tap_matrix(conv2), tap_matrix(flipped(conv1))]
    )
    bias = bias1.reshape(C, 1)
    flags = jnp.stack(
        [band_at > 0, band_at < 31, var_at > 0, var_at < 7, core_at > 0]
    ).astype(jnp.int32)
    normed, edge_right, edge_left, mats, bias, flags = lax.optimization_barrier(
        (normed, edge_right, edge_left, mats, bias, flags)
    )

    keyvals = jnp.dot(normed, wkv, preferred_element_type=F32).astype(BF)
    ahead = lax.ppermute(keyvals, "z", turn(8, 1))
    behind = lax.ppermute(keyvals, "z", turn(8, -1))
    queries = jnp.dot(normed, wq, preferred_element_type=F32).astype(BF)
    all_queries = [queries] + [lax.ppermute(queries, group, flip(4, k)) for k in (2, 3, 1)]
    fresh = [keyvals, ahead, behind]
    ahead = lax.ppermute(ahead, "z", turn(8, 1))
    behind = lax.ppermute(behind, "z", turn(8, -1))
    padded = jnp.pad(normed, ((1, 1), (0, 0)))
    around = lax.dynamic_slice_in_dim(padded, var_at * 32, 34, 0)
    carry = flash_step(all_queries, fresh, None, False)
    ahead, behind, carry, edge_right, edge_left, around = lax.optimization_barrier(
        (ahead, behind, carry, edge_right, edge_left, around)
    )
    from_right = lax.ppermute(edge_right, VAR, [(i + 1, i) for i in range(7)])
    from_left = lax.ppermute(edge_left, VAR, [(i, i + 1) for i in range(7)])
    for step in (2, 3):
        fresh = [ahead, behind]
        if step == 3:
            ahead, behind = ahead[:128], behind[128:]
        ahead = lax.ppermute(ahead, "z", turn(8, 1))
        behind = lax.ppermute(behind, "z", turn(8, -1))
        carry = flash_step(all_queries, fresh, carry, False)
        ahead, behind, carry, from_right, from_left = lax.optimization_barrier(
            (ahead, behind, carry, from_right, from_left)
        )
    fresh = [ahead, behind]
    rim = jnp.concatenate([from_right, from_left], axis=0)

    base = jnp.dot(around, w_up, preferred_element_type=F32)
    base_main = jnp.transpose(base[1:33].reshape(32, 2, 4, 128), (1, 2, 0, 3)).reshape(2, 128, 128)
    left = base[0].reshape(2, 4, 128)
    right = base[33].reshape(2, 4, 128)
    base_rim = jnp.where(jnp.arange(4)[None, :, None] % 2 == 0, right, left)
    base_all = jnp.concatenate([base_main, base_rim, jnp.zeros((2, 12, 128), F32)], axis=1)

    blocks = flash_step(all_queries, fresh, carry, True)
    parts = [blocks[0]] + [lax.ppermute(b, group, flip(4, k)) for b, k in zip(blocks[1:], (2, 3, 1))]
    pieces = lax.all_to_all(merge(parts, up_mat), VAR, 0, 0)
    up = (jnp.sum(pieces.astype(F32), axis=0) + base_all).astype(BF)
    near_up = lax.ppermute(lax.dynamic_index_in_dim(up, 1 - core_at, 0, False), "core", flip(2, 1))
    pairs = [(i, i + 1) for i in range(1, 31, 2)] + [(i + 1, i) for i in range(1, 31, 2)]
    far_up = lax.ppermute(lax.dynamic_index_in_dim(up, core_at, 0, False), BAND, pairs)
    factor = 1.0 / math.sqrt(128 * 1024)
    spread = jnp.asarray(spread_matrix(), BF)
    field_out, grad_fine, terms = fine_stage(
        flags, up, near_up, far_up, spread, jnp.asarray(edge_matrix(), BF), grad_rows, rim, mats, bias, factor
    )
    shares = lax.all_to_all(terms.reshape(32, 24, 128), PLANE, 0, 0)
    share = jnp.sum(shares.astype(F32), axis=0).astype(BF)
    share = jnp.sum(copies(share, "z", 8).astype(F32), axis=0).astype(BF)
    totals = copies(share, PLANE, 32).reshape(768, 128).astype(F32)
    grad_conv1 = totals[:576, :C].reshape(9, C, C)
    grad_conv2 = totals[:576, C:].reshape(9, C, C)
    return (field_out, grad_fine, grad_conv1, grad_conv2, totals[576, :C])


def solution(mesh):
    fine_mesh = Mesh(mesh.devices.reshape(2, 8, 2, 4, 2), BAND + VAR)
    in_specs = (
        P(VAR, BAND, None, None),
        P(VAR, None, None),
        P(VAR, None),
        P(),
        P(None, VAR),
        P(None, VAR),
        P(None, VAR),
        P(VAR, None),
        P(),
        P(),
        P(),
        P(),
        P(BAND, None, VAR),
    )
    out_specs = (P(BAND, None, VAR), P(BAND, None, VAR), P(), P(), P())
    return jax.shard_map(
        device_step, mesh=fine_mesh, in_specs=in_specs, out_specs=out_specs, check_vma=False
    )
```

```python
import math

import jax
import jax.numpy as jnp
import numpy as np
from jax import lax
from jax.experimental import pallas as pl
from jax.experimental.pallas import tpu as pltpu
from jax.sharding import Mesh, PartitionSpec as P


D = 2048
HD = 128
C = 64
BAND = ("xh", "z", "core")
VAR = ("y", "xl")
PLANE = ("xh", "core", "y", "xl")
BF = jnp.bfloat16
F32 = jnp.float32
VMEM_SPEC = pl.BlockSpec(memory_space=pltpu.VMEM)
SMEM_SPEC = pl.BlockSpec(memory_space=pltpu.SMEM)
SCORE_SCALE = math.log2(math.e) / math.sqrt(HD)


def dot_nn(a, b):
    return lax.dot_general(a, b, (((1,), (0,)), ((), ())), preferred_element_type=F32)


def dot_nt(a, b):
    return lax.dot_general(a, b, (((1,), (1,)), ((), ())), preferred_element_type=F32)


def dot_tn(a, b):
    return lax.dot_general(a, b, (((0,), (0,)), ((), ())), preferred_element_type=F32)


def near(x):
    return pltpu.with_memory_space_constraint(x, pltpu.VMEM)


def mix_body(patches, weights, offsets, out):
    lhs = patches[...]
    offset = offsets[0:1, :] + offsets[1:2, :]
    for k in range(8):
        cols = slice(k * 256, (k + 1) * 256)
        out[:, cols] = (dot_tn(lhs, weights[:, cols]) + offset[:, cols]).astype(BF)


def mix(patches, weights, offsets):
    return pl.pallas_call(
        mix_body,
        out_shape=pltpu.VMEM((256, D), BF),
        in_specs=[VMEM_SPEC] * 3,
        out_specs=VMEM_SPEC,
        compiler_params=pltpu.CompilerParams(vmem_limit_bytes=12 * 2**20),
        name="mix_variables",
    )(near(patches), near(weights), near(offsets))


def norm_body(pieces, gain, out, slab):
    total = pieces[0].astype(F32)
    for k in range(1, 8):
        total = total + pieces[k].astype(F32)
    scale = lax.rsqrt(jnp.mean(total * total, axis=1, keepdims=True) + 1e-05)
    normed = (total * scale * gain[...]).astype(BF)
    slab[...] = normed
    for k in range(8):
        out[k] = normed


def norm_copies(pieces, gain):
    return pl.pallas_call(
        norm_body,
        out_shape=[pltpu.VMEM((8, 32, D), BF), pltpu.VMEM((32, D), BF)],
        in_specs=[VMEM_SPEC] * 2,
        out_specs=[VMEM_SPEC] * 2,
        compiler_params=pltpu.CompilerParams(vmem_limit_bytes=12 * 2**20),
        name="norm_slab",
    )(near(pieces), near(gain))


def flash_kernel(blocks, chunks, first, last):
    def body(*refs):
        q_refs = refs[:blocks]
        kv_refs = refs[blocks : blocks + chunks]
        rest = refs[blocks + chunks :]
        if not first:
            stat_in, acc_in = rest[0], rest[1]
            rest = rest[2:]
        if last:
            stat_scr, acc_scr, whole = rest[blocks], rest[blocks + 1], rest[blocks + 2]
            for k in range(chunks):
                whole[k * 128 : (k + 1) * 128, :] = kv_refs[k][...]
            kv_refs = [whole]
        for block in range(blocks):
            for part in range(2):
                inner = slice(part * 128, (part + 1) * 128)
                cols = slice(block * 256 + part * 128, block * 256 + (part + 1) * 128)
                for h in range(2):
                    head = slice(h * HD, (h + 1) * HD)
                    vals = slice(256 + h * HD, 256 + (h + 1) * HD)
                    q = q_refs[block][inner, head]
                    state = None
                    if not first:
                        state = (
                            stat_in[h : h + 1, cols],
                            stat_in[2 + h : 3 + h, cols],
                            acc_in[head, cols],
                        )
                    for kv in kv_refs:
                        s = dot_nt(kv[:, head], q) * SCORE_SCALE
                        top = jnp.max(s, axis=0, keepdims=True)
                        if state is not None:
                            top = jnp.maximum(top, state[0])
                        w = jnp.exp2(s - top)
                        total = jnp.sum(w, axis=0, keepdims=True)
                        update = dot_tn(kv[:, vals], w.astype(BF))
                        if state is not None:
                            shrink = jnp.exp2(state[0] - top)
                            total = total + state[1] * shrink
                            update = update + state[2] * shrink
                        state = (top, total, update)
                    top, total, update = state
                    if last:
                        acc_scr[head, cols] = update
                        stat_scr[h : h + 1, cols] = top
                        stat_scr[2 + h : 3 + h, cols] = total
                    else:
                        rest[1][head, cols] = update
                        rest[0][h : h + 1, cols] = top
                        rest[0][2 + h : 3 + h, cols] = total
        if last:
            rows = []
            for r in (0, 2, 1, 3):
                value = stat_scr[r : r + 1, :]
                high = value.astype(BF).astype(F32)
                mid = (value - high).astype(BF).astype(F32)
                rows += [high, mid, value - high - mid]
            rows.append(jnp.zeros((4, 256 * blocks), F32))
            tail = jnp.concatenate(rows, axis=0).astype(BF)
            for block in range(blocks):
                cols = slice(block * 256, (block + 1) * 256)
                rest[block][0:256, :] = acc_scr[:, cols].astype(BF)
                rest[block][256:272, :] = tail[:, cols]

    return body


def flash_step(queries, chunks, carry, last):
    blocks = len(queries)
    first = carry is None
    ins = list(queries) + list(chunks) + ([] if first else list(carry))
    if last:
        outs = [pltpu.VMEM((272, 256), BF)] * blocks
    else:
        outs = [
            pltpu.VMEM((8, 256 * blocks), F32),
            pltpu.VMEM((256, 256 * blocks), F32),
        ]
    return pl.pallas_call(
        flash_kernel(blocks, len(chunks), first, last),
        out_shape=outs,
        in_specs=[VMEM_SPEC] * len(ins),
        out_specs=[VMEM_SPEC] * len(outs),
        scratch_shapes=[
            pltpu.VMEM((8, 256 * blocks), F32),
            pltpu.VMEM((256, 256 * blocks), F32),
            pltpu.VMEM((256, 512), BF),
        ]
        if last
        else [],
        compiler_params=pltpu.CompilerParams(vmem_limit_bytes=12 * 2**20),
        name="flash_last" if last else "flash_step",
    )(*[near(x) for x in ins])


def merge_body(place, base, b0, b1, b2, b3, mat, out):
    parts = (b0, b1, b2, b3)
    tails = [b[256:272, :].astype(F32) for b in parts]
    context = []
    for h in range(2):
        head = slice(h * HD, (h + 1) * HD)

        def whole(tail, row):
            return tail[row : row + 1] + tail[row + 1 : row + 2] + tail[row + 2 : row + 3]

        tops = [whole(tail, 6 * h) for tail in tails]
        top = jnp.maximum(jnp.maximum(tops[0], tops[1]), jnp.maximum(tops[2], tops[3]))
        ws = [jnp.exp2(v - top) for v in tops]
        total = sum(whole(tail, 6 * h + 3) * w for tail, w in zip(tails, ws))
        share = 1.0 / total
        mixed = sum(b[head, :].astype(F32) * (w * share) for b, w in zip(parts, ws))
        context.append(mixed.astype(BF))
    up = dot_tn(jnp.concatenate(context, axis=0), mat[...])
    own = place[0]
    for j in range(8):
        lower = jnp.where(own == j - 1, base[31:32, :], 0.0)
        upper = jnp.where(own == j + 1, base[0:1, :], 0.0)
        for half in range(2):
            rows = []
            for k in range(4):
                lanes = slice((half * 4 + k) * 128, (half * 4 + k + 1) * 128)
                out[j, half, k * 32 : (k + 1) * 32, :] = up[32 * j : 32 * j + 32, lanes].astype(BF)
                token = 32 * j + 32 if k % 2 == 0 else 32 * j - 1
                edge = upper if k % 2 == 0 else lower
                if 0 <= token < 256:
                    rows.append(up[token : token + 1, lanes] + edge[:, lanes])
                else:
                    rows.append(jnp.zeros((1, 128), F32))
            rows.append(jnp.zeros((12, 128), F32))
            out[j, half, 128:144, :] = jnp.concatenate(rows, axis=0).astype(BF)


def merge(place, base, parts, mat):
    return pl.pallas_call(
        merge_body,
        out_shape=pltpu.VMEM((8, 2, 144, 128), BF),
        in_specs=[SMEM_SPEC] + [VMEM_SPEC] * 6,
        out_specs=VMEM_SPEC,
        compiler_params=pltpu.CompilerParams(vmem_limit_bytes=12 * 2**20),
        name="merge_heads",
    )(place, near(base), *[near(x) for x in parts], near(mat))


def spread_matrix():
    spread = np.zeros((144, 2, 2, 256), np.float32)
    for a in range(2):
        for bh in range(2):
            k = 2 * a + bh
            for bl in range(2):
                for token in range(32):
                    spread[k * 32 + token, a, bl, 4 * token + 2 * bh + bl] = 1
                spread[128 + k, a, bl, (128 + bl) if bh == 0 else (254 + bl)] = 1
    return spread.reshape(144, 1024)


def edge_matrix():
    edges = np.zeros((2, 2, 8, 8, 128), np.float32)
    for q in range(2):
        for r in range(8):
            edges[0, q, r, r, q] = 1
            edges[1, q, r, r, 126 + q] = 1
    return edges.reshape(32, 1024)


def gelu_pair(x):
    root = math.sqrt(2.0 / math.pi)
    t = jnp.tanh(root * (x + 0.044715 * (x * x * x)))
    half = 0.5 * (1.0 + t)
    slope = half + 0.5 * x * (1.0 - t * t) * (root * (1.0 + 3 * 0.044715 * (x * x)))
    return x * half, slope


def shifted(row):
    return jnp.concatenate(
        [pltpu.roll(row, 1, 1), row, pltpu.roll(row, row.shape[1] - 1, 1)], axis=0
    )


def fine_body(factor):
    def body(flags, own, near_up, far_up, spread, edges, grad, rim, mats, bias, field, grad_fine, terms):
        spread_all = spread[...]
        ups = []
        second_core = flags[4] > 0
        close, distant = near_up[...].astype(F32), far_up[...].astype(F32)
        prev = jnp.where(second_core, close, distant).astype(BF)
        nxt = jnp.where(second_core, distant, close).astype(BF)
        for block in (prev, own[0], own[1], nxt):
            wide = dot_tn(block, spread_all)
            for a in range(2):
                ups.append(
                    wide[0:64, 512 * a : 512 * a + 256] + wide[64:128, 512 * a + 256 : 512 * a + 512]
                )
        rims = dot_tn(rim[...], edges[...])
        grads = [
            jnp.concatenate([grad[r].astype(F32), rims[:, r * 128 : (r + 1) * 128]], axis=1)
            for r in range(8)
        ]
        up_taps = [shifted(u).astype(BF) for u in ups]
        grad_taps = [shifted(g).astype(BF) for g in grads]
        pre_all = dot_nn(mats[0], jnp.concatenate(up_taps, axis=1))
        act_all = dot_nn(mats[1], jnp.concatenate(grad_taps, axis=1))

        def gather(products, i, width):
            return (
                products[0:64, i * width : (i + 1) * width]
                + products[64:128, (i + 1) * width : (i + 2) * width]
                + products[128:192, (i + 2) * width : (i + 3) * width]
            )

        lane = lax.broadcasted_iota(jnp.int32, (64, 256), 1)
        cols_ok = (lane < 128) | ((lane == 128) & (flags[3] > 0)) | ((lane == 255) & (flags[2] > 0))
        offset = bias[...]
        act_taps = []
        pre_taps = []
        d_rows = []
        for i in range(6):
            pre = gather(pre_all, i, 256) + offset
            value, slope = gelu_pair(pre)
            ok = cols_ok
            if i == 0:
                ok = ok & (flags[0] > 0)
            if i == 5:
                ok = ok & (flags[1] > 0)
            value = jnp.where(ok, value, 0.0)
            d_pre = jnp.where(ok, gather(act_all, i, 256) * slope, 0.0)
            act_taps.append(shifted(value)[:, 0:128].astype(BF))
            pre_taps.append(shifted(d_pre)[:, 0:128].astype(BF))
            if 1 <= i <= 4:
                d_rows.append(d_pre[:, 0:128].astype(BF))
        act_wide = jnp.concatenate(act_taps, axis=1)
        out_all = dot_nn(mats[2], act_wide)
        fine_all = dot_nn(mats[3], jnp.concatenate(pre_taps, axis=1))
        for j in range(4):
            field[j] = (
                gather(out_all, j, 128) + ups[j + 2][:, 0:128]
            ).astype(BF)
            grad_fine[j] = (gather(fine_all, j, 128) + grads[j + 2][:, 0:128]).astype(BF)
        d_own = jnp.concatenate(d_rows, axis=1)
        g_own = jnp.concatenate([grad[r] for r in range(2, 6)], axis=1)
        for p in range(3):
            up_cut = jnp.concatenate([up_taps[r][:, 0:128] for r in range(p + 1, p + 5)], axis=1)
            first = dot_nt(up_cut, d_own)
            second = dot_nt(act_wide[:, p * 128 : p * 128 + 512], g_own)
            terms[p * 192 : (p + 1) * 192, :] = (
                jnp.concatenate([first, second], axis=1) * factor
            ).astype(BF)
        ones = jnp.ones((16, 512), BF)
        third = dot_nt(ones, d_own) * factor
        terms[576:592, :] = jnp.concatenate([third, jnp.zeros((16, 64), F32)], axis=1).astype(BF)
        terms[592:768, :] = jnp.zeros((176, 128), BF)

    return body


def fine_stage(flags, own, near_up, far_up, spread, edges, grad, rim, mats, bias, factor):
    return pl.pallas_call(
        fine_body(factor),
        out_shape=[
            jax.ShapeDtypeStruct((4, 64, 128), BF),
            jax.ShapeDtypeStruct((4, 64, 128), BF),
            pltpu.VMEM((768, 128), BF),
        ],
        in_specs=[SMEM_SPEC] + [VMEM_SPEC] * 9,
        out_specs=[VMEM_SPEC] * 3,
        compiler_params=pltpu.CompilerParams(vmem_limit_bytes=20 * 2**20),
        name="fine_stage",
    )(flags, *[near(x) for x in (own, near_up, far_up, spread, edges, grad, rim, mats, bias)])


def copies(piece, axis, count):
    return lax.all_to_all(jnp.broadcast_to(piece[None], (count,) + piece.shape), axis, 0, 0)


def flip(count, bit):
    return [(i, i ^ bit) for i in range(count)]


def turn(count, step):
    return [(i, (i + step) % count) for i in range(count)]


def tap_matrix(weight):
    return jnp.transpose(weight.reshape(3, 3, C, C), (0, 3, 1, 2)).reshape(3 * C, 3 * C)


def flipped(weight):
    return jnp.transpose(weight[::-1], (0, 2, 1))


def device_step(
    patches, w_embed, var_bias, agg_gain, wq, wk, wv, wo, w_up, conv1, bias1, conv2, cotangent
):
    var_at = lax.axis_index(VAR)
    band_at = lax.axis_index(BAND)
    shift_down = [(i, i + 1) for i in range(31)]
    shift_up = [(i + 1, i) for i in range(31)]
    group = ("xh", "core")

    core_at = lax.axis_index("core")
    turned = jnp.transpose(patches, (0, 1, 3, 2)).reshape(128, 256)
    partial_mix = mix(turned, w_embed.reshape(128, D), var_bias).reshape(8, 32, D)
    partial_mix, cells, wo, wk, wv = lax.optimization_barrier((partial_mix, cotangent, wo, wk, wv))
    pieces = lax.all_to_all(partial_mix, VAR, 0, 0)
    up_mat = jnp.dot(wo, w_up, preferred_element_type=F32).astype(BF)
    wkv = jnp.concatenate([wk, wv], axis=1)
    grad_rows = jnp.concatenate(
        [
            lax.ppermute(cells[2:4], BAND, shift_down),
            cells,
            lax.ppermute(cells[0:2], BAND, shift_up),
        ],
        axis=0,
    )
    pieces, up_mat, wkv, grad_rows = lax.optimization_barrier((pieces, up_mat, wkv, grad_rows))
    spread_out, slab = norm_copies(pieces, agg_gain.reshape(1, D))
    spread_out, slab, grad_rows, conv1, conv2, bias1 = lax.optimization_barrier(
        (spread_out, slab, grad_rows, conv1, conv2, bias1)
    )
    normed = lax.all_to_all(spread_out, VAR, 0, 0).reshape(256, D)
    edge_right = jnp.transpose(grad_rows[:, :, 0:2], (2, 0, 1)).reshape(16, C)
    edge_left = jnp.transpose(grad_rows[:, :, 126:128], (2, 0, 1)).reshape(16, C)
    from_right = lax.ppermute(edge_right, VAR, [(i + 1, i) for i in range(7)])
    from_left = lax.ppermute(edge_left, VAR, [(i, i + 1) for i in range(7)])
    rim = jnp.concatenate([from_right, from_left], axis=0)
    base = jnp.dot(slab, w_up, preferred_element_type=F32)
    mats = jnp.stack(
        [tap_matrix(conv1), tap_matrix(flipped(conv2)), tap_matrix(conv2), tap_matrix(flipped(conv1))]
    )
    bias = bias1.reshape(C, 1)
    flags = jnp.stack(
        [band_at > 0, band_at < 31, var_at > 0, var_at < 7, core_at > 0]
    ).astype(jnp.int32)
    normed, rim, base, mats, bias, flags = lax.optimization_barrier(
        (normed, rim, base, mats, bias, flags)
    )

    keyvals = jnp.dot(normed, wkv, preferred_element_type=F32).astype(BF)
    ahead = lax.ppermute(keyvals, "z", turn(8, 1))
    behind = lax.ppermute(keyvals, "z", turn(8, -1))
    queries = jnp.dot(normed, wq, preferred_element_type=F32).astype(BF)
    all_queries = [queries] + [lax.ppermute(queries, group, flip(4, k)) for k in (2, 3, 1)]
    fresh = [keyvals, ahead, behind]
    ahead = lax.ppermute(ahead, "z", turn(8, 1))
    behind = lax.ppermute(behind, "z", turn(8, -1))
    carry = flash_step(all_queries, fresh, None, False)
    ahead, behind, carry = lax.optimization_barrier((ahead, behind, carry))
    for step in (2, 3):
        fresh = [ahead, behind]
        if step == 3:
            ahead, behind = ahead[:128], behind[128:]
        ahead = lax.ppermute(ahead, "z", turn(8, 1))
        behind = lax.ppermute(behind, "z", turn(8, -1))
        carry = flash_step(all_queries, fresh, carry, False)
        ahead, behind, carry = lax.optimization_barrier((ahead, behind, carry))
    fresh = [ahead, behind]

    blocks = flash_step(all_queries, fresh, carry, True)
    parts = [blocks[0]] + [lax.ppermute(b, group, flip(4, k)) for b, k in zip(blocks[1:], (2, 3, 1))]
    place = var_at.reshape(1).astype(jnp.int32)
    pieces = lax.all_to_all(merge(place, base, parts, up_mat), VAR, 0, 0)
    base_main = jnp.transpose(base.reshape(32, 2, 4, 128), (1, 2, 0, 3)).reshape(2, 128, 128)
    base_all = jnp.pad(base_main, ((0, 0), (0, 16), (0, 0)))
    up = (jnp.sum(pieces.astype(F32), axis=0) + base_all).astype(BF)
    near_up = lax.ppermute(lax.dynamic_index_in_dim(up, 1 - core_at, 0, False), "core", flip(2, 1))
    pairs = [(i, i + 1) for i in range(1, 31, 2)] + [(i + 1, i) for i in range(1, 31, 2)]
    far_up = lax.ppermute(lax.dynamic_index_in_dim(up, core_at, 0, False), BAND, pairs)
    factor = 1.0 / math.sqrt(128 * 1024)
    spread = jnp.asarray(spread_matrix(), BF)
    field_out, grad_fine, terms = fine_stage(
        flags, up, near_up, far_up, spread, jnp.asarray(edge_matrix(), BF), grad_rows, rim, mats, bias, factor
    )
    shares = lax.all_to_all(terms.reshape(32, 24, 128), PLANE, 0, 0)
    share = jnp.sum(shares.astype(F32), axis=0).astype(BF)
    share = jnp.sum(copies(share, "z", 8).astype(F32), axis=0).astype(BF)
    totals = copies(share, PLANE, 32).reshape(768, 128).astype(F32)
    grad_conv1 = totals[:576, :C].reshape(9, C, C)
    grad_conv2 = totals[:576, C:].reshape(9, C, C)
    return (field_out, grad_fine, grad_conv1, grad_conv2, totals[576, :C])


def solution(mesh):
    fine_mesh = Mesh(mesh.devices.reshape(2, 8, 2, 4, 2), BAND + VAR)
    in_specs = (
        P(VAR, BAND, None, None),
        P(VAR, None, None),
        P(VAR, None),
        P(),
        P(None, VAR),
        P(None, VAR),
        P(None, VAR),
        P(VAR, None),
        P(),
        P(),
        P(),
        P(),
        P(BAND, None, VAR),
    )
    out_specs = (P(BAND, None, VAR), P(BAND, None, VAR), P(), P(), P())
    return jax.shard_map(
        device_step, mesh=fine_mesh, in_specs=in_specs, out_specs=out_specs, check_vma=False
    )
```

```python
import math

import jax
import jax.numpy as jnp
import numpy as np
from jax import lax
from jax.experimental import pallas as pl
from jax.experimental.pallas import tpu as pltpu
from jax.sharding import Mesh, PartitionSpec as P


D = 2048
HD = 128
C = 64
BAND = ("xh", "z", "core")
VAR = ("y", "xl")
PLANE = ("xh", "core", "y", "xl")
BF = jnp.bfloat16
F32 = jnp.float32
VMEM_SPEC = pl.BlockSpec(memory_space=pltpu.VMEM)
SMEM_SPEC = pl.BlockSpec(memory_space=pltpu.SMEM)
SCORE_SCALE = math.log2(math.e) / math.sqrt(HD)


def dot_nn(a, b):
    return lax.dot_general(a, b, (((1,), (0,)), ((), ())), preferred_element_type=F32)


def dot_nt(a, b):
    return lax.dot_general(a, b, (((1,), (1,)), ((), ())), preferred_element_type=F32)


def dot_tn(a, b):
    return lax.dot_general(a, b, (((0,), (0,)), ((), ())), preferred_element_type=F32)


def near(x):
    return pltpu.with_memory_space_constraint(x, pltpu.VMEM)


def mix_body(patches, weights, offsets, out):
    offset = offsets[0:1, :] + offsets[1:2, :]
    out[...] = (dot_tn(patches[...], weights[...]) + offset).astype(BF)


def mix(patches, weights, offsets):
    args = [pltpu.with_memory_space_constraint(x, pltpu.HBM) for x in (patches, weights, offsets)]
    return pl.pallas_call(
        mix_body,
        grid=(4,),
        out_shape=jax.ShapeDtypeStruct((256, D), BF),
        in_specs=[
            pl.BlockSpec((128, 256), lambda k: (0, 0)),
            pl.BlockSpec((128, 512), lambda k: (0, k)),
            pl.BlockSpec((2, 512), lambda k: (0, k)),
        ],
        out_specs=pl.BlockSpec((256, 512), lambda k: (0, k)),
        compiler_params=pltpu.CompilerParams(vmem_limit_bytes=12 * 2**20),
        name="mix_variables",
    )(*args)


def norm_body(pieces, gain, out, slab):
    total = pieces[0].astype(F32)
    for k in range(1, 8):
        total = total + pieces[k].astype(F32)
    scale = lax.rsqrt(jnp.mean(total * total, axis=1, keepdims=True) + 1e-05)
    normed = (total * scale * gain[...]).astype(BF)
    slab[...] = normed
    for k in range(8):
        out[k] = normed


def norm_copies(pieces, gain):
    return pl.pallas_call(
        norm_body,
        out_shape=[pltpu.VMEM((8, 32, D), BF), pltpu.VMEM((32, D), BF)],
        in_specs=[VMEM_SPEC] * 2,
        out_specs=[VMEM_SPEC] * 2,
        compiler_params=pltpu.CompilerParams(vmem_limit_bytes=12 * 2**20),
        name="norm_slab",
    )(near(pieces), near(gain))


def flash_kernel(blocks, chunks, first, last):
    def body(*refs):
        q_refs = refs[:blocks]
        kv_refs = refs[blocks : blocks + chunks]
        rest = refs[blocks + chunks :]
        if not first:
            stat_in, acc_in = rest[0], rest[1]
            rest = rest[2:]
        if last:
            stat_scr, acc_scr, whole = rest[blocks], rest[blocks + 1], rest[blocks + 2]
            for k in range(chunks):
                whole[k * 128 : (k + 1) * 128, :] = kv_refs[k][...]
            kv_refs = [whole]
        for block in range(blocks):
            for part in range(2):
                inner = slice(part * 128, (part + 1) * 128)
                cols = slice(block * 256 + part * 128, block * 256 + (part + 1) * 128)
                for h in range(2):
                    head = slice(h * HD, (h + 1) * HD)
                    vals = slice(256 + h * HD, 256 + (h + 1) * HD)
                    q = q_refs[block][inner, head]
                    state = None
                    if not first:
                        state = (
                            stat_in[h : h + 1, cols],
                            stat_in[2 + h : 3 + h, cols],
                            acc_in[head, cols],
                        )
                    for kv in kv_refs:
                        s = dot_nt(kv[:, head], q) * SCORE_SCALE
                        top = jnp.max(s, axis=0, keepdims=True)
                        if state is not None:
                            top = jnp.maximum(top, state[0])
                        w = jnp.exp2(s - top)
                        total = jnp.sum(w, axis=0, keepdims=True)
                        update = dot_tn(kv[:, vals], w.astype(BF))
                        if state is not None:
                            shrink = jnp.exp2(state[0] - top)
                            total = total + state[1] * shrink
                            update = update + state[2] * shrink
                        state = (top, total, update)
                    top, total, update = state
                    if last:
                        acc_scr[head, cols] = update
                        stat_scr[h : h + 1, cols] = top
                        stat_scr[2 + h : 3 + h, cols] = total
                    else:
                        rest[1][head, cols] = update
                        rest[0][h : h + 1, cols] = top
                        rest[0][2 + h : 3 + h, cols] = total
        if last:
            rows = []
            for r in (0, 2, 1, 3):
                value = stat_scr[r : r + 1, :]
                high = value.astype(BF).astype(F32)
                mid = (value - high).astype(BF).astype(F32)
                rows += [high, mid, value - high - mid]
            rows.append(jnp.zeros((4, 256 * blocks), F32))
            tail = jnp.concatenate(rows, axis=0).astype(BF)
            for block in range(blocks):
                cols = slice(block * 256, (block + 1) * 256)
                rest[block][0:256, :] = acc_scr[:, cols].astype(BF)
                rest[block][256:272, :] = tail[:, cols]

    return body


def flash_step(queries, chunks, carry, last):
    blocks = len(queries)
    first = carry is None
    ins = list(queries) + list(chunks) + ([] if first else list(carry))
    if last:
        outs = [pltpu.VMEM((272, 256), BF)] * blocks
    else:
        outs = [
            pltpu.VMEM((8, 256 * blocks), F32),
            pltpu.VMEM((256, 256 * blocks), F32),
        ]
    return pl.pallas_call(
        flash_kernel(blocks, len(chunks), first, last),
        out_shape=outs,
        in_specs=[VMEM_SPEC] * len(ins),
        out_specs=[VMEM_SPEC] * len(outs),
        scratch_shapes=[
            pltpu.VMEM((8, 256 * blocks), F32),
            pltpu.VMEM((256, 256 * blocks), F32),
            pltpu.VMEM((256, 512), BF),
        ]
        if last
        else [],
        compiler_params=pltpu.CompilerParams(vmem_limit_bytes=12 * 2**20),
        name="flash_last" if last else "flash_step",
    )(*[near(x) for x in ins])


def merge_body(place, base, b0, b1, b2, b3, mat, out):
    parts = (b0, b1, b2, b3)
    tails = [b[256:272, :].astype(F32) for b in parts]
    context = []
    for h in range(2):
        head = slice(h * HD, (h + 1) * HD)

        def whole(tail, row):
            return tail[row : row + 1] + tail[row + 1 : row + 2] + tail[row + 2 : row + 3]

        tops = [whole(tail, 6 * h) for tail in tails]
        top = jnp.maximum(jnp.maximum(tops[0], tops[1]), jnp.maximum(tops[2], tops[3]))
        ws = [jnp.exp2(v - top) for v in tops]
        total = sum(whole(tail, 6 * h + 3) * w for tail, w in zip(tails, ws))
        share = 1.0 / total
        mixed = sum(b[head, :].astype(F32) * (w * share) for b, w in zip(parts, ws))
        context.append(mixed.astype(BF))
    up = dot_tn(jnp.concatenate(context, axis=0), mat[...])
    own = place[0]
    for j in range(8):
        lower = jnp.where(own == j - 1, base[31:32, :], 0.0)
        upper = jnp.where(own == j + 1, base[0:1, :], 0.0)
        for half in range(2):
            rows = []
            for k in range(4):
                lanes = slice((half * 4 + k) * 128, (half * 4 + k + 1) * 128)
                out[j, half, k * 32 : (k + 1) * 32, :] = up[32 * j : 32 * j + 32, lanes].astype(BF)
                token = 32 * j + 32 if k % 2 == 0 else 32 * j - 1
                edge = upper if k % 2 == 0 else lower
                if 0 <= token < 256:
                    rows.append(up[token : token + 1, lanes] + edge[:, lanes])
                else:
                    rows.append(jnp.zeros((1, 128), F32))
            rows.append(jnp.zeros((12, 128), F32))
            out[j, half, 128:144, :] = jnp.concatenate(rows, axis=0).astype(BF)


def merge(place, base, parts, mat):
    return pl.pallas_call(
        merge_body,
        out_shape=pltpu.VMEM((8, 2, 144, 128), BF),
        in_specs=[SMEM_SPEC] + [VMEM_SPEC] * 6,
        out_specs=VMEM_SPEC,
        compiler_params=pltpu.CompilerParams(vmem_limit_bytes=12 * 2**20),
        name="merge_heads",
    )(place, near(base), *[near(x) for x in parts], near(mat))


def spread_matrix():
    spread = np.zeros((144, 2, 2, 256), np.float32)
    for a in range(2):
        for bh in range(2):
            k = 2 * a + bh
            for bl in range(2):
                for token in range(32):
                    spread[k * 32 + token, a, bl, 4 * token + 2 * bh + bl] = 1
                spread[128 + k, a, bl, (128 + bl) if bh == 0 else (254 + bl)] = 1
    return spread.reshape(144, 1024)


def edge_matrix():
    edges = np.zeros((2, 2, 8, 8, 128), np.float32)
    for q in range(2):
        for r in range(8):
            edges[0, q, r, r, q] = 1
            edges[1, q, r, r, 126 + q] = 1
    return edges.reshape(32, 1024)


def gelu_pair(x):
    root = math.sqrt(2.0 / math.pi)
    t = jnp.tanh(root * (x + 0.044715 * (x * x * x)))
    half = 0.5 * (1.0 + t)
    slope = half + 0.5 * x * (1.0 - t * t) * (root * (1.0 + 3 * 0.044715 * (x * x)))
    return x * half, slope


def shifted(row):
    return jnp.concatenate(
        [pltpu.roll(row, 1, 1), row, pltpu.roll(row, row.shape[1] - 1, 1)], axis=0
    )


def fine_body(factor):
    def body(flags, own, near_up, far_up, spread, edges, grad, rim, mats, bias, field, grad_fine, terms):
        spread_all = spread[...]
        ups = []
        second_core = flags[4] > 0
        close, distant = near_up[...].astype(F32), far_up[...].astype(F32)
        prev = jnp.where(second_core, close, distant).astype(BF)
        nxt = jnp.where(second_core, distant, close).astype(BF)
        for block in (prev, own[0], own[1], nxt):
            wide = dot_tn(block, spread_all)
            for a in range(2):
                ups.append(
                    wide[0:64, 512 * a : 512 * a + 256] + wide[64:128, 512 * a + 256 : 512 * a + 512]
                )
        rims = dot_tn(rim[...], edges[...])
        grads = [
            jnp.concatenate([grad[r].astype(F32), rims[:, r * 128 : (r + 1) * 128]], axis=1)
            for r in range(8)
        ]
        up_taps = [shifted(u).astype(BF) for u in ups]
        grad_taps = [shifted(g).astype(BF) for g in grads]
        pre_all = dot_nn(mats[0], jnp.concatenate(up_taps, axis=1))
        act_all = dot_nn(mats[1], jnp.concatenate(grad_taps, axis=1))

        def gather(products, i, width):
            return (
                products[0:64, i * width : (i + 1) * width]
                + products[64:128, (i + 1) * width : (i + 2) * width]
                + products[128:192, (i + 2) * width : (i + 3) * width]
            )

        lane = lax.broadcasted_iota(jnp.int32, (64, 256), 1)
        cols_ok = (lane < 128) | ((lane == 128) & (flags[3] > 0)) | ((lane == 255) & (flags[2] > 0))
        offset = bias[...]
        act_taps = []
        pre_taps = []
        d_rows = []
        for i in range(6):
            pre = gather(pre_all, i, 256) + offset
            value, slope = gelu_pair(pre)
            ok = cols_ok
            if i == 0:
                ok = ok & (flags[0] > 0)
            if i == 5:
                ok = ok & (flags[1] > 0)
            value = jnp.where(ok, value, 0.0)
            d_pre = jnp.where(ok, gather(act_all, i, 256) * slope, 0.0)
            act_taps.append(shifted(value)[:, 0:128].astype(BF))
            pre_taps.append(shifted(d_pre)[:, 0:128].astype(BF))
            if 1 <= i <= 4:
                d_rows.append(d_pre[:, 0:128].astype(BF))
        act_wide = jnp.concatenate(act_taps, axis=1)
        out_all = dot_nn(mats[2], act_wide)
        fine_all = dot_nn(mats[3], jnp.concatenate(pre_taps, axis=1))
        for j in range(4):
            field[j] = (
                gather(out_all, j, 128) + ups[j + 2][:, 0:128]
            ).astype(BF)
            grad_fine[j] = (gather(fine_all, j, 128) + grads[j + 2][:, 0:128]).astype(BF)
        d_own = jnp.concatenate(d_rows, axis=1)
        g_own = jnp.concatenate([grad[r] for r in range(2, 6)], axis=1)
        for p in range(3):
            up_cut = jnp.concatenate([up_taps[r][:, 0:128] for r in range(p + 1, p + 5)], axis=1)
            first = dot_nt(up_cut, d_own)
            second = dot_nt(act_wide[:, p * 128 : p * 128 + 512], g_own)
            terms[p * 192 : (p + 1) * 192, :] = (
                jnp.concatenate([first, second], axis=1) * factor
            ).astype(BF)
        ones = jnp.ones((16, 512), BF)
        third = dot_nt(ones, d_own) * factor
        terms[576:592, :] = jnp.concatenate([third, jnp.zeros((16, 64), F32)], axis=1).astype(BF)
        terms[592:768, :] = jnp.zeros((176, 128), BF)

    return body


def fine_stage(flags, own, near_up, far_up, spread, edges, grad, rim, mats, bias, factor):
    return pl.pallas_call(
        fine_body(factor),
        out_shape=[
            jax.ShapeDtypeStruct((4, 64, 128), BF),
            jax.ShapeDtypeStruct((4, 64, 128), BF),
            pltpu.VMEM((768, 128), BF),
        ],
        in_specs=[SMEM_SPEC] + [VMEM_SPEC] * 9,
        out_specs=[VMEM_SPEC] * 3,
        compiler_params=pltpu.CompilerParams(vmem_limit_bytes=20 * 2**20),
        name="fine_stage",
    )(flags, *[near(x) for x in (own, near_up, far_up, spread, edges, grad, rim, mats, bias)])


def copies(piece, axis, count):
    return lax.all_to_all(jnp.broadcast_to(piece[None], (count,) + piece.shape), axis, 0, 0)


def flip(count, bit):
    return [(i, i ^ bit) for i in range(count)]


def turn(count, step):
    return [(i, (i + step) % count) for i in range(count)]


def tap_matrix(weight):
    return jnp.transpose(weight.reshape(3, 3, C, C), (0, 3, 1, 2)).reshape(3 * C, 3 * C)


def flipped(weight):
    return jnp.transpose(weight[::-1], (0, 2, 1))


def device_step(
    patches, w_embed, var_bias, agg_gain, wq, wk, wv, wo, w_up, conv1, bias1, conv2, cotangent
):
    var_at = lax.axis_index(VAR)
    band_at = lax.axis_index(BAND)
    shift_down = [(i, i + 1) for i in range(31)]
    shift_up = [(i + 1, i) for i in range(31)]
    group = ("xh", "core")

    core_at = lax.axis_index("core")
    turned = jnp.transpose(patches, (0, 1, 3, 2)).reshape(128, 256)
    partial_mix = mix(turned, w_embed.reshape(128, D), var_bias).reshape(8, 32, D)
    partial_mix, cells, wo, wk, wv = lax.optimization_barrier((partial_mix, cotangent, wo, wk, wv))
    pieces = lax.all_to_all(partial_mix, VAR, 0, 0)
    up_mat = jnp.dot(wo, w_up, preferred_element_type=F32).astype(BF)
    wkv = jnp.concatenate([wk, wv], axis=1)
    grad_rows = jnp.concatenate(
        [
            lax.ppermute(cells[2:4], BAND, shift_down),
            cells,
            lax.ppermute(cells[0:2], BAND, shift_up),
        ],
        axis=0,
    )
    pieces, up_mat, wkv, grad_rows = lax.optimization_barrier((pieces, up_mat, wkv, grad_rows))
    spread_out, slab = norm_copies(pieces, agg_gain.reshape(1, D))
    spread_out, slab, grad_rows, bias1 = lax.optimization_barrier(
        (spread_out, slab, grad_rows, bias1)
    )
    normed = lax.all_to_all(spread_out, VAR, 0, 0).reshape(256, D)
    edge_right = jnp.transpose(grad_rows[:, :, 0:2], (2, 0, 1)).reshape(16, C)
    edge_left = jnp.transpose(grad_rows[:, :, 126:128], (2, 0, 1)).reshape(16, C)
    from_right = lax.ppermute(edge_right, VAR, [(i + 1, i) for i in range(7)])
    from_left = lax.ppermute(edge_left, VAR, [(i, i + 1) for i in range(7)])
    rim = jnp.concatenate([from_right, from_left], axis=0)
    bias = bias1.reshape(C, 1)
    flags = jnp.stack(
        [band_at > 0, band_at < 31, var_at > 0, var_at < 7, core_at > 0]
    ).astype(jnp.int32)
    normed, rim, bias, flags = lax.optimization_barrier((normed, rim, bias, flags))

    keyvals = jnp.dot(normed, wkv, preferred_element_type=F32).astype(BF)
    ahead = lax.ppermute(keyvals, "z", turn(8, 1))
    behind = lax.ppermute(keyvals, "z", turn(8, -1))
    queries = jnp.dot(normed, wq, preferred_element_type=F32).astype(BF)
    all_queries = [queries] + [lax.ppermute(queries, group, flip(4, k)) for k in (2, 3, 1)]
    fresh = [keyvals, ahead, behind]
    ahead = lax.ppermute(ahead, "z", turn(8, 1))
    behind = lax.ppermute(behind, "z", turn(8, -1))
    carry = flash_step(all_queries, fresh, None, False)
    ahead, behind, carry = lax.optimization_barrier((ahead, behind, carry))
    for step in (2, 3):
        fresh = [ahead, behind]
        if step == 3:
            ahead, behind = ahead[:128], behind[128:]
        ahead = lax.ppermute(ahead, "z", turn(8, 1))
        behind = lax.ppermute(behind, "z", turn(8, -1))
        carry = flash_step(all_queries, fresh, carry, False)
        ahead, behind, carry = lax.optimization_barrier((ahead, behind, carry))
    fresh = [ahead, behind]

    blocks = list(flash_step(all_queries, fresh, carry, True))
    blocks[0], slab = lax.optimization_barrier((blocks[0], slab))
    base = jnp.dot(slab, w_up, preferred_element_type=F32)
    parts = [blocks[0]] + [lax.ppermute(b, group, flip(4, k)) for b, k in zip(blocks[1:], (2, 3, 1))]
    place = var_at.reshape(1).astype(jnp.int32)
    merged = merge(place, base, parts, up_mat)
    merged, conv1, conv2 = lax.optimization_barrier((merged, conv1, conv2))
    pieces = lax.all_to_all(merged, VAR, 0, 0)
    mats = jnp.stack(
        [tap_matrix(conv1), tap_matrix(flipped(conv2)), tap_matrix(conv2), tap_matrix(flipped(conv1))]
    )
    pieces, mats = lax.optimization_barrier((pieces, mats))
    base_main = jnp.transpose(base.reshape(32, 2, 4, 128), (1, 2, 0, 3)).reshape(2, 128, 128)
    base_all = jnp.pad(base_main, ((0, 0), (0, 16), (0, 0)))
    up = (jnp.sum(pieces.astype(F32), axis=0) + base_all).astype(BF)
    near_up = lax.ppermute(lax.dynamic_index_in_dim(up, 1 - core_at, 0, False), "core", flip(2, 1))
    pairs = [(i, i + 1) for i in range(1, 31, 2)] + [(i + 1, i) for i in range(1, 31, 2)]
    far_up = lax.ppermute(lax.dynamic_index_in_dim(up, core_at, 0, False), BAND, pairs)
    factor = 1.0 / math.sqrt(128 * 1024)
    spread = jnp.asarray(spread_matrix(), BF)
    field_out, grad_fine, terms = fine_stage(
        flags, up, near_up, far_up, spread, jnp.asarray(edge_matrix(), BF), grad_rows, rim, mats, bias, factor
    )
    shares = lax.all_to_all(terms.reshape(32, 24, 128), PLANE, 0, 0)
    share = jnp.sum(shares.astype(F32), axis=0).astype(BF)
    share = jnp.sum(copies(share, "z", 8).astype(F32), axis=0).astype(BF)
    totals = copies(share, PLANE, 32).reshape(768, 128).astype(F32)
    grad_conv1 = totals[:576, :C].reshape(9, C, C)
    grad_conv2 = totals[:576, C:].reshape(9, C, C)
    return (field_out, grad_fine, grad_conv1, grad_conv2, totals[576, :C])


def solution(mesh):
    fine_mesh = Mesh(mesh.devices.reshape(2, 8, 2, 4, 2), BAND + VAR)
    in_specs = (
        P(VAR, BAND, None, None),
        P(VAR, None, None),
        P(VAR, None),
        P(),
        P(None, VAR),
        P(None, VAR),
        P(None, VAR),
        P(VAR, None),
        P(),
        P(),
        P(),
        P(),
        P(BAND, None, VAR),
    )
    out_specs = (P(BAND, None, VAR), P(BAND, None, VAR), P(), P(), P())
    return jax.shard_map(
        device_step, mesh=fine_mesh, in_specs=in_specs, out_specs=out_specs, check_vma=False
    )
```

```python
import math

import jax
import jax.numpy as jnp
import numpy as np
from jax import lax
from jax.experimental import pallas as pl
from jax.experimental.pallas import tpu as pltpu
from jax.sharding import Mesh, PartitionSpec as P


D = 2048
HD = 128
C = 64
BAND = ("xh", "z", "core")
VAR = ("y", "xl")
PLANE = ("xh", "core", "y", "xl")
BF = jnp.bfloat16
F32 = jnp.float32
VMEM_SPEC = pl.BlockSpec(memory_space=pltpu.VMEM)
SMEM_SPEC = pl.BlockSpec(memory_space=pltpu.SMEM)
SCORE_SCALE = math.log2(math.e) / math.sqrt(HD)


def dot_nn(a, b):
    return lax.dot_general(a, b, (((1,), (0,)), ((), ())), preferred_element_type=F32)


def dot_nt(a, b):
    return lax.dot_general(a, b, (((1,), (1,)), ((), ())), preferred_element_type=F32)


def dot_tn(a, b):
    return lax.dot_general(a, b, (((0,), (0,)), ((), ())), preferred_element_type=F32)


def near(x):
    return pltpu.with_memory_space_constraint(x, pltpu.VMEM)


def mix_body(patches, weights, offsets, out):
    offset = offsets[0:1, :] + offsets[1:2, :]
    out[...] = (dot_tn(patches[...], weights[...]) + offset).astype(BF)


def mix(patches, weights, offsets):
    args = [pltpu.with_memory_space_constraint(x, pltpu.HBM) for x in (patches, weights, offsets)]
    return pl.pallas_call(
        mix_body,
        grid=(4,),
        out_shape=jax.ShapeDtypeStruct((256, D), BF),
        in_specs=[
            pl.BlockSpec((128, 256), lambda k: (0, 0)),
            pl.BlockSpec((128, 512), lambda k: (0, k)),
            pl.BlockSpec((2, 512), lambda k: (0, k)),
        ],
        out_specs=pl.BlockSpec((256, 512), lambda k: (0, k)),
        compiler_params=pltpu.CompilerParams(vmem_limit_bytes=12 * 2**20),
        name="mix_variables",
    )(*args)


def project(rows, weights):
    count = 2 * len(weights)

    def body(*refs):
        x, out = refs[0], refs[-1]
        step = pl.program_id(0)
        for k, w in enumerate(refs[1:-1]):

            @pl.when((step >= 2 * k) & (step < 2 * k + 2))
            def _():
                out[...] = dot_nn(x[...], w[...]).astype(BF)

    def columns(k):
        return lambda step: (0, jnp.clip(step - 2 * k, 0, 1))

    return pl.pallas_call(
        body,
        grid=(count,),
        out_shape=jax.ShapeDtypeStruct((256, 128 * count), BF),
        in_specs=[VMEM_SPEC]
        + [pl.BlockSpec((D, 128), columns(k)) for k in range(len(weights))],
        out_specs=pl.BlockSpec((256, 128), lambda step: (0, step)),
        compiler_params=pltpu.CompilerParams(vmem_limit_bytes=12 * 2**20),
        name="project_rows",
    )(near(rows), *[pltpu.with_memory_space_constraint(w, pltpu.HBM) for w in weights])


def norm_body(pieces, gain, out, slab):
    total = pieces[0].astype(F32)
    for k in range(1, 8):
        total = total + pieces[k].astype(F32)
    scale = lax.rsqrt(jnp.mean(total * total, axis=1, keepdims=True) + 1e-05)
    normed = (total * scale * gain[...]).astype(BF)
    slab[...] = normed
    for k in range(8):
        out[k] = normed


def norm_copies(pieces, gain):
    return pl.pallas_call(
        norm_body,
        out_shape=[pltpu.VMEM((8, 32, D), BF), pltpu.VMEM((32, D), BF)],
        in_specs=[VMEM_SPEC] * 2,
        out_specs=[VMEM_SPEC] * 2,
        compiler_params=pltpu.CompilerParams(vmem_limit_bytes=12 * 2**20),
        name="norm_slab",
    )(near(pieces), near(gain))


def flash_kernel(blocks, chunks, first, last):
    def body(*refs):
        q_refs = refs[:blocks]
        kv_refs = refs[blocks : blocks + chunks]
        rest = refs[blocks + chunks :]
        if not first:
            stat_in, acc_in = rest[0], rest[1]
            rest = rest[2:]
        if last:
            stat_scr, acc_scr, whole = rest[blocks], rest[blocks + 1], rest[blocks + 2]
            for k in range(chunks):
                whole[k * 128 : (k + 1) * 128, :] = kv_refs[k][...]
            kv_refs = [whole]
        for block in range(blocks):
            for part in range(2):
                inner = slice(part * 128, (part + 1) * 128)
                cols = slice(block * 256 + part * 128, block * 256 + (part + 1) * 128)
                for h in range(2):
                    head = slice(h * HD, (h + 1) * HD)
                    vals = slice(256 + h * HD, 256 + (h + 1) * HD)
                    q = q_refs[block][inner, head]
                    state = None
                    if not first:
                        state = (
                            stat_in[h : h + 1, cols],
                            stat_in[2 + h : 3 + h, cols],
                            acc_in[head, cols],
                        )
                    for kv in kv_refs:
                        s = dot_nt(kv[:, head], q) * SCORE_SCALE
                        top = jnp.max(s, axis=0, keepdims=True)
                        if state is not None:
                            top = jnp.maximum(top, state[0])
                        w = jnp.exp2(s - top)
                        total = jnp.sum(w, axis=0, keepdims=True)
                        update = dot_tn(kv[:, vals], w.astype(BF))
                        if state is not None:
                            shrink = jnp.exp2(state[0] - top)
                            total = total + state[1] * shrink
                            update = update + state[2] * shrink
                        state = (top, total, update)
                    top, total, update = state
                    if last:
                        acc_scr[head, cols] = update
                        stat_scr[h : h + 1, cols] = top
                        stat_scr[2 + h : 3 + h, cols] = total
                    else:
                        rest[1][head, cols] = update
                        rest[0][h : h + 1, cols] = top
                        rest[0][2 + h : 3 + h, cols] = total
        if last:
            rows = []
            for r in (0, 2, 1, 3):
                value = stat_scr[r : r + 1, :]
                high = value.astype(BF).astype(F32)
                mid = (value - high).astype(BF).astype(F32)
                rows += [high, mid, value - high - mid]
            rows.append(jnp.zeros((4, 256 * blocks), F32))
            tail = jnp.concatenate(rows, axis=0).astype(BF)
            for block in range(blocks):
                cols = slice(block * 256, (block + 1) * 256)
                rest[block][0:256, :] = acc_scr[:, cols].astype(BF)
                rest[block][256:272, :] = tail[:, cols]

    return body


def flash_step(queries, chunks, carry, last):
    blocks = len(queries)
    first = carry is None
    ins = list(queries) + list(chunks) + ([] if first else list(carry))
    if last:
        outs = [pltpu.VMEM((272, 256), BF)] * blocks
    else:
        outs = [
            pltpu.VMEM((8, 256 * blocks), F32),
            pltpu.VMEM((256, 256 * blocks), F32),
        ]
    return pl.pallas_call(
        flash_kernel(blocks, len(chunks), first, last),
        out_shape=outs,
        in_specs=[VMEM_SPEC] * len(ins),
        out_specs=[VMEM_SPEC] * len(outs),
        scratch_shapes=[
            pltpu.VMEM((8, 256 * blocks), F32),
            pltpu.VMEM((256, 256 * blocks), F32),
            pltpu.VMEM((256, 512), BF),
        ]
        if last
        else [],
        compiler_params=pltpu.CompilerParams(vmem_limit_bytes=12 * 2**20),
        name="flash_last" if last else "flash_step",
    )(*[near(x) for x in ins])


def merge_body(place, base, edges, b0, b1, b2, b3, mat, out):
    parts = (b0, b1, b2, b3)
    tails = [b[256:272, :].astype(F32) for b in parts]
    context = []
    for h in range(2):
        head = slice(h * HD, (h + 1) * HD)

        def whole(tail, row):
            return tail[row : row + 1] + tail[row + 1 : row + 2] + tail[row + 2 : row + 3]

        tops = [whole(tail, 6 * h) for tail in tails]
        top = jnp.maximum(jnp.maximum(tops[0], tops[1]), jnp.maximum(tops[2], tops[3]))
        ws = [jnp.exp2(v - top) for v in tops]
        total = sum(whole(tail, 6 * h + 3) * w for tail, w in zip(tails, ws))
        share = 1.0 / total
        mixed = sum(b[head, :].astype(F32) * (w * share) for b, w in zip(parts, ws))
        context.append(mixed.astype(BF))
    up = dot_tn(jnp.concatenate(context, axis=0), mat[...])
    own = place[0]
    sides = edges[...].astype(F32)
    for j in range(8):
        lower = jnp.where(own == j - 1, base[31:32, :], 0.0)
        upper = jnp.where(own == j + 1, base[0:1, :], 0.0)
        for half in range(2):
            rows = []
            for k in range(4):
                lanes = slice((half * 4 + k) * 128, (half * 4 + k + 1) * 128)
                out[j, half, k * 32 : (k + 1) * 32, :] = up[32 * j : 32 * j + 32, lanes].astype(BF)
                token = 32 * j + 32 if k % 2 == 0 else 32 * j - 1
                edge = upper if k % 2 == 0 else lower
                if 0 <= token < 256:
                    rows.append(up[token : token + 1, lanes] + edge[:, lanes])
                else:
                    rows.append(jnp.zeros((1, 128), F32))
            source = j - 1 if half == 0 else j + 1
            rows.append(jnp.where(own == source, sides[4 * half : 4 * half + 4], 0.0))
            rows.append(jnp.zeros((8, 128), F32))
            out[j, half, 128:144, :] = jnp.concatenate(rows, axis=0).astype(BF)


def merge(place, base, edges, parts, mat):
    return pl.pallas_call(
        merge_body,
        out_shape=pltpu.VMEM((8, 2, 144, 128), BF),
        in_specs=[SMEM_SPEC] + [VMEM_SPEC] * 7,
        out_specs=VMEM_SPEC,
        compiler_params=pltpu.CompilerParams(vmem_limit_bytes=12 * 2**20),
        name="merge_heads",
    )(place, near(base), near(edges), *[near(x) for x in parts], near(mat))


def collect_body(flags, pieces, base, grad, own, near_out, far_out):
    for half in range(2):
        total = pieces[0, half].astype(F32)
        for k in range(1, 8):
            total = total + pieces[k, half].astype(F32)
        own[half, 0:128, :] = (total[0:128] + base[half]).astype(BF)
        own[half, 128:144, :] = total[128:144].astype(BF)
    core = flags[4]
    for side, out in ((1 - core, near_out), (core, far_out)):
        out[0:144, :] = own[side]
        out[144:160, :] = own[1 - side, 128:144, :]
        for k in range(2):
            out[160 + 64 * k : 224 + 64 * k, :] = grad[2 * side + k]


def collect(flags, pieces, base, grad):
    return pl.pallas_call(
        collect_body,
        out_shape=[
            pltpu.VMEM((2, 144, 128), BF),
            pltpu.VMEM((288, 128), BF),
            pltpu.VMEM((288, 128), BF),
        ],
        in_specs=[SMEM_SPEC] + [VMEM_SPEC] * 3,
        out_specs=[VMEM_SPEC] * 3,
        compiler_params=pltpu.CompilerParams(vmem_limit_bytes=12 * 2**20),
        name="collect_slab",
    )(flags, near(pieces), near(base), near(grad))


def spread_matrix():
    spread = np.zeros((144, 2, 2, 256), np.float32)
    for a in range(2):
        for bh in range(2):
            k = 2 * a + bh
            for bl in range(2):
                for token in range(32):
                    spread[k * 32 + token, a, bl, 4 * token + 2 * bh + bl] = 1
                spread[128 + k, a, bl, (128 + bl) if bh == 0 else (254 + bl)] = 1
    return spread.reshape(144, 1024)


def edge_matrix():
    edges = np.zeros((2, 16, 2, 4, 128), np.float32)
    for q in range(2):
        for r in range(4):
            k, m = divmod(4 * q + r, 2)
            edges[0, 4 + k, m, r, 126 + q] = 1
            edges[1, 4 + k, m, r, q] = 1
    return edges.reshape(32, 1024)


def gelu_pair(x):
    root = math.sqrt(2.0 / math.pi)
    t = jnp.tanh(root * (x + 0.044715 * (x * x * x)))
    half = 0.5 * (1.0 + t)
    slope = half + 0.5 * x * (1.0 - t * t) * (root * (1.0 + 3 * 0.044715 * (x * x)))
    return x * half, slope


def shifted(row):
    return jnp.concatenate(
        [pltpu.roll(row, 1, 1), row, pltpu.roll(row, row.shape[1] - 1, 1)], axis=0
    )


def fine_body(factor):
    def body(flags, own, near_up, far_up, spread, edges, grad, mats, bias, field, grad_fine, terms):
        spread_all = spread[...]
        ups = []
        second_core = flags[4] > 0
        close, distant = near_up[...].astype(F32), far_up[...].astype(F32)
        prev = jnp.where(second_core, close, distant).astype(BF)
        nxt = jnp.where(second_core, distant, close).astype(BF)
        for block in (prev[0:144], own[0], own[1], nxt[0:144]):
            wide = dot_tn(block, spread_all)
            for a in range(2):
                ups.append(
                    wide[0:64, 512 * a : 512 * a + 256] + wide[64:128, 512 * a + 256 : 512 * a + 512]
                )
        edge_all = edges[...]
        rows_of = [
            [prev[160:224], prev[224:288]],
            [grad[r] for r in range(4)],
            [nxt[160:224], nxt[224:288]],
        ]
        lefts = [prev[144:160], own[0, 128:144, :], nxt[128:144]]
        rights = [prev[128:144], own[1, 128:144, :], nxt[144:160]]
        grads = []
        for k in range(3):
            wide = dot_tn(jnp.concatenate([lefts[k], rights[k]], axis=0), edge_all)
            for r, row in enumerate(rows_of[k]):
                at = (r + 2 if k == 0 else r) * 128
                rim = wide[0:64, at : at + 128] + wide[64:128, 512 + at : 640 + at]
                grads.append(jnp.concatenate([row.astype(F32), rim], axis=1))
        up_taps = [shifted(u).astype(BF) for u in ups]
        grad_taps = [shifted(g).astype(BF) for g in grads]
        pre_all = dot_nn(mats[0], jnp.concatenate(up_taps, axis=1))
        act_all = dot_nn(mats[1], jnp.concatenate(grad_taps, axis=1))

        def gather(products, i, width):
            return (
                products[0:64, i * width : (i + 1) * width]
                + products[64:128, (i + 1) * width : (i + 2) * width]
                + products[128:192, (i + 2) * width : (i + 3) * width]
            )

        lane = lax.broadcasted_iota(jnp.int32, (64, 256), 1)
        cols_ok = (lane < 128) | ((lane == 128) & (flags[3] > 0)) | ((lane == 255) & (flags[2] > 0))
        offset = bias[...]
        act_taps = []
        pre_taps = []
        d_rows = []
        for i in range(6):
            pre = gather(pre_all, i, 256) + offset
            value, slope = gelu_pair(pre)
            ok = cols_ok
            if i == 0:
                ok = ok & (flags[0] > 0)
            if i == 5:
                ok = ok & (flags[1] > 0)
            value = jnp.where(ok, value, 0.0)
            d_pre = jnp.where(ok, gather(act_all, i, 256) * slope, 0.0)
            act_taps.append(shifted(value)[:, 0:128].astype(BF))
            pre_taps.append(shifted(d_pre)[:, 0:128].astype(BF))
            if 1 <= i <= 4:
                d_rows.append(d_pre[:, 0:128].astype(BF))
        act_wide = jnp.concatenate(act_taps, axis=1)
        out_all = dot_nn(mats[2], act_wide)
        fine_all = dot_nn(mats[3], jnp.concatenate(pre_taps, axis=1))
        for j in range(4):
            field[j] = (
                gather(out_all, j, 128) + ups[j + 2][:, 0:128]
            ).astype(BF)
            grad_fine[j] = (gather(fine_all, j, 128) + grads[j + 2][:, 0:128]).astype(BF)
        d_own = jnp.concatenate(d_rows, axis=1)
        g_own = jnp.concatenate([grad[r] for r in range(4)], axis=1)
        for p in range(3):
            up_cut = jnp.concatenate([up_taps[r][:, 0:128] for r in range(p + 1, p + 5)], axis=1)
            first = dot_nt(up_cut, d_own)
            second = dot_nt(act_wide[:, p * 128 : p * 128 + 512], g_own)
            terms[p * 192 : (p + 1) * 192, :] = (
                jnp.concatenate([first, second], axis=1) * factor
            ).astype(BF)
        ones = jnp.ones((16, 512), BF)
        third = dot_nt(ones, d_own) * factor
        terms[576:592, :] = jnp.concatenate([third, jnp.zeros((16, 64), F32)], axis=1).astype(BF)
        terms[592:768, :] = jnp.zeros((176, 128), BF)

    return body


def fine_stage(flags, own, near_up, far_up, spread, edges, grad, mats, bias, factor):
    return pl.pallas_call(
        fine_body(factor),
        out_shape=[
            jax.ShapeDtypeStruct((4, 64, 128), BF),
            jax.ShapeDtypeStruct((4, 64, 128), BF),
            pltpu.VMEM((768, 128), BF),
        ],
        in_specs=[SMEM_SPEC] + [VMEM_SPEC] * 8,
        out_specs=[VMEM_SPEC] * 3,
        compiler_params=pltpu.CompilerParams(vmem_limit_bytes=20 * 2**20),
        name="fine_stage",
    )(flags, *[near(x) for x in (own, near_up, far_up, spread, edges, grad, mats, bias)])


def copies(piece, axis, count):
    return lax.all_to_all(jnp.broadcast_to(piece[None], (count,) + piece.shape), axis, 0, 0)


def flip(count, bit):
    return [(i, i ^ bit) for i in range(count)]


def turn(count, step):
    return [(i, (i + step) % count) for i in range(count)]


def tap_matrix(weight):
    return jnp.transpose(weight.reshape(3, 3, C, C), (0, 3, 1, 2)).reshape(3 * C, 3 * C)


def flipped(weight):
    return jnp.transpose(weight[::-1], (0, 2, 1))


def device_step(
    patches, w_embed, var_bias, agg_gain, wq, wk, wv, wo, w_up, conv1, bias1, conv2, cotangent
):
    var_at = lax.axis_index(VAR)
    band_at = lax.axis_index(BAND)
    group = ("xh", "core")

    core_at = lax.axis_index("core")
    turned = jnp.transpose(patches, (0, 1, 3, 2)).reshape(128, 256)
    partial_mix = mix(turned, w_embed.reshape(128, D), var_bias).reshape(8, 32, D)
    pieces = lax.all_to_all(partial_mix, VAR, 0, 0)
    spread_out, slab = norm_copies(pieces, agg_gain.reshape(1, D))
    normed = lax.all_to_all(spread_out, VAR, 0, 0).reshape(256, D)

    keyvals = project(normed, [wk, wv])
    ahead = lax.ppermute(keyvals, "z", turn(8, 1))
    behind = lax.ppermute(keyvals, "z", turn(8, -1))
    queries = project(normed, [wq])
    all_queries = [queries] + [lax.ppermute(queries, group, flip(4, k)) for k in (2, 3, 1)]
    fresh = [keyvals, ahead, behind]
    ahead = lax.ppermute(ahead, "z", turn(8, 1))
    behind = lax.ppermute(behind, "z", turn(8, -1))
    carry = flash_step(all_queries, fresh, None, False)
    ahead, behind, carry = lax.optimization_barrier((ahead, behind, carry))
    for step in (2, 3):
        fresh = [ahead, behind]
        if step == 3:
            ahead, behind = ahead[:128], behind[128:]
        ahead = lax.ppermute(ahead, "z", turn(8, 1))
        behind = lax.ppermute(behind, "z", turn(8, -1))
        carry = flash_step(all_queries, fresh, carry, False)
        if step == 2:
            carry, wo = lax.optimization_barrier((carry, wo))
            up_mat = jnp.dot(wo, w_up, preferred_element_type=F32).astype(BF)
            ahead, behind, carry, up_mat = lax.optimization_barrier((ahead, behind, carry, up_mat))
        else:
            ahead, behind, carry = lax.optimization_barrier((ahead, behind, carry))
    fresh = [ahead, behind]

    blocks = list(flash_step(all_queries, fresh, carry, True))
    blocks[0], slab, cells, bias1 = lax.optimization_barrier((blocks[0], slab, cotangent, bias1))
    base = jnp.dot(slab, w_up, preferred_element_type=F32)
    edges = jnp.concatenate(
        [
            jnp.transpose(cells[:, :, at : at + 2], (2, 0, 1)).reshape(4, 128) for at in (126, 0)
        ],
        axis=0,
    )
    bias = bias1.reshape(C, 1)
    flags = jnp.stack(
        [band_at > 0, band_at < 31, var_at > 0, var_at < 7, core_at > 0]
    ).astype(jnp.int32)
    parts = [blocks[0]] + [lax.ppermute(b, group, flip(4, k)) for b, k in zip(blocks[1:], (2, 3, 1))]
    place = var_at.reshape(1).astype(jnp.int32)
    merged = merge(place, base, edges, parts, up_mat)
    merged, conv1, conv2 = lax.optimization_barrier((merged, conv1, conv2))
    pieces = lax.all_to_all(merged, VAR, 0, 0)
    mats = jnp.stack(
        [tap_matrix(conv1), tap_matrix(flipped(conv2)), tap_matrix(conv2), tap_matrix(flipped(conv1))]
    )
    pieces, mats = lax.optimization_barrier((pieces, mats))
    base_main = jnp.transpose(base.reshape(32, 2, 4, 128), (1, 2, 0, 3)).reshape(2, 128, 128)
    up, near_rows, far_rows = collect(flags, pieces, base_main, cells)
    near_up = lax.ppermute(near_rows, "core", flip(2, 1))
    pairs = [(i, i + 1) for i in range(1, 31, 2)] + [(i + 1, i) for i in range(1, 31, 2)]
    far_up = lax.ppermute(far_rows, BAND, pairs)
    factor = 1.0 / math.sqrt(128 * 1024)
    spread = jnp.asarray(spread_matrix(), BF)
    field_out, grad_fine, terms = fine_stage(
        flags, up, near_up, far_up, spread, jnp.asarray(edge_matrix(), BF), cells, mats, bias, factor
    )
    shares = lax.all_to_all(terms.reshape(32, 24, 128), PLANE, 0, 0)
    share = jnp.sum(shares.astype(F32), axis=0).astype(BF)
    share = jnp.sum(copies(share, "z", 8).astype(F32), axis=0).astype(BF)
    totals = copies(share, PLANE, 32).reshape(768, 128).astype(F32)
    grad_conv1 = totals[:576, :C].reshape(9, C, C)
    grad_conv2 = totals[:576, C:].reshape(9, C, C)
    return (field_out, grad_fine, grad_conv1, grad_conv2, totals[576, :C])


def solution(mesh):
    fine_mesh = Mesh(mesh.devices.reshape(2, 8, 2, 4, 2), BAND + VAR)
    in_specs = (
        P(VAR, BAND, None, None),
        P(VAR, None, None),
        P(VAR, None),
        P(),
        P(None, VAR),
        P(None, VAR),
        P(None, VAR),
        P(VAR, None),
        P(),
        P(),
        P(),
        P(),
        P(BAND, None, VAR),
    )
    out_specs = (P(BAND, None, VAR), P(BAND, None, VAR), P(), P(), P())
    return jax.shard_map(
        device_step, mesh=fine_mesh, in_specs=in_specs, out_specs=out_specs, check_vma=False
    )
```

```python
import math

import jax
import jax.numpy as jnp
import numpy as np
from jax import lax
from jax.experimental import pallas as pl
from jax.experimental.pallas import tpu as pltpu
from jax.sharding import Mesh, PartitionSpec as P


D = 2048
HD = 128
C = 64
BAND = ("xh", "z", "core")
VAR = ("y", "xl")
PLANE = ("xh", "core", "y", "xl")
BF = jnp.bfloat16
F32 = jnp.float32
VMEM_SPEC = pl.BlockSpec(memory_space=pltpu.VMEM)
SMEM_SPEC = pl.BlockSpec(memory_space=pltpu.SMEM)
SCORE_SCALE = math.log2(math.e) / math.sqrt(HD)


def dot_nn(a, b):
    return lax.dot_general(a, b, (((1,), (0,)), ((), ())), preferred_element_type=F32)


def dot_nt(a, b):
    return lax.dot_general(a, b, (((1,), (1,)), ((), ())), preferred_element_type=F32)


def dot_tn(a, b):
    return lax.dot_general(a, b, (((0,), (0,)), ((), ())), preferred_element_type=F32)


def near(x):
    return pltpu.with_memory_space_constraint(x, pltpu.VMEM)


def mix_body(patches, weights, offsets, out):
    offset = offsets[0:1, :] + offsets[1:2, :]
    out[...] = (dot_tn(patches[...], weights[...]) + offset).astype(BF)


def mix(patches, weights, offsets):
    args = [pltpu.with_memory_space_constraint(x, pltpu.HBM) for x in (patches, weights, offsets)]
    return pl.pallas_call(
        mix_body,
        grid=(4,),
        out_shape=jax.ShapeDtypeStruct((256, D), BF),
        in_specs=[
            pl.BlockSpec((128, 256), lambda k: (0, 0)),
            pl.BlockSpec((128, 512), lambda k: (0, k)),
            pl.BlockSpec((2, 512), lambda k: (0, k)),
        ],
        out_specs=pl.BlockSpec((256, 512), lambda k: (0, k)),
        compiler_params=pltpu.CompilerParams(vmem_limit_bytes=12 * 2**20),
        name="mix_variables",
    )(*args)


def norm_body(pieces, gain, out, slab):
    total = pieces[0].astype(F32)
    for k in range(1, 8):
        total = total + pieces[k].astype(F32)
    scale = lax.rsqrt(jnp.mean(total * total, axis=1, keepdims=True) + 1e-05)
    normed = (total * scale * gain[...]).astype(BF)
    slab[...] = normed
    for k in range(8):
        out[k] = normed


def norm_copies(pieces, gain):
    return pl.pallas_call(
        norm_body,
        out_shape=[pltpu.VMEM((8, 32, D), BF), pltpu.VMEM((32, D), BF)],
        in_specs=[VMEM_SPEC] * 2,
        out_specs=[VMEM_SPEC] * 2,
        compiler_params=pltpu.CompilerParams(vmem_limit_bytes=12 * 2**20),
        name="norm_slab",
    )(near(pieces), near(gain))


def flash_kernel(blocks, chunks, first, last):
    def body(*refs):
        q_refs = refs[:blocks]
        kv_refs = refs[blocks : blocks + chunks]
        rest = refs[blocks + chunks :]
        if not first:
            stat_in, acc_in = rest[0], rest[1]
            rest = rest[2:]
        if last:
            stat_scr, acc_scr, whole = rest[blocks], rest[blocks + 1], rest[blocks + 2]
            for k in range(chunks):
                whole[k * 128 : (k + 1) * 128, :] = kv_refs[k][...]
            kv_refs = [whole]
        for block in range(blocks):
            for part in range(2):
                inner = slice(part * 128, (part + 1) * 128)
                cols = slice(block * 256 + part * 128, block * 256 + (part + 1) * 128)
                for h in range(2):
                    head = slice(h * HD, (h + 1) * HD)
                    vals = slice(256 + h * HD, 256 + (h + 1) * HD)
                    q = q_refs[block][inner, head]
                    state = None
                    if not first:
                        state = (
                            stat_in[h : h + 1, cols],
                            stat_in[2 + h : 3 + h, cols],
                            acc_in[head, cols],
                        )
                    for kv in kv_refs:
                        s = dot_nt(kv[:, head], q) * SCORE_SCALE
                        top = jnp.max(s, axis=0, keepdims=True)
                        if state is not None:
                            top = jnp.maximum(top, state[0])
                        w = jnp.exp2(s - top)
                        total = jnp.sum(w, axis=0, keepdims=True)
                        update = dot_tn(kv[:, vals], w.astype(BF))
                        if state is not None:
                            shrink = jnp.exp2(state[0] - top)
                            total = total + state[1] * shrink
                            update = update + state[2] * shrink
                        state = (top, total, update)
                    top, total, update = state
                    if last:
                        acc_scr[head, cols] = update
                        stat_scr[h : h + 1, cols] = top
                        stat_scr[2 + h : 3 + h, cols] = total
                    else:
                        rest[1][head, cols] = update
                        rest[0][h : h + 1, cols] = top
                        rest[0][2 + h : 3 + h, cols] = total
        if last:
            rows = []
            for r in (0, 2, 1, 3):
                value = stat_scr[r : r + 1, :]
                high = value.astype(BF).astype(F32)
                mid = (value - high).astype(BF).astype(F32)
                rows += [high, mid, value - high - mid]
            rows.append(jnp.zeros((4, 256 * blocks), F32))
            tail = jnp.concatenate(rows, axis=0).astype(BF)
            for block in range(blocks):
                cols = slice(block * 256, (block + 1) * 256)
                rest[block][0:256, :] = acc_scr[:, cols].astype(BF)
                rest[block][256:272, :] = tail[:, cols]

    return body


def flash_step(queries, chunks, carry, last):
    blocks = len(queries)
    first = carry is None
    ins = list(queries) + list(chunks) + ([] if first else list(carry))
    if last:
        outs = [pltpu.VMEM((272, 256), BF)] * blocks
    else:
        outs = [
            pltpu.VMEM((8, 256 * blocks), F32),
            pltpu.VMEM((256, 256 * blocks), F32),
        ]
    return pl.pallas_call(
        flash_kernel(blocks, len(chunks), first, last),
        out_shape=outs,
        in_specs=[VMEM_SPEC] * len(ins),
        out_specs=[VMEM_SPEC] * len(outs),
        scratch_shapes=[
            pltpu.VMEM((8, 256 * blocks), F32),
            pltpu.VMEM((256, 256 * blocks), F32),
            pltpu.VMEM((256, 512), BF),
        ]
        if last
        else [],
        compiler_params=pltpu.CompilerParams(vmem_limit_bytes=12 * 2**20),
        name="flash_last" if last else "flash_step",
    )(*[near(x) for x in ins])


def merge_body(place, base, edges, b0, b1, b2, b3, mat, out):
    parts = (b0, b1, b2, b3)
    tails = [b[256:272, :].astype(F32) for b in parts]
    context = []
    for h in range(2):
        head = slice(h * HD, (h + 1) * HD)

        def whole(tail, row):
            return tail[row : row + 1] + tail[row + 1 : row + 2] + tail[row + 2 : row + 3]

        tops = [whole(tail, 6 * h) for tail in tails]
        top = jnp.maximum(jnp.maximum(tops[0], tops[1]), jnp.maximum(tops[2], tops[3]))
        ws = [jnp.exp2(v - top) for v in tops]
        total = sum(whole(tail, 6 * h + 3) * w for tail, w in zip(tails, ws))
        share = 1.0 / total
        mixed = sum(b[head, :].astype(F32) * (w * share) for b, w in zip(parts, ws))
        context.append(mixed.astype(BF))
    up = dot_tn(jnp.concatenate(context, axis=0), mat[...])
    own = place[0]
    sides = edges[...].astype(F32)
    for j in range(8):
        lower = jnp.where(own == j - 1, base[31:32, :], 0.0)
        upper = jnp.where(own == j + 1, base[0:1, :], 0.0)
        for half in range(2):
            rows = []
            for k in range(4):
                lanes = slice((half * 4 + k) * 128, (half * 4 + k + 1) * 128)
                out[j, half, k * 32 : (k + 1) * 32, :] = up[32 * j : 32 * j + 32, lanes].astype(BF)
                token = 32 * j + 32 if k % 2 == 0 else 32 * j - 1
                edge = upper if k % 2 == 0 else lower
                if 0 <= token < 256:
                    rows.append(up[token : token + 1, lanes] + edge[:, lanes])
                else:
                    rows.append(jnp.zeros((1, 128), F32))
            source = j - 1 if half == 0 else j + 1
            rows.append(jnp.where(own == source, sides[4 * half : 4 * half + 4], 0.0))
            rows.append(jnp.zeros((8, 128), F32))
            out[j, half, 128:144, :] = jnp.concatenate(rows, axis=0).astype(BF)


def merge(place, base, edges, parts, mat):
    return pl.pallas_call(
        merge_body,
        out_shape=pltpu.VMEM((8, 2, 144, 128), BF),
        in_specs=[SMEM_SPEC] + [VMEM_SPEC] * 7,
        out_specs=VMEM_SPEC,
        compiler_params=pltpu.CompilerParams(vmem_limit_bytes=12 * 2**20),
        name="merge_heads",
    )(place, near(base), near(edges), *[near(x) for x in parts], near(mat))


def collect_body(flags, pieces, base, grad, own, near_out, far_out):
    for half in range(2):
        total = pieces[0, half].astype(F32)
        for k in range(1, 8):
            total = total + pieces[k, half].astype(F32)
        own[half, 0:128, :] = (total[0:128] + base[half]).astype(BF)
        own[half, 128:144, :] = total[128:144].astype(BF)
    core = flags[4]
    for side, out in ((1 - core, near_out), (core, far_out)):
        out[0:144, :] = own[side]
        out[144:160, :] = own[1 - side, 128:144, :]
        for k in range(2):
            out[160 + 64 * k : 224 + 64 * k, :] = grad[2 * side + k]


def collect(flags, pieces, base, grad):
    return pl.pallas_call(
        collect_body,
        out_shape=[
            pltpu.VMEM((2, 144, 128), BF),
            pltpu.VMEM((288, 128), BF),
            pltpu.VMEM((288, 128), BF),
        ],
        in_specs=[SMEM_SPEC] + [VMEM_SPEC] * 3,
        out_specs=[VMEM_SPEC] * 3,
        compiler_params=pltpu.CompilerParams(vmem_limit_bytes=12 * 2**20),
        name="collect_slab",
    )(flags, near(pieces), near(base), near(grad))


def spread_matrix():
    spread = np.zeros((144, 2, 2, 256), np.float32)
    for a in range(2):
        for bh in range(2):
            k = 2 * a + bh
            for bl in range(2):
                for token in range(32):
                    spread[k * 32 + token, a, bl, 4 * token + 2 * bh + bl] = 1
                spread[128 + k, a, bl, (128 + bl) if bh == 0 else (254 + bl)] = 1
    return spread.reshape(144, 1024)


def edge_matrix():
    edges = np.zeros((2, 16, 2, 4, 128), np.float32)
    for q in range(2):
        for r in range(4):
            k, m = divmod(4 * q + r, 2)
            edges[0, 4 + k, m, r, 126 + q] = 1
            edges[1, 4 + k, m, r, q] = 1
    return edges.reshape(32, 1024)


def gelu_pair(x):
    root = math.sqrt(2.0 / math.pi)
    t = jnp.tanh(root * (x + 0.044715 * (x * x * x)))
    half = 0.5 * (1.0 + t)
    slope = half + 0.5 * x * (1.0 - t * t) * (root * (1.0 + 3 * 0.044715 * (x * x)))
    return x * half, slope


def shifted(row):
    return jnp.concatenate(
        [pltpu.roll(row, 1, 1), row, pltpu.roll(row, row.shape[1] - 1, 1)], axis=0
    )


def fine_body(factor):
    def body(flags, own, near_up, far_up, spread, edges, grad, mats, bias, field, grad_fine, terms):
        spread_all = spread[...]
        ups = []
        second_core = flags[4] > 0
        close, distant = near_up[...].astype(F32), far_up[...].astype(F32)
        prev = jnp.where(second_core, close, distant).astype(BF)
        nxt = jnp.where(second_core, distant, close).astype(BF)
        for block in (prev[0:144], own[0], own[1], nxt[0:144]):
            wide = dot_tn(block, spread_all)
            for a in range(2):
                ups.append(
                    wide[0:64, 512 * a : 512 * a + 256] + wide[64:128, 512 * a + 256 : 512 * a + 512]
                )
        edge_all = edges[...]
        rows_of = [
            [prev[160:224], prev[224:288]],
            [grad[r] for r in range(4)],
            [nxt[160:224], nxt[224:288]],
        ]
        lefts = [prev[144:160], own[0, 128:144, :], nxt[128:144]]
        rights = [prev[128:144], own[1, 128:144, :], nxt[144:160]]
        grads = []
        for k in range(3):
            wide = dot_tn(jnp.concatenate([lefts[k], rights[k]], axis=0), edge_all)
            for r, row in enumerate(rows_of[k]):
                at = (r + 2 if k == 0 else r) * 128
                rim = wide[0:64, at : at + 128] + wide[64:128, 512 + at : 640 + at]
                grads.append(jnp.concatenate([row.astype(F32), rim], axis=1))
        up_taps = [shifted(u).astype(BF) for u in ups]
        grad_taps = [shifted(g).astype(BF) for g in grads]
        pre_all = dot_nn(mats[0], jnp.concatenate(up_taps, axis=1))
        act_all = dot_nn(mats[1], jnp.concatenate(grad_taps, axis=1))

        def gather(products, i, width):
            return (
                products[0:64, i * width : (i + 1) * width]
                + products[64:128, (i + 1) * width : (i + 2) * width]
                + products[128:192, (i + 2) * width : (i + 3) * width]
            )

        lane = lax.broadcasted_iota(jnp.int32, (64, 256), 1)
        cols_ok = (lane < 128) | ((lane == 128) & (flags[3] > 0)) | ((lane == 255) & (flags[2] > 0))
        offset = bias[...]
        act_taps = []
        pre_taps = []
        d_rows = []
        for i in range(6):
            pre = gather(pre_all, i, 256) + offset
            value, slope = gelu_pair(pre)
            ok = cols_ok
            if i == 0:
                ok = ok & (flags[0] > 0)
            if i == 5:
                ok = ok & (flags[1] > 0)
            value = jnp.where(ok, value, 0.0)
            d_pre = jnp.where(ok, gather(act_all, i, 256) * slope, 0.0)
            act_taps.append(shifted(value)[:, 0:128].astype(BF))
            pre_taps.append(shifted(d_pre)[:, 0:128].astype(BF))
            if 1 <= i <= 4:
                d_rows.append(d_pre[:, 0:128].astype(BF))
        act_wide = jnp.concatenate(act_taps, axis=1)
        out_all = dot_nn(mats[2], act_wide)
        fine_all = dot_nn(mats[3], jnp.concatenate(pre_taps, axis=1))
        for j in range(4):
            field[j] = (
                gather(out_all, j, 128) + ups[j + 2][:, 0:128]
            ).astype(BF)
            grad_fine[j] = (gather(fine_all, j, 128) + grads[j + 2][:, 0:128]).astype(BF)
        d_own = jnp.concatenate(d_rows, axis=1)
        g_own = jnp.concatenate([grad[r] for r in range(4)], axis=1)
        for p in range(3):
            up_cut = jnp.concatenate([up_taps[r][:, 0:128] for r in range(p + 1, p + 5)], axis=1)
            first = dot_nt(up_cut, d_own)
            second = dot_nt(act_wide[:, p * 128 : p * 128 + 512], g_own)
            terms[p * 192 : (p + 1) * 192, :] = (
                jnp.concatenate([first, second], axis=1) * factor
            ).astype(BF)
        ones = jnp.ones((16, 512), BF)
        third = dot_nt(ones, d_own) * factor
        terms[576:592, :] = jnp.concatenate([third, jnp.zeros((16, 64), F32)], axis=1).astype(BF)
        terms[592:768, :] = jnp.zeros((176, 128), BF)

    return body


def fine_stage(flags, own, near_up, far_up, spread, edges, grad, mats, bias, factor):
    return pl.pallas_call(
        fine_body(factor),
        out_shape=[
            jax.ShapeDtypeStruct((4, 64, 128), BF),
            jax.ShapeDtypeStruct((4, 64, 128), BF),
            pltpu.VMEM((768, 128), BF),
        ],
        in_specs=[SMEM_SPEC] + [VMEM_SPEC] * 8,
        out_specs=[VMEM_SPEC] * 3,
        compiler_params=pltpu.CompilerParams(vmem_limit_bytes=20 * 2**20),
        name="fine_stage",
    )(flags, *[near(x) for x in (own, near_up, far_up, spread, edges, grad, mats, bias)])


def finish_body(totals, first, second, third):
    first[...] = totals[0:576, 0:64].astype(F32)
    second[...] = totals[0:576, 64:128].astype(F32)
    third[...] = totals[576:584, 0:64].astype(F32)


def finish(totals):
    return pl.pallas_call(
        finish_body,
        out_shape=[
            jax.ShapeDtypeStruct((576, 64), F32),
            jax.ShapeDtypeStruct((576, 64), F32),
            jax.ShapeDtypeStruct((8, 64), F32),
        ],
        in_specs=[VMEM_SPEC],
        out_specs=[VMEM_SPEC] * 3,
        compiler_params=pltpu.CompilerParams(vmem_limit_bytes=12 * 2**20),
        name="finish_grads",
    )(near(totals))


def copies(piece, axis, count):
    return lax.all_to_all(jnp.broadcast_to(piece[None], (count,) + piece.shape), axis, 0, 0)


def flip(count, bit):
    return [(i, i ^ bit) for i in range(count)]


def turn(count, step):
    return [(i, (i + step) % count) for i in range(count)]


def tap_matrix(weight):
    return jnp.transpose(weight.reshape(3, 3, C, C), (0, 3, 1, 2)).reshape(3 * C, 3 * C)


def flipped(weight):
    return jnp.transpose(weight[::-1], (0, 2, 1))


def device_step(
    patches, w_embed, var_bias, agg_gain, wq, wk, wv, wo, w_up, conv1, bias1, conv2, cotangent
):
    var_at = lax.axis_index(VAR)
    band_at = lax.axis_index(BAND)
    group = ("xh", "core")

    core_at = lax.axis_index("core")
    turned = jnp.transpose(patches, (0, 1, 3, 2)).reshape(128, 256)
    partial_mix = mix(turned, w_embed.reshape(128, D), var_bias).reshape(8, 32, D)
    partial_mix, wo = lax.optimization_barrier((partial_mix, wo))
    pieces = lax.all_to_all(partial_mix, VAR, 0, 0)
    up_mat = jnp.dot(wo, w_up, preferred_element_type=F32).astype(BF)
    pieces, up_mat = lax.optimization_barrier((pieces, up_mat))
    spread_out, slab = norm_copies(pieces, agg_gain.reshape(1, D))
    normed = lax.all_to_all(spread_out, VAR, 0, 0).reshape(256, D)

    keyvals = jnp.concatenate(
        [jnp.dot(normed, w, preferred_element_type=F32).astype(BF) for w in (wk, wv)], axis=1
    )
    ahead = lax.ppermute(keyvals, "z", turn(8, 1))
    behind = lax.ppermute(keyvals, "z", turn(8, -1))
    queries = jnp.dot(normed, wq, preferred_element_type=F32).astype(BF)
    all_queries = [queries] + [lax.ppermute(queries, group, flip(4, k)) for k in (2, 3, 1)]
    fresh = [keyvals, ahead, behind]
    ahead = lax.ppermute(ahead, "z", turn(8, 1))
    behind = lax.ppermute(behind, "z", turn(8, -1))
    carry = flash_step(all_queries, fresh, None, False)
    ahead, behind, carry = lax.optimization_barrier((ahead, behind, carry))
    for step in (2, 3):
        fresh = [ahead, behind]
        if step == 3:
            ahead, behind = ahead[:128], behind[128:]
        ahead = lax.ppermute(ahead, "z", turn(8, 1))
        behind = lax.ppermute(behind, "z", turn(8, -1))
        carry = flash_step(all_queries, fresh, carry, False)
        ahead, behind, carry = lax.optimization_barrier((ahead, behind, carry))
    fresh = [ahead, behind]

    blocks = list(flash_step(all_queries, fresh, carry, True))
    blocks[0], slab, cells, bias1 = lax.optimization_barrier((blocks[0], slab, cotangent, bias1))
    base = jnp.dot(slab, w_up, preferred_element_type=F32)
    edges = jnp.concatenate(
        [
            jnp.transpose(cells[:, :, at : at + 2], (2, 0, 1)).reshape(4, 128) for at in (126, 0)
        ],
        axis=0,
    )
    bias = bias1.reshape(C, 1)
    flags = jnp.stack(
        [band_at > 0, band_at < 31, var_at > 0, var_at < 7, core_at > 0]
    ).astype(jnp.int32)
    parts = [blocks[0]] + [lax.ppermute(b, group, flip(4, k)) for b, k in zip(blocks[1:], (2, 3, 1))]
    place = var_at.reshape(1).astype(jnp.int32)
    merged = merge(place, base, edges, parts, up_mat)
    merged, conv1, conv2 = lax.optimization_barrier((merged, conv1, conv2))
    pieces = lax.all_to_all(merged, VAR, 0, 0)
    mats = jnp.stack(
        [tap_matrix(conv1), tap_matrix(flipped(conv2)), tap_matrix(conv2), tap_matrix(flipped(conv1))]
    )
    pieces, mats = lax.optimization_barrier((pieces, mats))
    base_main = jnp.transpose(base.reshape(32, 2, 4, 128), (1, 2, 0, 3)).reshape(2, 128, 128)
    up, near_rows, far_rows = collect(flags, pieces, base_main, cells)
    near_up = lax.ppermute(near_rows, "core", flip(2, 1))
    pairs = [(i, i + 1) for i in range(1, 31, 2)] + [(i + 1, i) for i in range(1, 31, 2)]
    far_up = lax.ppermute(far_rows, BAND, pairs)
    factor = 1.0 / math.sqrt(128 * 1024)
    spread = jnp.asarray(spread_matrix(), BF)
    field_out, grad_fine, terms = fine_stage(
        flags, up, near_up, far_up, spread, jnp.asarray(edge_matrix(), BF), cells, mats, bias, factor
    )
    shares = lax.all_to_all(terms.reshape(32, 24, 128), PLANE, 0, 0)
    share = jnp.sum(shares.astype(F32), axis=0).astype(BF)
    share = jnp.sum(copies(share, "z", 8).astype(F32), axis=0).astype(BF)
    totals = copies(share, PLANE, 32).reshape(768, 128)
    first, second, third = finish(totals)
    return (field_out, grad_fine, first.reshape(9, C, C), second.reshape(9, C, C), third[0])


def solution(mesh):
    fine_mesh = Mesh(mesh.devices.reshape(2, 8, 2, 4, 2), BAND + VAR)
    in_specs = (
        P(VAR, BAND, None, None),
        P(VAR, None, None),
        P(VAR, None),
        P(),
        P(None, VAR),
        P(None, VAR),
        P(None, VAR),
        P(VAR, None),
        P(),
        P(),
        P(),
        P(),
        P(BAND, None, VAR),
    )
    out_specs = (P(BAND, None, VAR), P(BAND, None, VAR), P(), P(), P())
    return jax.shard_map(
        device_step, mesh=fine_mesh, in_specs=in_specs, out_specs=out_specs, check_vma=False
    )
```

```python
import math

import jax
import jax.numpy as jnp
import numpy as np
from jax import lax
from jax.experimental import pallas as pl
from jax.experimental.pallas import tpu as pltpu
from jax.sharding import Mesh, PartitionSpec as P


D = 2048
HD = 128
C = 64
BAND = ("xh", "z", "core")
VAR = ("y", "xl")
BOARD = ("core", "y", "xl")
BF = jnp.bfloat16
F32 = jnp.float32
VMEM_SPEC = pl.BlockSpec(memory_space=pltpu.VMEM)
SMEM_SPEC = pl.BlockSpec(memory_space=pltpu.SMEM)
SCORE_SCALE = math.log2(math.e) / math.sqrt(HD)


def dot_nn(a, b):
    return lax.dot_general(a, b, (((1,), (0,)), ((), ())), preferred_element_type=F32)


def dot_nt(a, b):
    return lax.dot_general(a, b, (((1,), (1,)), ((), ())), preferred_element_type=F32)


def dot_tn(a, b):
    return lax.dot_general(a, b, (((0,), (0,)), ((), ())), preferred_element_type=F32)


def near(x):
    return pltpu.with_memory_space_constraint(x, pltpu.VMEM)


def mix_body(patches, weights, offsets, out):
    offset = offsets[0:1, :] + offsets[1:2, :]
    out[...] = (dot_tn(patches[...], weights[...]) + offset).astype(BF)


def mix(patches, weights, offsets):
    args = [pltpu.with_memory_space_constraint(x, pltpu.HBM) for x in (patches, weights, offsets)]
    return pl.pallas_call(
        mix_body,
        grid=(2,),
        out_shape=jax.ShapeDtypeStruct((256, D), BF),
        in_specs=[
            pl.BlockSpec((128, 256), lambda k: (0, 0)),
            pl.BlockSpec((128, 1024), lambda k: (0, k)),
            pl.BlockSpec((2, 1024), lambda k: (0, k)),
        ],
        out_specs=pl.BlockSpec((256, 1024), lambda k: (0, k)),
        compiler_params=pltpu.CompilerParams(vmem_limit_bytes=12 * 2**20),
        name="mix_variables",
    )(*args)


def residual_body(slab, weights, out):
    out[...] = dot_nn(slab[...], weights[...])


def residual(slab, weights):
    return pl.pallas_call(
        residual_body,
        grid=(4,),
        out_shape=jax.ShapeDtypeStruct((32, 1024), F32),
        in_specs=[
            pl.BlockSpec((32, D), lambda k: (0, 0)),
            pl.BlockSpec((D, 256), lambda k: (0, k)),
        ],
        out_specs=pl.BlockSpec((32, 256), lambda k: (0, k)),
        compiler_params=pltpu.CompilerParams(vmem_limit_bytes=12 * 2**20),
        name="residual_up",
    )(slab, pltpu.with_memory_space_constraint(weights, pltpu.HBM))


def norm_body(pieces, gain, out, slab):
    total = pieces[0].astype(F32)
    for k in range(1, 8):
        total = total + pieces[k].astype(F32)
    scale = lax.rsqrt(jnp.mean(total * total, axis=1, keepdims=True) + 1e-05)
    normed = (total * scale * gain[...]).astype(BF)
    slab[...] = normed
    for k in range(8):
        out[k] = normed


def norm_copies(pieces, gain):
    return pl.pallas_call(
        norm_body,
        out_shape=[pltpu.VMEM((8, 32, D), BF), pltpu.VMEM((32, D), BF)],
        in_specs=[VMEM_SPEC] * 2,
        out_specs=[VMEM_SPEC] * 2,
        compiler_params=pltpu.CompilerParams(vmem_limit_bytes=12 * 2**20),
        name="norm_slab",
    )(near(pieces), near(gain))


def flash_kernel(blocks, chunks, first, last):
    def body(*refs):
        q_refs = refs[:blocks]
        kv_refs = refs[blocks : blocks + chunks]
        rest = refs[blocks + chunks :]
        if not first:
            stat_in, acc_in = rest[0], rest[1]
            rest = rest[2:]
        if last:
            stat_scr, acc_scr, whole = rest[blocks], rest[blocks + 1], rest[blocks + 2]
            for k in range(chunks):
                whole[k * 128 : (k + 1) * 128, :] = kv_refs[k][...]
            kv_refs = [whole]
        for block in range(blocks):
            for part in range(2):
                inner = slice(part * 128, (part + 1) * 128)
                cols = slice(block * 256 + part * 128, block * 256 + (part + 1) * 128)
                for h in range(2):
                    head = slice(h * HD, (h + 1) * HD)
                    vals = slice(256 + h * HD, 256 + (h + 1) * HD)
                    q = q_refs[block][inner, head]
                    state = None
                    if not first:
                        state = (
                            stat_in[h : h + 1, cols],
                            stat_in[2 + h : 3 + h, cols],
                            acc_in[head, cols],
                        )
                    for kv in kv_refs:
                        s = dot_nt(kv[:, head], q) * SCORE_SCALE
                        top = jnp.max(s, axis=0, keepdims=True)
                        if state is not None:
                            top = jnp.maximum(top, state[0])
                        w = jnp.exp2(s - top)
                        total = jnp.sum(w, axis=0, keepdims=True)
                        update = dot_tn(kv[:, vals], w.astype(BF))
                        if state is not None:
                            shrink = jnp.exp2(state[0] - top)
                            total = total + state[1] * shrink
                            update = update + state[2] * shrink
                        state = (top, total, update)
                    top, total, update = state
                    if last:
                        acc_scr[head, cols] = update
                        stat_scr[h : h + 1, cols] = top
                        stat_scr[2 + h : 3 + h, cols] = total
                    else:
                        rest[1][head, cols] = update
                        rest[0][h : h + 1, cols] = top
                        rest[0][2 + h : 3 + h, cols] = total
        if last:
            rows = []
            for r in (0, 2, 1, 3):
                value = stat_scr[r : r + 1, :]
                high = value.astype(BF).astype(F32)
                mid = (value - high).astype(BF).astype(F32)
                rows += [high, mid, value - high - mid]
            rows.append(jnp.zeros((4, 256 * blocks), F32))
            tail = jnp.concatenate(rows, axis=0).astype(BF)
            for block in range(blocks):
                cols = slice(block * 256, (block + 1) * 256)
                rest[block][0:256, :] = acc_scr[:, cols].astype(BF)
                rest[block][256:272, :] = tail[:, cols]

    return body


def flash_step(queries, chunks, carry, last):
    blocks = len(queries)
    first = carry is None
    ins = list(queries) + list(chunks) + ([] if first else list(carry))
    if last:
        outs = [pltpu.VMEM((272, 256), BF)] * blocks
    else:
        outs = [
            pltpu.VMEM((8, 256 * blocks), F32),
            pltpu.VMEM((256, 256 * blocks), F32),
        ]
    return pl.pallas_call(
        flash_kernel(blocks, len(chunks), first, last),
        out_shape=outs,
        in_specs=[VMEM_SPEC] * len(ins),
        out_specs=[VMEM_SPEC] * len(outs),
        scratch_shapes=[
            pltpu.VMEM((8, 256 * blocks), F32),
            pltpu.VMEM((256, 256 * blocks), F32),
            pltpu.VMEM((256, 512), BF),
        ]
        if last
        else [],
        compiler_params=pltpu.CompilerParams(vmem_limit_bytes=12 * 2**20),
        name="flash_last" if last else "flash_step",
    )(*[near(x) for x in ins])


def merge_body(place, base, edges, b0, b1, b2, b3, mat, out):
    parts = (b0, b1, b2, b3)
    tails = [b[256:272, :].astype(F32) for b in parts]
    context = []
    for h in range(2):
        head = slice(h * HD, (h + 1) * HD)

        def whole(tail, row):
            return tail[row : row + 1] + tail[row + 1 : row + 2] + tail[row + 2 : row + 3]

        tops = [whole(tail, 6 * h) for tail in tails]
        top = jnp.maximum(jnp.maximum(tops[0], tops[1]), jnp.maximum(tops[2], tops[3]))
        ws = [jnp.exp2(v - top) for v in tops]
        total = sum(whole(tail, 6 * h + 3) * w for tail, w in zip(tails, ws))
        share = 1.0 / total
        mixed = sum(b[head, :].astype(F32) * (w * share) for b, w in zip(parts, ws))
        context.append(mixed.astype(BF))
    up = dot_tn(jnp.concatenate(context, axis=0), mat[...])
    own = place[0]
    sides = edges[...].astype(F32)
    for j in range(8):
        lower = jnp.where(own == j - 1, base[31:32, :], 0.0)
        upper = jnp.where(own == j + 1, base[0:1, :], 0.0)
        for half in range(2):
            rows = []
            for k in range(4):
                lanes = slice((half * 4 + k) * 128, (half * 4 + k + 1) * 128)
                out[j, half, k * 32 : (k + 1) * 32, :] = up[32 * j : 32 * j + 32, lanes].astype(BF)
                token = 32 * j + 32 if k % 2 == 0 else 32 * j - 1
                edge = upper if k % 2 == 0 else lower
                if 0 <= token < 256:
                    rows.append(up[token : token + 1, lanes] + edge[:, lanes])
                else:
                    rows.append(jnp.zeros((1, 128), F32))
            source = j - 1 if half == 0 else j + 1
            rows.append(jnp.where(own == source, sides[4 * half : 4 * half + 4], 0.0))
            rows.append(jnp.zeros((8, 128), F32))
            out[j, half, 128:144, :] = jnp.concatenate(rows, axis=0).astype(BF)


def merge(place, base, edges, parts, mat):
    return pl.pallas_call(
        merge_body,
        out_shape=pltpu.VMEM((8, 2, 144, 128), BF),
        in_specs=[SMEM_SPEC] + [VMEM_SPEC] * 7,
        out_specs=VMEM_SPEC,
        compiler_params=pltpu.CompilerParams(vmem_limit_bytes=12 * 2**20),
        name="merge_heads",
    )(place, near(base), near(edges), *[near(x) for x in parts], near(mat))


def collect_body(flags, pieces, base, grad, own, near_out, far_out):
    for half in range(2):
        total = pieces[0, half].astype(F32)
        for k in range(1, 8):
            total = total + pieces[k, half].astype(F32)
        own[half, 0:128, :] = (total[0:128] + base[half]).astype(BF)
        own[half, 128:144, :] = total[128:144].astype(BF)
    core = flags[4]
    for side, out in ((1 - core, near_out), (core, far_out)):
        out[0:144, :] = own[side]
        out[144:160, :] = own[1 - side, 128:144, :]
        for k in range(2):
            out[160 + 64 * k : 224 + 64 * k, :] = grad[2 * side + k]


def collect(flags, pieces, base, grad):
    return pl.pallas_call(
        collect_body,
        out_shape=[
            pltpu.VMEM((2, 144, 128), BF),
            pltpu.VMEM((288, 128), BF),
            pltpu.VMEM((288, 128), BF),
        ],
        in_specs=[SMEM_SPEC] + [VMEM_SPEC] * 3,
        out_specs=[VMEM_SPEC] * 3,
        compiler_params=pltpu.CompilerParams(vmem_limit_bytes=12 * 2**20),
        name="collect_slab",
    )(flags, near(pieces), near(base), near(grad))


def spread_matrix():
    spread = np.zeros((144, 2, 2, 256), np.float32)
    for a in range(2):
        for bh in range(2):
            k = 2 * a + bh
            for bl in range(2):
                for token in range(32):
                    spread[k * 32 + token, a, bl, 4 * token + 2 * bh + bl] = 1
                spread[128 + k, a, bl, (128 + bl) if bh == 0 else (254 + bl)] = 1
    return spread.reshape(144, 1024)


def edge_matrix():
    edges = np.zeros((2, 16, 2, 4, 128), np.float32)
    for q in range(2):
        for r in range(4):
            k, m = divmod(4 * q + r, 2)
            edges[0, 4 + k, m, r, 126 + q] = 1
            edges[1, 4 + k, m, r, q] = 1
    return edges.reshape(32, 1024)


def gelu_pair(x):
    root = math.sqrt(2.0 / math.pi)
    t = jnp.tanh(root * (x + 0.044715 * (x * x * x)))
    half = 0.5 * (1.0 + t)
    slope = half + 0.5 * x * (1.0 - t * t) * (root * (1.0 + 3 * 0.044715 * (x * x)))
    return x * half, slope


def shifted(row):
    return jnp.concatenate(
        [pltpu.roll(row, 1, 1), row, pltpu.roll(row, row.shape[1] - 1, 1)], axis=0
    )


def fine_body(factor):
    def body(flags, own, near_up, far_up, spread, edges, grad, mats, bias, field, grad_fine, terms):
        spread_all = spread[...]
        ups = []
        second_core = flags[4] > 0
        close, distant = near_up[...].astype(F32), far_up[...].astype(F32)
        prev = jnp.where(second_core, close, distant).astype(BF)
        nxt = jnp.where(second_core, distant, close).astype(BF)
        for block in (prev[0:144], own[0], own[1], nxt[0:144]):
            wide = dot_tn(block, spread_all)
            for a in range(2):
                ups.append(
                    wide[0:64, 512 * a : 512 * a + 256] + wide[64:128, 512 * a + 256 : 512 * a + 512]
                )
        edge_all = edges[...]
        rows_of = [
            [prev[160:224], prev[224:288]],
            [grad[r] for r in range(4)],
            [nxt[160:224], nxt[224:288]],
        ]
        lefts = [prev[144:160], own[0, 128:144, :], nxt[128:144]]
        rights = [prev[128:144], own[1, 128:144, :], nxt[144:160]]
        grads = []
        for k in range(3):
            wide = dot_tn(jnp.concatenate([lefts[k], rights[k]], axis=0), edge_all)
            for r, row in enumerate(rows_of[k]):
                at = (r + 2 if k == 0 else r) * 128
                rim = wide[0:64, at : at + 128] + wide[64:128, 512 + at : 640 + at]
                grads.append(jnp.concatenate([row.astype(F32), rim], axis=1))
        up_taps = [shifted(u).astype(BF) for u in ups]
        grad_taps = [shifted(g).astype(BF) for g in grads]
        pre_all = dot_nn(mats[0], jnp.concatenate(up_taps, axis=1))
        act_all = dot_nn(mats[1], jnp.concatenate(grad_taps, axis=1))

        def gather(products, i, width):
            return (
                products[0:64, i * width : (i + 1) * width]
                + products[64:128, (i + 1) * width : (i + 2) * width]
                + products[128:192, (i + 2) * width : (i + 3) * width]
            )

        lane = lax.broadcasted_iota(jnp.int32, (64, 256), 1)
        cols_ok = (lane < 128) | ((lane == 128) & (flags[3] > 0)) | ((lane == 255) & (flags[2] > 0))
        offset = bias[...]
        act_taps = []
        pre_taps = []
        d_rows = []
        for i in range(6):
            pre = gather(pre_all, i, 256) + offset
            value, slope = gelu_pair(pre)
            ok = cols_ok
            if i == 0:
                ok = ok & (flags[0] > 0)
            if i == 5:
                ok = ok & (flags[1] > 0)
            value = jnp.where(ok, value, 0.0)
            d_pre = jnp.where(ok, gather(act_all, i, 256) * slope, 0.0)
            act_taps.append(shifted(value)[:, 0:128].astype(BF))
            pre_taps.append(shifted(d_pre)[:, 0:128].astype(BF))
            if 1 <= i <= 4:
                d_rows.append(d_pre[:, 0:128].astype(BF))
        act_wide = jnp.concatenate(act_taps, axis=1)
        out_all = dot_nn(mats[2], act_wide)
        fine_all = dot_nn(mats[3], jnp.concatenate(pre_taps, axis=1))
        for j in range(4):
            field[j] = (
                gather(out_all, j, 128) + ups[j + 2][:, 0:128]
            ).astype(BF)
            grad_fine[j] = (gather(fine_all, j, 128) + grads[j + 2][:, 0:128]).astype(BF)
        d_own = jnp.concatenate(d_rows, axis=1)
        g_own = jnp.concatenate([grad[r] for r in range(4)], axis=1)
        for p in range(3):
            up_cut = jnp.concatenate([up_taps[r][:, 0:128] for r in range(p + 1, p + 5)], axis=1)
            first = dot_nt(up_cut, d_own)
            second = dot_nt(act_wide[:, p * 128 : p * 128 + 512], g_own)
            terms[p * 192 : (p + 1) * 192, :] = (
                jnp.concatenate([first, second], axis=1) * factor
            ).astype(BF)
        ones = jnp.ones((16, 512), BF)
        third = dot_nt(ones, d_own) * factor
        terms[576:592, :] = jnp.concatenate([third, jnp.zeros((16, 64), F32)], axis=1).astype(BF)
        terms[592:768, :] = jnp.zeros((176, 128), BF)

    return body


def fine_stage(flags, own, near_up, far_up, spread, edges, grad, mats, bias, factor):
    return pl.pallas_call(
        fine_body(factor),
        out_shape=[
            jax.ShapeDtypeStruct((4, 64, 128), BF),
            jax.ShapeDtypeStruct((4, 64, 128), BF),
            pltpu.VMEM((768, 128), BF),
        ],
        in_specs=[SMEM_SPEC] + [VMEM_SPEC] * 8,
        out_specs=[VMEM_SPEC] * 3,
        compiler_params=pltpu.CompilerParams(vmem_limit_bytes=20 * 2**20),
        name="fine_stage",
    )(flags, *[near(x) for x in (own, near_up, far_up, spread, edges, grad, mats, bias)])


def finish_body(totals, first, second, third):
    first[...] = totals[0:576, 0:64].astype(F32)
    second[...] = totals[0:576, 64:128].astype(F32)
    third[...] = totals[576:592, 0:64].astype(F32)[0:1]


def finish(totals):
    return pl.pallas_call(
        finish_body,
        out_shape=[
            jax.ShapeDtypeStruct((576, 64), F32),
            jax.ShapeDtypeStruct((576, 64), F32),
            jax.ShapeDtypeStruct((1, 64), F32),
        ],
        in_specs=[VMEM_SPEC],
        out_specs=[VMEM_SPEC] * 3,
        compiler_params=pltpu.CompilerParams(vmem_limit_bytes=12 * 2**20),
        name="finish_grads",
    )(near(totals))


def copies(piece, axis, count):
    return lax.all_to_all(jnp.broadcast_to(piece[None], (count,) + piece.shape), axis, 0, 0)


def flip(count, bit):
    return [(i, i ^ bit) for i in range(count)]


def turn(count, step):
    return [(i, (i + step) % count) for i in range(count)]


def tap_matrix(weight):
    return jnp.transpose(weight.reshape(3, 3, C, C), (0, 3, 1, 2)).reshape(3 * C, 3 * C)


def flipped(weight):
    return jnp.transpose(weight[::-1], (0, 2, 1))


def device_step(
    patches, w_embed, var_bias, agg_gain, wq, wk, wv, wo, w_up, conv1, bias1, conv2, cotangent
):
    var_at = lax.axis_index(VAR)
    band_at = lax.axis_index(BAND)
    group = ("xh", "core")

    core_at = lax.axis_index("core")
    turned = jnp.transpose(patches, (0, 1, 3, 2)).reshape(128, 256)
    partial_mix = mix(turned, w_embed.reshape(128, D), var_bias).reshape(8, 32, D)
    partial_mix, wo, cells = lax.optimization_barrier((partial_mix, wo, cotangent))
    pieces = lax.all_to_all(partial_mix, VAR, 0, 0)
    up_mat = jnp.dot(wo, w_up, preferred_element_type=F32).astype(BF)
    edges = jnp.concatenate(
        [
            jnp.transpose(cells[:, :, at : at + 2], (2, 0, 1)).reshape(4, 128) for at in (126, 0)
        ],
        axis=0,
    )
    pieces, up_mat, edges = lax.optimization_barrier((pieces, up_mat, edges))
    spread_out, slab = norm_copies(pieces, agg_gain.reshape(1, D))
    normed = lax.all_to_all(spread_out, VAR, 0, 0).reshape(256, D)

    keyvals = jnp.concatenate(
        [jnp.dot(normed, w, preferred_element_type=F32).astype(BF) for w in (wk, wv)], axis=1
    )
    ahead = lax.ppermute(keyvals, "z", turn(8, 1))
    behind = lax.ppermute(keyvals, "z", turn(8, -1))
    queries = jnp.dot(normed, wq, preferred_element_type=F32).astype(BF)
    all_queries = [queries] + [lax.ppermute(queries, group, flip(4, k)) for k in (2, 3, 1)]
    fresh = [keyvals, ahead, behind]
    ahead = lax.ppermute(ahead, "z", turn(8, 1))
    behind = lax.ppermute(behind, "z", turn(8, -1))
    carry = flash_step(all_queries, fresh, None, False)
    ahead, behind, carry = lax.optimization_barrier((ahead, behind, carry))
    for step in (2, 3):
        fresh = [ahead, behind]
        if step == 3:
            ahead, behind = ahead[:128], behind[128:]
        ahead = lax.ppermute(ahead, "z", turn(8, 1))
        behind = lax.ppermute(behind, "z", turn(8, -1))
        carry = flash_step(all_queries, fresh, carry, False)
        ahead, behind, carry = lax.optimization_barrier((ahead, behind, carry))
    fresh = [ahead, behind]

    blocks = list(flash_step(all_queries, fresh, carry, True))
    blocks[0], slab, bias1 = lax.optimization_barrier((blocks[0], slab, bias1))
    base = residual(slab, w_up)
    bias = bias1.reshape(C, 1)
    flags = jnp.stack(
        [band_at > 0, band_at < 31, var_at > 0, var_at < 7, core_at > 0]
    ).astype(jnp.int32)
    parts = [blocks[0]] + [lax.ppermute(b, group, flip(4, k)) for b, k in zip(blocks[1:], (2, 3, 1))]
    place = var_at.reshape(1).astype(jnp.int32)
    merged = merge(place, base, edges, parts, up_mat)
    merged, conv1, conv2 = lax.optimization_barrier((merged, conv1, conv2))
    pieces = lax.all_to_all(merged, VAR, 0, 0)
    mats = jnp.stack(
        [tap_matrix(conv1), tap_matrix(flipped(conv2)), tap_matrix(conv2), tap_matrix(flipped(conv1))]
    )
    pieces, mats = lax.optimization_barrier((pieces, mats))
    base_main = jnp.transpose(base.reshape(32, 2, 4, 128), (1, 2, 0, 3)).reshape(2, 128, 128)
    up, near_rows, far_rows = collect(flags, pieces, base_main, cells)
    near_up = lax.ppermute(near_rows, "core", flip(2, 1))
    pairs = [(i, i + 1) for i in range(1, 31, 2)] + [(i + 1, i) for i in range(1, 31, 2)]
    far_up = lax.ppermute(far_rows, BAND, pairs)
    factor = 1.0 / math.sqrt(128 * 1024)
    spread = jnp.asarray(spread_matrix(), BF)
    field_out, grad_fine, terms = fine_stage(
        flags, up, near_up, far_up, spread, jnp.asarray(edge_matrix(), BF), cells, mats, bias, factor
    )
    shares = lax.all_to_all(terms.reshape(16, 48, 128), BOARD, 0, 0)
    share = jnp.sum(shares.astype(F32), axis=0).astype(BF)
    other = lax.ppermute(share, "xh", flip(2, 1))
    share = (share.astype(F32) + other.astype(F32)).astype(BF)
    share = jnp.sum(copies(share, "z", 8).astype(F32), axis=0).astype(BF)
    totals = copies(share, BOARD, 16).reshape(768, 128)
    first, second, third = finish(totals)
    return (field_out, grad_fine, first.reshape(9, C, C), second.reshape(9, C, C), third.reshape(C))


def solution(mesh):
    fine_mesh = Mesh(mesh.devices.reshape(2, 8, 2, 4, 2), BAND + VAR)
    in_specs = (
        P(VAR, BAND, None, None),
        P(VAR, None, None),
        P(VAR, None),
        P(),
        P(None, VAR),
        P(None, VAR),
        P(None, VAR),
        P(VAR, None),
        P(),
        P(),
        P(),
        P(),
        P(BAND, None, VAR),
    )
    out_specs = (P(BAND, None, VAR), P(BAND, None, VAR), P(), P(), P())
    return jax.shard_map(
        device_step, mesh=fine_mesh, in_specs=in_specs, out_specs=out_specs, check_vma=False
    )
```

```python
import math

import jax
import jax.numpy as jnp
import numpy as np
from jax import lax
from jax.experimental import pallas as pl
from jax.experimental.pallas import tpu as pltpu
from jax.sharding import Mesh, PartitionSpec as P


D = 2048
HD = 128
C = 64
BAND = ("xh", "z", "core")
VAR = ("y", "xl")
PLANE = ("xh", "core", "y", "xl")
BF = jnp.bfloat16
F32 = jnp.float32
VMEM_SPEC = pl.BlockSpec(memory_space=pltpu.VMEM)
SMEM_SPEC = pl.BlockSpec(memory_space=pltpu.SMEM)
SCORE_SCALE = math.log2(math.e) / math.sqrt(HD)


def dot_nn(a, b):
    return lax.dot_general(a, b, (((1,), (0,)), ((), ())), preferred_element_type=F32)


def dot_nt(a, b):
    return lax.dot_general(a, b, (((1,), (1,)), ((), ())), preferred_element_type=F32)


def dot_tn(a, b):
    return lax.dot_general(a, b, (((0,), (0,)), ((), ())), preferred_element_type=F32)


def near(x):
    return pltpu.with_memory_space_constraint(x, pltpu.VMEM)


def mix_body(patches, weights, offsets, out):
    offset = offsets[0:1, :] + offsets[1:2, :]
    out[...] = (dot_tn(patches[...], weights[...]) + offset).astype(BF)


def mix(patches, weights, offsets):
    args = [pltpu.with_memory_space_constraint(x, pltpu.HBM) for x in (patches, weights, offsets)]
    return pl.pallas_call(
        mix_body,
        grid=(2,),
        out_shape=jax.ShapeDtypeStruct((256, D), BF),
        in_specs=[
            pl.BlockSpec((128, 256), lambda k: (0, 0)),
            pl.BlockSpec((128, 1024), lambda k: (0, k)),
            pl.BlockSpec((2, 1024), lambda k: (0, k)),
        ],
        out_specs=pl.BlockSpec((256, 1024), lambda k: (0, k)),
        compiler_params=pltpu.CompilerParams(vmem_limit_bytes=12 * 2**20),
        name="mix_variables",
    )(*args)


def residual_body(slab, weights, out):
    out[...] = dot_nn(slab[...], weights[...])


def residual(slab, weights):
    return pl.pallas_call(
        residual_body,
        grid=(4,),
        out_shape=jax.ShapeDtypeStruct((32, 1024), F32),
        in_specs=[
            pl.BlockSpec((32, D), lambda k: (0, 0)),
            pl.BlockSpec((D, 256), lambda k: (0, k)),
        ],
        out_specs=pl.BlockSpec((32, 256), lambda k: (0, k)),
        compiler_params=pltpu.CompilerParams(vmem_limit_bytes=12 * 2**20),
        name="residual_up",
    )(slab, pltpu.with_memory_space_constraint(weights, pltpu.HBM))


def norm_body(pieces, gain, out, slab):
    total = pieces[0].astype(F32)
    for k in range(1, 8):
        total = total + pieces[k].astype(F32)
    scale = lax.rsqrt(jnp.mean(total * total, axis=1, keepdims=True) + 1e-05)
    normed = (total * scale * gain[...]).astype(BF)
    slab[...] = normed
    for k in range(8):
        out[k] = normed


def norm_copies(pieces, gain):
    return pl.pallas_call(
        norm_body,
        out_shape=[pltpu.VMEM((8, 32, D), BF), pltpu.VMEM((32, D), BF)],
        in_specs=[VMEM_SPEC] * 2,
        out_specs=[VMEM_SPEC] * 2,
        compiler_params=pltpu.CompilerParams(vmem_limit_bytes=12 * 2**20),
        name="norm_slab",
    )(near(pieces), near(gain))


def flash_kernel(blocks, chunks, first, last):
    def body(*refs):
        q_refs = refs[:blocks]
        kv_refs = refs[blocks : blocks + chunks]
        rest = refs[blocks + chunks :]
        if not first:
            stat_in, acc_in = rest[0], rest[1]
            rest = rest[2:]
        if last:
            stat_scr, acc_scr, whole = rest[blocks], rest[blocks + 1], rest[blocks + 2]
            for k in range(chunks):
                whole[k * 128 : (k + 1) * 128, :] = kv_refs[k][...]
            kv_refs = [whole]
        for block in range(blocks):
            for part in range(2):
                inner = slice(part * 128, (part + 1) * 128)
                cols = slice(block * 256 + part * 128, block * 256 + (part + 1) * 128)
                for h in range(2):
                    head = slice(h * HD, (h + 1) * HD)
                    vals = slice(256 + h * HD, 256 + (h + 1) * HD)
                    q = q_refs[block][inner, head]
                    state = None
                    if not first:
                        state = (
                            stat_in[h : h + 1, cols],
                            stat_in[2 + h : 3 + h, cols],
                            acc_in[head, cols],
                        )
                    for kv in kv_refs:
                        s = dot_nt(kv[:, head], q) * SCORE_SCALE
                        top = jnp.max(s, axis=0, keepdims=True)
                        if state is not None:
                            top = jnp.maximum(top, state[0])
                        w = jnp.exp2(s - top)
                        total = jnp.sum(w, axis=0, keepdims=True)
                        update = dot_tn(kv[:, vals], w.astype(BF))
                        if state is not None:
                            shrink = jnp.exp2(state[0] - top)
                            total = total + state[1] * shrink
                            update = update + state[2] * shrink
                        state = (top, total, update)
                    top, total, update = state
                    if last:
                        acc_scr[head, cols] = update
                        stat_scr[h : h + 1, cols] = top
                        stat_scr[2 + h : 3 + h, cols] = total
                    else:
                        rest[1][head, cols] = update
                        rest[0][h : h + 1, cols] = top
                        rest[0][2 + h : 3 + h, cols] = total
        if last:
            rows = []
            for r in (0, 2, 1, 3):
                value = stat_scr[r : r + 1, :]
                high = value.astype(BF).astype(F32)
                mid = (value - high).astype(BF).astype(F32)
                rows += [high, mid, value - high - mid]
            rows.append(jnp.zeros((4, 256 * blocks), F32))
            tail = jnp.concatenate(rows, axis=0).astype(BF)
            for block in range(blocks):
                cols = slice(block * 256, (block + 1) * 256)
                rest[block][0:256, :] = acc_scr[:, cols].astype(BF)
                rest[block][256:272, :] = tail[:, cols]

    return body


def flash_step(queries, chunks, carry, last):
    blocks = len(queries)
    first = carry is None
    ins = list(queries) + list(chunks) + ([] if first else list(carry))
    if last:
        outs = [pltpu.VMEM((272, 256), BF)] * blocks
    else:
        outs = [
            pltpu.VMEM((8, 256 * blocks), F32),
            pltpu.VMEM((256, 256 * blocks), F32),
        ]
    return pl.pallas_call(
        flash_kernel(blocks, len(chunks), first, last),
        out_shape=outs,
        in_specs=[VMEM_SPEC] * len(ins),
        out_specs=[VMEM_SPEC] * len(outs),
        scratch_shapes=[
            pltpu.VMEM((8, 256 * blocks), F32),
            pltpu.VMEM((256, 256 * blocks), F32),
            pltpu.VMEM((256, 512), BF),
        ]
        if last
        else [],
        compiler_params=pltpu.CompilerParams(vmem_limit_bytes=12 * 2**20),
        name="flash_last" if last else "flash_step",
    )(*[near(x) for x in ins])


def merge_body(place, base, edges, b0, b1, b2, b3, mat, out):
    parts = (b0, b1, b2, b3)
    tails = [b[256:272, :].astype(F32) for b in parts]
    context = []
    for h in range(2):
        head = slice(h * HD, (h + 1) * HD)

        def whole(tail, row):
            return tail[row : row + 1] + tail[row + 1 : row + 2] + tail[row + 2 : row + 3]

        tops = [whole(tail, 6 * h) for tail in tails]
        top = jnp.maximum(jnp.maximum(tops[0], tops[1]), jnp.maximum(tops[2], tops[3]))
        ws = [jnp.exp2(v - top) for v in tops]
        total = sum(whole(tail, 6 * h + 3) * w for tail, w in zip(tails, ws))
        share = 1.0 / total
        mixed = sum(b[head, :].astype(F32) * (w * share) for b, w in zip(parts, ws))
        context.append(mixed.astype(BF))
    up = dot_tn(jnp.concatenate(context, axis=0), mat[...])
    own = place[0]
    sides = edges[...].astype(F32)
    for j in range(8):
        lower = jnp.where(own == j - 1, base[31:32, :], 0.0)
        upper = jnp.where(own == j + 1, base[0:1, :], 0.0)
        for half in range(2):
            rows = []
            for k in range(4):
                lanes = slice((half * 4 + k) * 128, (half * 4 + k + 1) * 128)
                out[j, half, k * 32 : (k + 1) * 32, :] = up[32 * j : 32 * j + 32, lanes].astype(BF)
                token = 32 * j + 32 if k % 2 == 0 else 32 * j - 1
                edge = upper if k % 2 == 0 else lower
                if 0 <= token < 256:
                    rows.append(up[token : token + 1, lanes] + edge[:, lanes])
                else:
                    rows.append(jnp.zeros((1, 128), F32))
            source = j - 1 if half == 0 else j + 1
            rows.append(jnp.where(own == source, sides[4 * half : 4 * half + 4], 0.0))
            rows.append(jnp.zeros((8, 128), F32))
            out[j, half, 128:144, :] = jnp.concatenate(rows, axis=0).astype(BF)


def merge(place, base, edges, parts, mat):
    return pl.pallas_call(
        merge_body,
        out_shape=pltpu.VMEM((8, 2, 144, 128), BF),
        in_specs=[SMEM_SPEC] + [VMEM_SPEC] * 7,
        out_specs=VMEM_SPEC,
        compiler_params=pltpu.CompilerParams(vmem_limit_bytes=12 * 2**20),
        name="merge_heads",
    )(place, near(base), near(edges), *[near(x) for x in parts], near(mat))


def collect_body(flags, pieces, base, grad, own, near_out, far_out):
    for half in range(2):
        total = pieces[0, half].astype(F32)
        for k in range(1, 8):
            total = total + pieces[k, half].astype(F32)
        own[half, 0:128, :] = (total[0:128] + base[half]).astype(BF)
        own[half, 128:144, :] = total[128:144].astype(BF)
    core = flags[4]
    for side, out in ((1 - core, near_out), (core, far_out)):
        out[0:144, :] = own[side]
        out[144:160, :] = own[1 - side, 128:144, :]
        for k in range(2):
            out[160 + 64 * k : 224 + 64 * k, :] = grad[2 * side + k]


def collect(flags, pieces, base, grad):
    return pl.pallas_call(
        collect_body,
        out_shape=[
            pltpu.VMEM((2, 144, 128), BF),
            pltpu.VMEM((288, 128), BF),
            pltpu.VMEM((288, 128), BF),
        ],
        in_specs=[SMEM_SPEC] + [VMEM_SPEC] * 3,
        out_specs=[VMEM_SPEC] * 3,
        compiler_params=pltpu.CompilerParams(vmem_limit_bytes=12 * 2**20),
        name="collect_slab",
    )(flags, near(pieces), near(base), near(grad))


def spread_matrix():
    spread = np.zeros((144, 2, 2, 256), np.float32)
    for a in range(2):
        for bh in range(2):
            k = 2 * a + bh
            for bl in range(2):
                for token in range(32):
                    spread[k * 32 + token, a, bl, 4 * token + 2 * bh + bl] = 1
                spread[128 + k, a, bl, (128 + bl) if bh == 0 else (254 + bl)] = 1
    return spread.reshape(144, 1024)


def edge_matrix():
    edges = np.zeros((2, 16, 2, 4, 128), np.float32)
    for q in range(2):
        for r in range(4):
            k, m = divmod(4 * q + r, 2)
            edges[0, 4 + k, m, r, 126 + q] = 1
            edges[1, 4 + k, m, r, q] = 1
    return edges.reshape(32, 1024)


def gelu_pair(x):
    root = math.sqrt(2.0 / math.pi)
    t = jnp.tanh(root * (x + 0.044715 * (x * x * x)))
    half = 0.5 * (1.0 + t)
    slope = half + 0.5 * x * (1.0 - t * t) * (root * (1.0 + 3 * 0.044715 * (x * x)))
    return x * half, slope


def shifted(row):
    return jnp.concatenate(
        [pltpu.roll(row, 1, 1), row, pltpu.roll(row, row.shape[1] - 1, 1)], axis=0
    )


def fine_body(factor):
    def body(flags, own, near_up, far_up, spread, edges, grad, mats, bias, field, grad_fine, terms):
        spread_all = spread[...]
        ups = []
        second_core = flags[4] > 0
        close, distant = near_up[...].astype(F32), far_up[...].astype(F32)
        prev = jnp.where(second_core, close, distant).astype(BF)
        nxt = jnp.where(second_core, distant, close).astype(BF)
        for block in (prev[0:144], own[0], own[1], nxt[0:144]):
            wide = dot_tn(block, spread_all)
            for a in range(2):
                ups.append(
                    wide[0:64, 512 * a : 512 * a + 256] + wide[64:128, 512 * a + 256 : 512 * a + 512]
                )
        edge_all = edges[...]
        rows_of = [
            [prev[160:224], prev[224:288]],
            [grad[r] for r in range(4)],
            [nxt[160:224], nxt[224:288]],
        ]
        lefts = [prev[144:160], own[0, 128:144, :], nxt[128:144]]
        rights = [prev[128:144], own[1, 128:144, :], nxt[144:160]]
        grads = []
        for k in range(3):
            wide = dot_tn(jnp.concatenate([lefts[k], rights[k]], axis=0), edge_all)
            for r, row in enumerate(rows_of[k]):
                at = (r + 2 if k == 0 else r) * 128
                rim = wide[0:64, at : at + 128] + wide[64:128, 512 + at : 640 + at]
                grads.append(jnp.concatenate([row.astype(F32), rim], axis=1))
        up_taps = [shifted(u).astype(BF) for u in ups]
        grad_taps = [shifted(g).astype(BF) for g in grads]
        pre_all = dot_nn(mats[0], jnp.concatenate(up_taps, axis=1))
        act_all = dot_nn(mats[1], jnp.concatenate(grad_taps, axis=1))

        def gather(products, i, width):
            return (
                products[0:64, i * width : (i + 1) * width]
                + products[64:128, (i + 1) * width : (i + 2) * width]
                + products[128:192, (i + 2) * width : (i + 3) * width]
            )

        lane = lax.broadcasted_iota(jnp.int32, (64, 256), 1)
        cols_ok = (lane < 128) | ((lane == 128) & (flags[3] > 0)) | ((lane == 255) & (flags[2] > 0))
        offset = bias[...]
        act_taps = []
        pre_taps = []
        d_rows = []
        for i in range(6):
            pre = gather(pre_all, i, 256) + offset
            value, slope = gelu_pair(pre)
            ok = cols_ok
            if i == 0:
                ok = ok & (flags[0] > 0)
            if i == 5:
                ok = ok & (flags[1] > 0)
            value = jnp.where(ok, value, 0.0)
            d_pre = jnp.where(ok, gather(act_all, i, 256) * slope, 0.0)
            act_taps.append(shifted(value)[:, 0:128].astype(BF))
            pre_taps.append(shifted(d_pre)[:, 0:128].astype(BF))
            if 1 <= i <= 4:
                d_rows.append(d_pre[:, 0:128].astype(BF))
        act_wide = jnp.concatenate(act_taps, axis=1)
        out_all = dot_nn(mats[2], act_wide)
        fine_all = dot_nn(mats[3], jnp.concatenate(pre_taps, axis=1))
        for j in range(4):
            field[j] = (
                gather(out_all, j, 128) + ups[j + 2][:, 0:128]
            ).astype(BF)
            grad_fine[j] = (gather(fine_all, j, 128) + grads[j + 2][:, 0:128]).astype(BF)
        d_own = jnp.concatenate(d_rows, axis=1)
        g_own = jnp.concatenate([grad[r] for r in range(4)], axis=1)
        for p in range(3):
            up_cut = jnp.concatenate([up_taps[r][:, 0:128] for r in range(p + 1, p + 5)], axis=1)
            first = dot_nt(up_cut, d_own)
            second = dot_nt(act_wide[:, p * 128 : p * 128 + 512], g_own)
            terms[p * 192 : (p + 1) * 192, :] = (
                jnp.concatenate([first, second], axis=1) * factor
            ).astype(BF)
        ones = jnp.ones((16, 512), BF)
        third = dot_nt(ones, d_own) * factor
        terms[576:592, :] = jnp.concatenate([third, jnp.zeros((16, 64), F32)], axis=1).astype(BF)
        terms[592:768, :] = jnp.zeros((176, 128), BF)

    return body


def fine_stage(flags, own, near_up, far_up, spread, edges, grad, mats, bias, factor):
    return pl.pallas_call(
        fine_body(factor),
        out_shape=[
            jax.ShapeDtypeStruct((4, 64, 128), BF),
            jax.ShapeDtypeStruct((4, 64, 128), BF),
            pltpu.VMEM((768, 128), BF),
        ],
        in_specs=[SMEM_SPEC] + [VMEM_SPEC] * 8,
        out_specs=[VMEM_SPEC] * 3,
        compiler_params=pltpu.CompilerParams(vmem_limit_bytes=20 * 2**20),
        name="fine_stage",
    )(flags, *[near(x) for x in (own, near_up, far_up, spread, edges, grad, mats, bias)])


def finish_body(totals, first, second, third):
    first[...] = totals[0:576, 0:64].astype(F32)
    second[...] = totals[0:576, 64:128].astype(F32)
    third[...] = totals[576:592, 0:64].astype(F32)[0:1]


def finish(totals):
    return pl.pallas_call(
        finish_body,
        out_shape=[
            jax.ShapeDtypeStruct((576, 64), F32),
            jax.ShapeDtypeStruct((576, 64), F32),
            jax.ShapeDtypeStruct((1, 64), F32),
        ],
        in_specs=[VMEM_SPEC],
        out_specs=[VMEM_SPEC] * 3,
        compiler_params=pltpu.CompilerParams(vmem_limit_bytes=12 * 2**20),
        name="finish_grads",
    )(near(totals))


def copies(piece, axis, count):
    return lax.all_to_all(jnp.broadcast_to(piece[None], (count,) + piece.shape), axis, 0, 0)


def flip(count, bit):
    return [(i, i ^ bit) for i in range(count)]


def turn(count, step):
    return [(i, (i + step) % count) for i in range(count)]


def tap_matrix(weight):
    return jnp.transpose(weight.reshape(3, 3, C, C), (0, 3, 1, 2)).reshape(3 * C, 3 * C)


def flipped(weight):
    return jnp.transpose(weight[::-1], (0, 2, 1))


def device_step(
    patches, w_embed, var_bias, agg_gain, wq, wk, wv, wo, w_up, conv1, bias1, conv2, cotangent
):
    var_at = lax.axis_index(VAR)
    band_at = lax.axis_index(BAND)
    group = ("xh", "core")

    core_at = lax.axis_index("core")
    turned = jnp.transpose(patches, (0, 1, 3, 2)).reshape(128, 256)
    partial_mix = mix(turned, w_embed.reshape(128, D), var_bias).reshape(8, 32, D)
    partial_mix, wo, cells = lax.optimization_barrier((partial_mix, wo, cotangent))
    pieces = lax.all_to_all(partial_mix, VAR, 0, 0)
    up_mat = jnp.dot(wo, w_up, preferred_element_type=F32).astype(BF)
    edges = jnp.concatenate(
        [
            jnp.transpose(cells[:, :, at : at + 2], (2, 0, 1)).reshape(4, 128) for at in (126, 0)
        ],
        axis=0,
    )
    pieces, up_mat, edges = lax.optimization_barrier((pieces, up_mat, edges))
    spread_out, slab = norm_copies(pieces, agg_gain.reshape(1, D))
    normed = lax.all_to_all(spread_out, VAR, 0, 0).reshape(256, D)

    keyvals = jnp.concatenate(
        [jnp.dot(normed, w, preferred_element_type=F32).astype(BF) for w in (wk, wv)], axis=1
    )
    ahead = lax.ppermute(keyvals, "z", turn(8, 1))
    behind = lax.ppermute(keyvals, "z", turn(8, -1))
    queries = jnp.dot(normed, wq, preferred_element_type=F32).astype(BF)
    all_queries = [queries] + [lax.ppermute(queries, group, flip(4, k)) for k in (2, 3, 1)]
    fresh = [keyvals, ahead, behind]
    ahead = lax.ppermute(ahead, "z", turn(8, 1))
    behind = lax.ppermute(behind, "z", turn(8, -1))
    carry = flash_step(all_queries, fresh, None, False)
    ahead, behind, carry = lax.optimization_barrier((ahead, behind, carry))
    for step in (2, 3):
        fresh = [ahead, behind]
        if step == 3:
            ahead, behind = ahead[:128], behind[128:]
        ahead = lax.ppermute(ahead, "z", turn(8, 1))
        behind = lax.ppermute(behind, "z", turn(8, -1))
        carry = flash_step(all_queries, fresh, carry, False)
        ahead, behind, carry = lax.optimization_barrier((ahead, behind, carry))
    fresh = [ahead, behind]

    blocks = list(flash_step(all_queries, fresh, carry, True))
    blocks[0], slab, bias1 = lax.optimization_barrier((blocks[0], slab, bias1))
    base = residual(slab, w_up)
    bias = bias1.reshape(C, 1)
    flags = jnp.stack(
        [band_at > 0, band_at < 31, var_at > 0, var_at < 7, core_at > 0]
    ).astype(jnp.int32)
    parts = [blocks[0]] + [lax.ppermute(b, group, flip(4, k)) for b, k in zip(blocks[1:], (2, 3, 1))]
    place = var_at.reshape(1).astype(jnp.int32)
    merged = merge(place, base, edges, parts, up_mat)
    merged, conv1, conv2 = lax.optimization_barrier((merged, conv1, conv2))
    pieces = lax.all_to_all(merged, VAR, 0, 0)
    mats = jnp.stack(
        [tap_matrix(conv1), tap_matrix(flipped(conv2)), tap_matrix(conv2), tap_matrix(flipped(conv1))]
    )
    pieces, mats = lax.optimization_barrier((pieces, mats))
    base_main = jnp.transpose(base.reshape(32, 2, 4, 128), (1, 2, 0, 3)).reshape(2, 128, 128)
    up, near_rows, far_rows = collect(flags, pieces, base_main, cells)
    near_up = lax.ppermute(near_rows, "core", flip(2, 1))
    pairs = [(i, i + 1) for i in range(1, 31, 2)] + [(i + 1, i) for i in range(1, 31, 2)]
    far_up = lax.ppermute(far_rows, BAND, pairs)
    factor = 1.0 / math.sqrt(128 * 1024)
    spread = jnp.asarray(spread_matrix(), BF)
    field_out, grad_fine, terms = fine_stage(
        flags, up, near_up, far_up, spread, jnp.asarray(edge_matrix(), BF), cells, mats, bias, factor
    )
    shares = lax.all_to_all(terms.reshape(32, 24, 128), PLANE, 0, 0)
    share = jnp.sum(shares.astype(F32), axis=0).astype(BF)
    share = jnp.sum(copies(share, "z", 8).astype(F32), axis=0).astype(BF)
    totals = copies(share, PLANE, 32).reshape(768, 128)
    first, second, third = finish(totals)
    return (field_out, grad_fine, first.reshape(9, C, C), second.reshape(9, C, C), third.reshape(C))


def solution(mesh):
    fine_mesh = Mesh(mesh.devices.reshape(2, 8, 2, 4, 2), BAND + VAR)
    in_specs = (
        P(VAR, BAND, None, None),
        P(VAR, None, None),
        P(VAR, None),
        P(),
        P(None, VAR),
        P(None, VAR),
        P(None, VAR),
        P(VAR, None),
        P(),
        P(),
        P(),
        P(),
        P(BAND, None, VAR),
    )
    out_specs = (P(BAND, None, VAR), P(BAND, None, VAR), P(), P(), P())
    return jax.shard_map(
        device_step, mesh=fine_mesh, in_specs=in_specs, out_specs=out_specs, check_vma=False
    )
```
